32 devices in a mesh: dp: 8 (over z, y), tensor: 4 (over x, core).
Axes of the slice: x: 2, y: 2, z: 4, core: 2. Of those that a mesh axis runs over, the one named last changes fastest.
Arguments:
- tokens: bfloat16 [8192, 1152], P(('dp', 'tensor')), may hold values from -6 to 6
- w_query: bfloat16 [1152, 1152], P(None, 'tensor'), may hold values from -0.1875 to 0.1875
- w_key: bfloat16 [1152, 1152], P(None, 'tensor'), may hold values from -0.1875 to 0.1875
- w_value: bfloat16 [1152, 1152], P(None, 'tensor'), may hold values from -0.1875 to 0.1875
- w_out: bfloat16 [1152, 1152], P('tensor'), may hold values from -1.5 to 1.5
- w_gate: bfloat16 [1152, 3072], P(None, 'tensor'), may hold values from -0.1875 to 0.1875
- w_up: bfloat16 [1152, 3072], P(None, 'tensor'), may hold values from -0.1875 to 0.1875
- w_down: bfloat16 [3072, 1152], P('tensor'), may hold values from -0.109375 to 0.109375
- w_mod: bfloat16 [1152, 6912], P('tensor'), may hold values from -0.1875 to 0.1875
- b_mod: float32 [6912], P('tensor'), may hold values from -3 to 3
- class_table: bfloat16 [1000, 1152], P(None, 'tensor'), may hold values from -6 to 6
- q_gain: float32 [72], replicated, may hold values from 0.8 to 1.8
- k_gain: float32 [72], replicated, may hold values from 0.8 to 1.8
- slot_item: int32 [8, 4], P('dp'), may hold values from -1 to 3, as said below
- labels: int32 [8, 4], P('dp'), may hold values from 0 to 999
- tsteps: int32 [8, 4], P('dp'), may hold values from 0 to 999
- cotangent: bfloat16 [8192, 1152], P(('dp', 'tensor')), may hold values from -6 to 6
Outputs:
- output: bfloat16 [8192, 1152], P(('dp', 'tensor'))
- grad_tokens: bfloat16 [8192, 1152], P(('dp', 'tensor'))
- grad_w_query: float32 [1152, 1152], P(None, 'tensor')
- grad_w_key: float32 [1152, 1152], P(None, 'tensor')
- grad_w_value: float32 [1152, 1152], P(None, 'tensor')
- grad_w_out: float32 [1152, 1152], P('tensor')
- grad_w_gate: float32 [1152, 3072], P(None, 'tensor')
- grad_w_up: float32 [1152, 3072], P(None, 'tensor')
- grad_w_down: float32 [3072, 1152], P('tensor')
- grad_w_mod: float32 [1152, 6912], P('tensor')
- grad_b_mod: float32 [6912], P('tensor')
- grad_class_table: float32 [1000, 1152], P(None, 'tensor')
- grad_q_gain: float32 [72], replicated
- grad_k_gain: float32 [72], replicated
The draws below stay inside these ranges and needn't reach their ends.
Inputs may be any that keep to these rules, and one draw needn't show every extreme that they name: `slot_item`: on each dp index, slot s covers that index's rows s*256 to (s+1)*256 - 1 and holds the number of the item that fills it, or -1 for padding. Items are numbered 0, 1, 2 and so on in slot order; an item fills either one slot or all four slots of one aligned group of four slots.
All inputs are finite; a program needn't handle non-finite values.
Results may differ from the reference program's by a relative error of at most 0.025.
Values may be sent and summed in bfloat16 or wider, within the bound.
No kernel may reach another device: no remote copies, remote signals or barrier semaphores. Data moves between devices by JAX's collectives and lax.ppermute only.
A program may use at most 192 MiB of HBM per device.

```python
import math
import jax
import jax.numpy as jnp
from jax import lax

D = 1152
HEADS = 16
HEAD_DIM = 72
FF = 3072
NCLASS = 1000
TSTEPS = 1000
SIDE = 16
GROUPS = 1
SLOT_TOK = 256
GROUP_TOK = 1024
SLOTS = 4
ROWS = 1024
TOKENS = 8192
N_DP = 8


def draw_slot_item(key, part):
    key_used = jax.random.fold_in(key, 11)
    key_kind = jax.random.fold_in(key, 12)
    key_fill = jax.random.fold_in(key, 13)
    used_groups = jax.random.randint(key_used, (N_DP,), 1, GROUPS + 1)
    used_groups = used_groups.at[0].set(GROUPS).at[1].set(1)
    group_kind = jax.random.randint(key_kind, (N_DP, GROUPS), 0, 3)
    group_kind = group_kind.at[0].set(1).at[1].set(2)
    partial_fill = jax.random.randint(key_fill, (N_DP, GROUPS), 2, 4)
    group_index = jnp.arange(GROUPS, dtype=jnp.int32)[None, :]
    active = group_index < used_groups[:, None]
    group_items = jnp.where(group_kind == 0, 1, jnp.where(group_kind == 1, 4, partial_fill))
    group_items = jnp.where(active, group_items, 0)
    offsets = jnp.cumsum(group_items, axis=1) - group_items
    within = jnp.arange(4, dtype=jnp.int32)[None, None, :]
    kind_wide = group_kind[:, :, None]
    local_item = jnp.where(kind_wide == 0, 0, within)
    is_valid = active[:, :, None] & ((kind_wide != 2) | (within < partial_fill[:, :, None]))
    slot_ids = jnp.where(is_valid, offsets[:, :, None] + local_item, -1)
    return slot_ids.reshape(N_DP, 4 * GROUPS).astype(jnp.int32)


def plant(drawn, rng, least, top_value):
    spot = [jax.random.randint(jax.random.fold_in(rng, axis), (), 0, length) for axis, length in enumerate(drawn.shape)]
    main_axis = drawn.shape.index(max(drawn.shape))
    neighbour = spot[:main_axis] + [(spot[main_axis] + 1) % drawn.shape[main_axis]] + spot[main_axis + 1:]
    return drawn.at[tuple(spot)].set(least).at[tuple(neighbour)].set(top_value)


def shard_levels(rng, dims, pieces, least, top_value):
    loudness = 1.0
    for axis_at, parts in pieces:
        steps = jax.random.uniform(jax.random.fold_in(jax.random.fold_in(rng, 6), axis_at), (parts,), jnp.float32, least / len(pieces), top_value / len(pieces))
        loudness = loudness * jnp.repeat(jnp.exp(steps), dims[axis_at] // parts).reshape((-1,) + (1,) * (len(dims) - 1 - axis_at))
    return loudness


def centred(rng, shape, deviation, reach, cuts=(), kind=jnp.bfloat16):
    values = deviation * jax.random.normal(rng, shape, jnp.float32)
    if cuts:
        values = values * shard_levels(rng, shape, cuts, -0.22, 0.18)
    return jnp.clip(values, -reach, reach).astype(kind)


def setup_inputs(seed: int = 0) -> dict:
    streams_of = jax.random.split(jax.random.key(seed), 18)
    tokens = centred(streams_of[0], (TOKENS, D), 1.0, 6.0, ((0, 32),))
    w_query = centred(streams_of[1], (D, D), D ** -0.5, 0.1875, ((1, 4),))
    w_key = centred(streams_of[2], (D, D), D ** -0.5, 0.1875, ((1, 4),))
    w_value = centred(streams_of[3], (D, D), D ** -0.5, 0.1875, ((1, 4),))
    w_out = centred(streams_of[4], (D, D), (max(D // 64, 1)) ** -0.5, 1.5, ((0, 4),))
    w_gate = centred(streams_of[5], (D, FF), D ** -0.5, 0.1875, ((1, 4),))
    w_up = centred(streams_of[6], (D, FF), D ** -0.5, 0.1875, ((1, 4),))
    w_down = centred(streams_of[7], (FF, D), FF ** -0.5, 0.109375, ((0, 4),))
    w_mod = centred(streams_of[8], (D, 6 * D), D ** -0.5, 0.1875, ((0, 4),))
    b_mod = centred(streams_of[9], (6 * D,), 0.5, 3.0, ((0, 4),), jnp.float32)
    class_table = centred(streams_of[10], (NCLASS, D), 1.0, 6.0, ((1, 4),))
    q_gain = jnp.clip(jax.random.uniform(streams_of[11], (HEAD_DIM,), jnp.float32, 0.8, 1.8), 0.8, 1.8)
    k_gain = jnp.clip(jax.random.uniform(streams_of[12], (HEAD_DIM,), jnp.float32, 0.8, 1.8), 0.8, 1.8)
    slot_item = draw_slot_item(jax.random.fold_in(streams_of[17], 71), 0)
    labels = plant(jax.random.randint(streams_of[14], (N_DP, SLOTS), 0, NCLASS), jax.random.fold_in(streams_of[14], 1), 0, NCLASS - 1).astype(jnp.int32)
    tsteps = plant(jax.random.randint(streams_of[15], (N_DP, SLOTS), 0, TSTEPS), jax.random.fold_in(streams_of[15], 1), 0, TSTEPS - 1).astype(jnp.int32)
    cotangent = centred(streams_of[16], (TOKENS, D), 1.0, 6.0, ((0, 32),))
    return dict(tokens=tokens, w_query=w_query, w_key=w_key, w_value=w_value, w_out=w_out, w_gate=w_gate, w_up=w_up, w_down=w_down, w_mod=w_mod, b_mod=b_mod, class_table=class_table, q_gain=q_gain, k_gain=k_gain, slot_item=slot_item, labels=labels, tsteps=tsteps, cotangent=cotangent)


EPSILON = 1e-06
MASKED = -1000000000.0

@jax.custom_vjp
def low(v):
    return lax.optimization_barrier(v.astype(jnp.bfloat16)).astype(jnp.float32)

@jax.custom_vjp
def low_back(v):
    return v

def low_keep(v):
    return (low(v), None)

def low_pass(kept, grad):
    return (grad,)

def back_keep(v):
    return (v, None)

def back_low(kept, grad):
    return (low(grad),)
low.defvjp(low_keep, low_pass)
low_back.defvjp(back_keep, back_low)

def exact_dot(left, right):
    return jnp.dot(left, right, precision=lax.Precision.HIGHEST, preferred_element_type=jnp.float32)

def sinusoid(step_ids, first_col, col_count):
    half_width = D // 2
    feature = first_col + jnp.arange(col_count, dtype=jnp.int32)
    freq_index = (feature % half_width).astype(jnp.float32)
    rates = jnp.exp(-math.log(10000.0) * freq_index / half_width)
    angles = step_ids.astype(jnp.float32)[:, None] * rates[None, :]
    return jnp.where(feature[None, :] < half_width, jnp.cos(angles), jnp.sin(angles))

def grid_positions(slot_ids):
    slot_count = slot_ids.shape[0]
    slot_order = jnp.arange(slot_count, dtype=jnp.int32)
    same_item = (slot_ids[:, None] == slot_ids[None, :]) & (slot_ids[:, None] >= 0)
    members = lax.optimization_barrier(jnp.sum(same_item.astype(jnp.int32), axis=1))
    first_slot = lax.optimization_barrier(jnp.min(jnp.where(same_item, slot_order[None, :], slot_count), axis=1))
    first_slot = jnp.where(members > 0, first_slot, slot_order)
    side_len = jnp.where(members > 1, 2 * SIDE, SIDE)
    within = jnp.arange(SLOT_TOK, dtype=jnp.int32)
    place_in = (slot_order - first_slot)[:, None] * SLOT_TOK + within[None, :]
    return ((place_in // side_len[:, None]).reshape(-1), (place_in % side_len[:, None]).reshape(-1))

def turn_half(values, grid_index):
    half_len = values.shape[-1] // 2
    rates = jnp.exp(-math.log(10000.0) * jnp.arange(half_len, dtype=jnp.float32) / half_len)
    angles = grid_index.astype(jnp.float32)[:, None] * rates[None, :]
    cosine = jnp.cos(angles)[:, None, :]
    sine_v = jnp.sin(angles)[:, None, :]
    front = values[..., :half_len]
    back_half = values[..., half_len:]
    return jnp.concatenate([front * cosine - back_half * sine_v, back_half * cosine + front * sine_v], axis=-1)

def head_rotary(linear, head_gain, grid_row, grid_col):
    per_head = linear.reshape(linear.shape[0], -1, HEAD_DIM)
    normed = per_head * lax.rsqrt(lax.optimization_barrier(jnp.mean(per_head * per_head, axis=-1, keepdims=True)) + EPSILON) * head_gain
    half_dim = HEAD_DIM // 2
    return jnp.concatenate([turn_half(normed[..., :half_dim], grid_row), turn_half(normed[..., half_dim:], grid_col)], axis=-1)

def modulated_norm(values, shift_by, scale_by):
    normed = values * lax.rsqrt(lax.optimization_barrier(jnp.mean(values * values, axis=-1, keepdims=True)) + EPSILON)
    return normed * (1.0 + scale_by[:, None, :]) + shift_by[:, None, :]

def attend_group(group_args):
    query_blk, key_blk, value_blk, item_of = group_args
    scores = jnp.einsum('qhd,khd->hqk', query_blk, key_blk, precision=lax.Precision.HIGHEST) * (1.0 / math.sqrt(HEAD_DIM))
    scores = low_back(scores)
    allowed = item_of[:, None] == item_of[None, :]
    scores = jnp.where(allowed[None], scores, MASKED)
    probs = jax.nn.softmax(scores, axis=-1)
    return jnp.einsum('hqk,khd->qhd', low(probs), value_blk, precision=lax.Precision.HIGHEST)

def block_forward(token_rows, w_query, w_key, w_value, w_out, w_gate, w_up, w_down, w_mod, b_mod, class_table, q_gain, k_gain, slot_ids, item_labels, item_steps):
    slot_count = slot_ids.shape[0]
    group_count = slot_count // 4
    embedded = jnp.take(class_table, item_labels, axis=0)
    cond_pre = embedded + sinusoid(item_steps, 0, D)
    cond = low(jax.nn.silu(cond_pre))
    modul = low_back(exact_dot(cond, w_mod) + b_mod)
    item_ids = jnp.arange(item_labels.shape[0], dtype=jnp.int32)
    picker = (slot_ids[:, None] == item_ids[None, :]).astype(jnp.float32)
    per_slot = exact_dot(picker, modul)
    shift_a, scale_a, gate_a, shift_m, scale_m, gate_m = jnp.split(per_slot, 6, axis=1)
    resid = token_rows.reshape(slot_count, SLOT_TOK, D)
    normed_attn = low(modulated_norm(resid, shift_a, scale_a)).reshape(-1, D)
    grid_row, grid_col = grid_positions(slot_ids)
    query_rot = low(head_rotary(low_back(exact_dot(normed_attn, w_query)), q_gain, grid_row, grid_col))
    key_rot = low(head_rotary(low_back(exact_dot(normed_attn, w_key)), k_gain, grid_row, grid_col))
    value_all = low(low_back(exact_dot(normed_attn, w_value))).reshape(-1, HEADS, HEAD_DIM)
    token_items = jnp.repeat(slot_ids, SLOT_TOK).reshape(group_count, GROUP_TOK)
    grouped = lambda arr: arr.reshape(group_count, GROUP_TOK, HEADS, HEAD_DIM)
    mixed = lax.map(jax.checkpoint(attend_group), (grouped(query_rot), grouped(key_rot), grouped(value_all), token_items))
    mixed = low_back(low(mixed.reshape(-1, D)))
    attn = low_back(exact_dot(mixed, w_out)).reshape(resid.shape)
    middle = resid + gate_a[:, None, :] * attn
    normed_mlp = low(modulated_norm(middle, shift_m, scale_m)).reshape(-1, D)
    gate_lin = low_back(exact_dot(normed_mlp, w_gate))
    up_lin = low_back(exact_dot(normed_mlp, w_up))
    hidden = low(jax.nn.silu(gate_lin) * up_lin)
    branch = low_back(exact_dot(hidden, w_down)).reshape(resid.shape)
    return (middle + gate_m[:, None, :] * branch).reshape(-1, D)

def reference(tokens, w_query, w_key, w_value, w_out, w_gate, w_up, w_down, w_mod, b_mod, class_table, q_gain, k_gain, slot_item, labels, tsteps, cotangent):
    weights = tuple((w.astype(jnp.float32) for w in (w_query, w_key, w_value, w_out, w_gate, w_up, w_down, w_mod, b_mod, class_table, q_gain, k_gain)))

    def one_index(totals, inputs):
        token_rows, cot_rows, slot_ids, item_labels, item_steps = inputs

        def run_block(rows_in, *params):
            return block_forward(rows_in, *params, slot_ids, item_labels, item_steps)
        result, pullback = jax.vjp(run_block, token_rows.astype(jnp.float32), *weights)
        grads = pullback(cot_rows.astype(jnp.float32))
        totals = tuple((total + grad for total, grad in zip(totals, grads[1:])))
        return (totals, (result.astype(jnp.bfloat16), grads[0].astype(jnp.bfloat16)))
    zero_grads = tuple((jnp.zeros(w.shape, jnp.float32) for w in weights))
    totals, (outputs, grad_rows) = lax.scan(one_index, zero_grads, (tokens.reshape(N_DP, ROWS, D), cotangent.reshape(N_DP, ROWS, D), slot_item, labels, tsteps))
    return (outputs.reshape(-1, D), grad_rows.reshape(-1, D), totals[0], totals[1], totals[2], totals[3], totals[4], totals[5], totals[6], totals[7], totals[8], totals[9], totals[10], totals[11])
```

```python
import math

import jax
import jax.numpy as jnp
from jax import lax
from jax.sharding import PartitionSpec as P

D = 1152
HEAD_DIM = 72
SIDE = 16
SLOT_TOK = 256


EPSILON = 1e-06
MASKED = -1000000000.0
CONTRACT_ROWS = (((0,), (0,)), ((), ()))
CONTRACT_COLS = (((1,), (1,)), ((), ()))


def sinusoid(step_ids, first_col, col_count):
    half_width = D // 2
    feature = first_col + jnp.arange(col_count, dtype=jnp.int32)
    freq_index = (feature % half_width).astype(jnp.float32)
    rates = jnp.exp(-math.log(10000.0) * freq_index / half_width)
    angles = step_ids.astype(jnp.float32)[:, None] * rates[None, :]
    return jnp.where(feature[None, :] < half_width, jnp.cos(angles), jnp.sin(angles))


def grid_positions(slot_ids):
    slot_count = slot_ids.shape[0]
    slot_order = jnp.arange(slot_count, dtype=jnp.int32)
    same_item = (slot_ids[:, None] == slot_ids[None, :]) & (slot_ids[:, None] >= 0)
    members = jnp.sum(same_item.astype(jnp.int32), axis=1)
    first_slot = jnp.min(jnp.where(same_item, slot_order[None, :], slot_count), axis=1)
    first_slot = jnp.where(members > 0, first_slot, slot_order)
    side_len = jnp.where(members > 1, 2 * SIDE, SIDE)
    within = jnp.arange(SLOT_TOK, dtype=jnp.int32)
    place_in = (slot_order - first_slot)[:, None] * SLOT_TOK + within[None, :]
    return ((place_in // side_len[:, None]).reshape(-1), (place_in % side_len[:, None]).reshape(-1))


def turn_half(values, grid_index):
    half_len = values.shape[-1] // 2
    rates = jnp.exp(-math.log(10000.0) * jnp.arange(half_len, dtype=jnp.float32) / half_len)
    angles = grid_index.astype(jnp.float32)[:, None] * rates[None, :]
    cosine = jnp.cos(angles)[:, None, :]
    sine_v = jnp.sin(angles)[:, None, :]
    front = values[..., :half_len]
    back_half = values[..., half_len:]
    return jnp.concatenate(
        [front * cosine - back_half * sine_v, back_half * cosine + front * sine_v], axis=-1
    )


def head_rotary(linear, head_gain, grid_row, grid_col):
    per_head = linear.reshape(linear.shape[0], -1, HEAD_DIM)
    normed = (
        per_head
        * lax.rsqrt(jnp.mean(per_head * per_head, axis=-1, keepdims=True) + EPSILON)
        * head_gain
    )
    half_dim = HEAD_DIM // 2
    return jnp.concatenate(
        [turn_half(normed[..., :half_dim], grid_row), turn_half(normed[..., half_dim:], grid_col)],
        axis=-1,
    )


def modulated_norm(values, shift_by, scale_by):
    normed = values * lax.rsqrt(jnp.mean(values * values, axis=-1, keepdims=True) + EPSILON)
    return normed * (1.0 + scale_by[:, None, :]) + shift_by[:, None, :]


def masked_scores(query_blk, key_blk, item_of):
    raw_scores = jnp.einsum(
        "qhd,khd->hqk", query_blk, key_blk, preferred_element_type=jnp.float32
    ) * (1.0 / math.sqrt(HEAD_DIM))
    allowed = item_of[:, None] == item_of[None, :]
    return jnp.where(allowed[None], raw_scores, MASKED)


def forward_group(group_args):
    query_blk, key_blk, value_blk, item_of = group_args
    scores = masked_scores(query_blk, key_blk, item_of)
    row_max = jnp.max(scores, axis=-1, keepdims=True)
    weights_exp = jnp.exp(scores - row_max)
    row_total = jnp.sum(weights_exp, axis=-1, keepdims=True)
    probs_low = (weights_exp / row_total).astype(jnp.bfloat16)
    mixed_blk = jnp.einsum("hqk,khd->qhd", probs_low, value_blk, preferred_element_type=jnp.float32)
    return (mixed_blk, (row_max + jnp.log(row_total))[..., 0])


def backward_group(group_args):
    query_blk, key_blk, value_blk, grad_blk, log_total, item_of = group_args
    scores = masked_scores(query_blk, key_blk, item_of)
    probs = jnp.exp(scores - log_total[..., None])
    grad_value = jnp.einsum(
        "hqk,qhd->khd", probs.astype(jnp.bfloat16), grad_blk, preferred_element_type=jnp.float32
    )
    grad_probs = jnp.einsum("qhd,khd->hqk", grad_blk, value_blk, preferred_element_type=jnp.float32)
    row_dot = jnp.sum(probs * grad_probs, axis=-1, keepdims=True)
    grad_scores = (probs * (grad_probs - row_dot)).astype(jnp.bfloat16)
    inv_root = 1.0 / math.sqrt(HEAD_DIM)
    grad_query = (
        jnp.einsum("hqk,khd->qhd", grad_scores, key_blk, preferred_element_type=jnp.float32)
        * inv_root
    )
    grad_key = (
        jnp.einsum("hqk,qhd->khd", grad_scores, query_blk, preferred_element_type=jnp.float32)
        * inv_root
    )
    return (grad_query, grad_key, grad_value)


def swap(values, axis_name, bit):
    count = lax.axis_size(axis_name)
    return lax.ppermute(values, axis_name, [(i, i ^ bit) for i in range(count)])


def gather_rows(own):
    near = swap(own, "tensor", 1)
    far = swap(own, "tensor", 2)
    diag = swap(far, "tensor", 1)
    return jnp.concatenate([own, near, far, diag], axis=0)


def scatter_rows(partials):
    far_keep, far_send = partials[2], partials[3]
    far_sum = far_keep.astype(jnp.float32) + swap(far_send, "tensor", 1).astype(jnp.float32)
    far_got = swap(far_sum.astype(jnp.bfloat16), "tensor", 2)
    near_sum = partials[0].astype(jnp.float32) + swap(partials[1], "tensor", 1).astype(jnp.float32)
    return near_sum + far_got.astype(jnp.float32)


def bits_of(axis_name):
    count = lax.axis_size(axis_name)
    bits = []
    bit = 1
    while bit < count:
        bits.append(bit)
        bit *= 2
    assert bit == count
    return bits


def gather_dp(values):
    for bit in reversed(bits_of("dp")):
        values = jnp.concatenate([values, swap(values, "dp", bit)], axis=0)
    return values


def reduce_dp(grad, bits):
    place = lax.axis_index("dp")
    low = grad.astype(jnp.bfloat16)
    for bit in bits:
        half = low.shape[0] // 2
        upper = (place // bit) % 2
        mine = lax.dynamic_slice_in_dim(low, upper * half, half, 0)
        other = lax.dynamic_slice_in_dim(low, (1 - upper) * half, half, 0)
        low = (mine.astype(jnp.float32) + swap(other, "dp", bit).astype(jnp.float32)).astype(
            jnp.bfloat16
        )
    for bit in reversed(bits):
        upper = (place // bit) % 2
        got = swap(low, "dp", bit)
        low = jnp.where(
            upper == 1,
            jnp.concatenate([got, low], axis=0),
            jnp.concatenate([low, got], axis=0),
        )
    return low.astype(jnp.float32)


def rows_dot(source, weight):
    return jnp.dot(source, weight, preferred_element_type=jnp.float32)


def dot_cols(source, weight):
    return lax.dot_general(source, weight, CONTRACT_COLS, preferred_element_type=jnp.float32)


def dot_rows(left, right):
    return lax.dot_general(left, right, CONTRACT_ROWS, preferred_element_type=jnp.float32)


def slot_parts(rows_fn, source):
    far = rows_fn(source[2 * SLOT_TOK :]).astype(jnp.bfloat16)
    near = rows_fn(source[: 2 * SLOT_TOK]).astype(jnp.bfloat16)
    return [near[:SLOT_TOK], near[SLOT_TOK:], far[:SLOT_TOK], far[SLOT_TOK:]]


def local(
    tokens,
    w_query,
    w_key,
    w_value,
    w_out,
    w_gate,
    w_up,
    w_down,
    w_mod,
    b_mod,
    class_table,
    q_gain,
    k_gain,
    slot_item,
    labels,
    tsteps,
    cotangent,
):
    tensor_count = lax.axis_size("tensor")
    tensor_place = lax.axis_index("tensor")
    slot_count = slot_item.shape[1]
    assert tensor_count == 4 and slot_count == 4
    local_rows = tokens.shape[0]
    model_width = tokens.shape[1]
    all_rows = local_rows * tensor_count
    head_cols = w_query.shape[1]
    local_heads = head_cols // HEAD_DIM
    bias_len = b_mod.shape[0]
    item_count = labels.shape[1]
    slot_ids = slot_item[0]
    rel_slots = tensor_place ^ jnp.arange(slot_count, dtype=jnp.int32)

    tokens_all = gather_rows(tokens)

    ids_all = gather_dp(jnp.stack([labels[0], tsteps[0]], axis=1))
    item_ids = jnp.arange(item_count, dtype=jnp.int32)
    class_ids = jnp.arange(class_table.shape[0], dtype=jnp.int32)

    def condition(label_ids, step_ids):
        label_hot = (label_ids[:, None] == class_ids[None, :]).astype(jnp.float32)
        embedded = jnp.dot(
            label_hot.astype(jnp.bfloat16), class_table, preferred_element_type=jnp.float32
        )
        cond_pre = embedded + sinusoid(step_ids, tensor_place * head_cols, head_cols)
        return label_hot, cond_pre

    _, cond_own = condition(labels[0], tsteps[0])
    cond_low = jax.nn.silu(cond_own).astype(jnp.bfloat16)
    bias_full = lax.dynamic_update_slice_in_dim(
        jnp.zeros((6 * model_width,), jnp.float32), b_mod, tensor_place * bias_len, 0
    )
    modul = jnp.dot(cond_low, w_mod, preferred_element_type=jnp.float32) + bias_full[None, :]
    modul = modul + swap(modul, "tensor", 1)
    modul = modul + swap(modul, "tensor", 2)
    picker = (slot_ids[:, None] == item_ids[None, :]).astype(jnp.float32)
    rel_hot = (rel_slots[:, None] == jnp.arange(slot_count, dtype=jnp.int32)[None, :]).astype(
        jnp.float32
    )
    rel_pick = jnp.dot(rel_hot, picker, precision=lax.Precision.HIGHEST)
    per_slot = jnp.dot(rel_pick, modul, precision=lax.Precision.HIGHEST)
    shift_a_all, scale_a_all = per_slot[:, :model_width], per_slot[:, model_width : 2 * model_width]
    shift_a, scale_a, gate_a, shift_m, scale_m, gate_m = jnp.split(per_slot[:1], 6, axis=1)

    grad_out = cotangent.astype(jnp.float32)
    grad_branch = gather_rows((gate_m * grad_out).astype(jnp.bfloat16))

    resid = tokens.astype(jnp.float32)
    attn_all = (
        modulated_norm(
            tokens_all.astype(jnp.float32).reshape(slot_count, SLOT_TOK, model_width),
            shift_a_all,
            scale_a_all,
        )
        .astype(jnp.bfloat16)
        .reshape(all_rows, model_width)
    )
    w_qkv = jnp.concatenate([w_query, w_key, w_value], axis=1)
    qkv_lin = rows_dot(attn_all, w_qkv)
    q_lin, k_lin, v_lin = jnp.split(qkv_lin, 3, axis=1)
    rel_int = rel_hot.astype(jnp.int32)
    grid_row, grid_col = grid_positions(slot_ids)

    def rel_tokens(per_token):
        return jnp.sum(
            rel_int[:, :, None] * per_token.reshape(1, slot_count, SLOT_TOK), axis=1
        ).reshape(-1)

    grid_row, grid_col = rel_tokens(grid_row), rel_tokens(grid_col)
    token_items = rel_tokens(jnp.repeat(slot_ids, SLOT_TOK))

    def prepare(query_part, key_part, query_gain, key_gain):
        return (
            head_rotary(query_part, query_gain, grid_row, grid_col),
            head_rotary(key_part, key_gain, grid_row, grid_col),
        )

    (query_full, key_full), prep_back = jax.vjp(prepare, q_lin, k_lin, q_gain, k_gain)
    query_rot = query_full.astype(jnp.bfloat16)
    key_rot = key_full.astype(jnp.bfloat16)
    value_all = v_lin.astype(jnp.bfloat16).reshape(all_rows, local_heads, HEAD_DIM)
    mixed_f, log_totals = forward_group((query_rot, key_rot, value_all, token_items))
    mixed = mixed_f.reshape(all_rows, head_cols).astype(jnp.bfloat16)
    attn = scatter_rows(slot_parts(lambda rows: rows_dot(rows, w_out), mixed))
    middle = resid + gate_a * attn

    def norm_rows(values, shift_by, scale_by):
        return modulated_norm(values[None], shift_by, scale_by)[0]

    normed_two, norm_two_back = jax.vjp(norm_rows, middle, shift_m, scale_m)
    mlp_all = gather_rows(normed_two.astype(jnp.bfloat16))
    w_gate_up = jnp.concatenate([w_gate, w_up], axis=1)
    gate_up_lin = rows_dot(mlp_all, w_gate_up)
    gate_lin, up_lin = jnp.split(gate_up_lin, 2, axis=1)

    def swiglu(gate_part, up_part):
        return jax.nn.silu(gate_part) * up_part

    hidden_f, swiglu_back = jax.vjp(swiglu, gate_lin, up_lin)
    hidden = hidden_f.astype(jnp.bfloat16)
    grad_gate, grad_up = swiglu_back(dot_cols(grad_branch, w_down))
    grad_gate_up = jnp.concatenate([grad_gate, grad_up], axis=1).astype(jnp.bfloat16)
    grad_normed_mlp = scatter_rows(slot_parts(lambda rows: dot_cols(rows, w_gate_up), grad_gate_up))
    grad_w_gate_up = reduce_dp(dot_rows(mlp_all, grad_gate_up), bits_of("dp"))
    grad_w_down = reduce_dp(dot_rows(hidden, grad_branch), bits_of("dp")[1:] + [1])
    grad_w_gate, grad_w_up = jnp.split(grad_w_gate_up, 2, axis=1)

    branch = scatter_rows(slot_parts(lambda rows: rows_dot(rows, w_down), hidden))
    output = (middle + gate_m * branch).astype(jnp.bfloat16)
    grad_gate_m = jnp.sum(branch * grad_out, axis=0, keepdims=True)

    grad_mid_norm, grad_shift_m, grad_scale_m = norm_two_back(grad_normed_mlp)
    grad_middle = grad_out + grad_mid_norm
    grad_gate_a = jnp.sum(attn * grad_middle, axis=0, keepdims=True)
    grad_attn = gather_rows((gate_a * grad_middle).astype(jnp.bfloat16))
    grad_mixed = dot_cols(grad_attn, w_out).astype(jnp.bfloat16)
    grad_w_out = reduce_dp(dot_rows(mixed, grad_attn), bits_of("dp"))
    grad_q_rot, grad_k_rot, grad_v_all = backward_group(
        (
            query_rot,
            key_rot,
            value_all,
            grad_mixed.reshape(all_rows, local_heads, HEAD_DIM),
            log_totals,
            token_items,
        )
    )
    grad_q_lin, grad_k_lin, grad_q_gain, grad_k_gain = prep_back((grad_q_rot, grad_k_rot))
    grad_qkv = jnp.concatenate(
        [grad_q_lin, grad_k_lin, grad_v_all.reshape(all_rows, head_cols)], axis=1
    ).astype(jnp.bfloat16)
    grad_normed_attn = scatter_rows(slot_parts(lambda rows: dot_cols(rows, w_qkv), grad_qkv))
    grad_w_qkv = reduce_dp(dot_rows(attn_all, grad_qkv), bits_of("dp"))
    grad_w_query, grad_w_key, grad_w_value = jnp.split(grad_w_qkv, 3, axis=1)
    _, norm_one_back = jax.vjp(norm_rows, resid, shift_a, scale_a)
    grad_resid_norm, grad_shift_a, grad_scale_a = norm_one_back(grad_normed_attn)
    grad_tokens = (grad_middle + grad_resid_norm).astype(jnp.bfloat16)

    grad_slot = jnp.concatenate(
        [
            grad_shift_a,
            grad_scale_a,
            grad_gate_a,
            grad_shift_m,
            grad_scale_m,
            grad_gate_m,
            grad_q_gain[None],
            grad_k_gain[None],
        ],
        axis=1,
    )
    grad_slots = gather_rows(grad_slot)
    mod_width = 6 * model_width
    grad_items = lax.dot_general(
        rel_pick,
        grad_slots[:, :mod_width],
        CONTRACT_ROWS,
        precision=lax.Precision.HIGHEST,
        preferred_element_type=jnp.float32,
    ).astype(jnp.bfloat16)
    gain_sum = jnp.sum(grad_slots[:, mod_width:], axis=0, keepdims=True)
    gain_rows = jnp.concatenate(
        [gain_sum, jnp.zeros((item_count - 1, gain_sum.shape[1]), jnp.float32)], axis=0
    )
    items_all = gather_dp(jnp.concatenate([grad_items, gain_rows.astype(jnp.bfloat16)], axis=1))
    grad_modul_low = items_all[:, :mod_width]
    gains = jnp.sum(items_all[:, mod_width:].astype(jnp.float32), axis=0)
    grad_q_gain, grad_k_gain = gains[:HEAD_DIM], gains[HEAD_DIM:]
    label_hot, cond_pre = condition(ids_all[:, 0], ids_all[:, 1])
    cond_full, silu_back = jax.vjp(jax.nn.silu, cond_pre)
    grad_w_mod = dot_rows(cond_full.astype(jnp.bfloat16), grad_modul_low)
    grad_bias_full = jnp.sum(grad_modul_low.astype(jnp.float32), axis=0)
    grad_b_mod = lax.dynamic_slice_in_dim(grad_bias_full, tensor_place * bias_len, bias_len, 0)
    grad_cond_pre = silu_back(dot_cols(grad_modul_low, w_mod))[0]
    grad_class_table = lax.dot_general(
        label_hot,
        grad_cond_pre,
        CONTRACT_ROWS,
        precision=lax.Precision.HIGHEST,
        preferred_element_type=jnp.float32,
    )
    return (
        output,
        grad_tokens,
        grad_w_query,
        grad_w_key,
        grad_w_value,
        grad_w_out,
        grad_w_gate,
        grad_w_up,
        grad_w_down,
        grad_w_mod,
        grad_b_mod,
        grad_class_table,
        grad_q_gain,
        grad_k_gain,
    )


def solution(mesh):
    in_specs = (
        P(("dp", "tensor"), None),
        P(None, "tensor"),
        P(None, "tensor"),
        P(None, "tensor"),
        P("tensor", None),
        P(None, "tensor"),
        P(None, "tensor"),
        P("tensor", None),
        P("tensor", None),
        P("tensor"),
        P(None, "tensor"),
        P(),
        P(),
        P("dp", None),
        P("dp", None),
        P("dp", None),
        P(("dp", "tensor"), None),
    )
    out_specs = (
        P(("dp", "tensor"), None),
        P(("dp", "tensor"), None),
        P(None, "tensor"),
        P(None, "tensor"),
        P(None, "tensor"),
        P("tensor", None),
        P(None, "tensor"),
        P(None, "tensor"),
        P("tensor", None),
        P("tensor", None),
        P("tensor"),
        P(None, "tensor"),
        P(),
        P(),
    )
    return jax.shard_map(local, mesh=mesh, in_specs=in_specs, out_specs=out_specs, check_vma=False)
```

```python
import functools
import math

import jax
import jax.numpy as jnp
from jax import lax
from jax.experimental import pallas as pl
from jax.experimental.pallas import tpu as pltpu
from jax.sharding import PartitionSpec as P

D = 1152
HEAD_DIM = 72
PAD = 128
SIDE = 16
SLOT_TOK = 256
EPSILON = 1e-06
SCORE_LOG2 = math.log2(math.e) / math.sqrt(HEAD_DIM)
INV_ROOT = 1.0 / math.sqrt(HEAD_DIM)
TOTAL_LANE = HEAD_DIM
DOT_LANE = HEAD_DIM + 1
ITEM_LANE = HEAD_DIM + 4
LOG_LANE = ITEM_LANE + 8
FAR_ITEM = 16384.0
CONTRACT_ROWS = (((0,), (0,)), ((), ()))
CONTRACT_COLS = (((1,), (1,)), ((), ()))
VMEM_LIMIT = 56 * 1024 * 1024


def sinusoid(step_ids, first_col, col_count):
    half_width = D // 2
    feature = first_col + jnp.arange(col_count, dtype=jnp.int32)
    freq_index = (feature % half_width).astype(jnp.float32)
    rates = jnp.exp(-math.log(10000.0) * freq_index / half_width)
    angles = step_ids.astype(jnp.float32)[:, None] * rates[None, :]
    return jnp.where(feature[None, :] < half_width, jnp.cos(angles), jnp.sin(angles))


def grid_positions(slot_ids):
    slot_count = slot_ids.shape[0]
    slot_order = jnp.arange(slot_count, dtype=jnp.int32)
    same_item = (slot_ids[:, None] == slot_ids[None, :]) & (slot_ids[:, None] >= 0)
    members = jnp.sum(same_item.astype(jnp.int32), axis=1)
    first_slot = jnp.min(jnp.where(same_item, slot_order[None, :], slot_count), axis=1)
    first_slot = jnp.where(members > 0, first_slot, slot_order)
    side_len = jnp.where(members > 1, 2 * SIDE, SIDE)
    within = jnp.arange(SLOT_TOK, dtype=jnp.int32)
    place_in = (slot_order - first_slot)[:, None] * SLOT_TOK + within[None, :]
    return ((place_in // side_len[:, None]).reshape(-1), (place_in % side_len[:, None]).reshape(-1))


def modulated_norm(values, shift_by, scale_by):
    normed = values * lax.rsqrt(jnp.mean(values * values, axis=-1, keepdims=True) + EPSILON)
    return normed * (1.0 + scale_by[:, None, :]) + shift_by[:, None, :]


def full_dot(left, right, dims=(((1,), (0,)), ((), ()))):
    return lax.dot_general(left, right, dims, preferred_element_type=jnp.float32)


def rotate(values, cosine, sine_front, sine_back):
    quarter = HEAD_DIM // 4
    return (
        values * cosine
        + pltpu.roll(values, PAD - quarter, 1) * sine_front
        + pltpu.roll(values, quarter, 1) * sine_back
    )


def head_inverse(lin):
    return lax.rsqrt(jnp.sum(lin * lin, axis=-1, keepdims=True) * (1.0 / HEAD_DIM) + EPSILON)


def prepare_kernel(
    x_ref, mod_ref, wq_ref, wk_ref, wv_ref, cos_ref, front_ref, back_ref, gain_ref, extra_ref,
    normed_ref, lin_ref, q_ref, k_ref, v_ref,
):
    heads = q_ref.shape[1] // PAD
    span = heads * PAD
    width = x_ref.shape[1]
    x = x_ref[...].astype(jnp.float32)
    rms = lax.rsqrt(jnp.mean(x * x, axis=-1, keepdims=True) + EPSILON)
    shift_by = mod_ref[0, :, :width]
    scale_by = mod_ref[0, :, width:]
    normed = (x * rms * (1.0 + scale_by) + shift_by).astype(jnp.bfloat16)
    normed_ref[...] = normed
    cosine, front, back = cos_ref[...], front_ref[...], back_ref[...]
    q_gain, k_gain = gain_ref[0:1, :], gain_ref[1:2, :]
    for part, w_ref in enumerate((wq_ref, wk_ref, wv_ref)):
        lin = full_dot(normed, w_ref[...])
        for h in range(heads):
            cols = slice(h * PAD, (h + 1) * PAD)
            piece = lin[:, cols]
            extra = extra_ref[0, part : part + 1, :]
            if part == 2:
                v_ref[:, cols] = (piece + extra).astype(jnp.bfloat16)
                continue
            lin_ref[:, part * span + h * PAD : part * span + (h + 1) * PAD] = piece.astype(
                jnp.bfloat16
            )
            gain = q_gain if part == 0 else k_gain
            turned = rotate(piece * head_inverse(piece) * gain, cosine, front, back)
            out_ref = q_ref if part == 0 else k_ref
            out_ref[:, cols] = (turned + extra).astype(jnp.bfloat16)


def prepare(x, mods, weights, tables, gains, extras):
    rows, width = x.shape
    span = weights[0].shape[1]
    blocks = rows // SLOT_TOK
    row_block = lambda cols: pl.BlockSpec((SLOT_TOK, cols), lambda i: (i, 0))
    whole = lambda arr: pl.BlockSpec(arr.shape, lambda i: (0,) * arr.ndim)
    out = lambda cols: jax.ShapeDtypeStruct((rows, cols), jnp.bfloat16)
    return pl.pallas_call(
        prepare_kernel,
        grid=(blocks,),
        in_specs=[
            row_block(width),
            pl.BlockSpec((1, 1, 2 * width), lambda i: (i, 0, 0)),
            *(whole(w) for w in weights),
            row_block(PAD), row_block(PAD), row_block(PAD),
            whole(gains),
            pl.BlockSpec((1, 3, PAD), lambda i: (i, 0, 0)),
        ],
        out_specs=[row_block(width), row_block(2 * span), row_block(span), row_block(span), row_block(span)],
        out_shape=[out(width), out(2 * span), out(span), out(span), out(span)],
        compiler_params=pltpu.CompilerParams(vmem_limit_bytes=VMEM_LIMIT),
        cost_estimate=pl.CostEstimate(
            flops=6 * rows * width * span, bytes_accessed=2 * (rows * (2 * width + 5 * span) + 3 * width * span),
            transcendentals=0,
        ),
    )(x, mods, *weights, *tables, gains, extras)


def split_lanes(values, first_lane, shape):
    lane = lax.broadcasted_iota(jnp.int32, shape, 1)
    high = values.astype(jnp.bfloat16).astype(jnp.float32)
    rest = values - high
    mid = rest.astype(jnp.bfloat16).astype(jnp.float32)
    low = rest - mid
    return jnp.where(
        lane == first_lane, high, jnp.where(lane == first_lane + 1, mid, jnp.where(lane == first_lane + 2, low, 0.0))
    )


def attend_kernel(q_ref, kn_ref, kf_ref, vn_ref, vf_ref, mixed_ref, qlog_ref, *, step):
    keys = (kn_ref[...], kf_ref[...])
    values = (vn_ref[...], vf_ref[...])
    for first in range(0, q_ref.shape[0], step):
        rows = slice(first, first + step)
        q = q_ref[rows, :]
        total = None
        for key, value in zip(keys, values):
            weight = jnp.exp2(full_dot(q, key, CONTRACT_COLS) * SCORE_LOG2).astype(jnp.bfloat16)
            term = full_dot(weight, value)
            total = term if total is None else total + term
        row_sum = total[:, TOTAL_LANE : TOTAL_LANE + 1]
        mixed_ref[rows, :] = (total * (1.0 / row_sum)).astype(jnp.bfloat16)
        log_sum = jnp.log2(row_sum) * (-1.0 / SCORE_LOG2)
        qlog_ref[rows, :] = (q.astype(jnp.float32) + split_lanes(log_sum, LOG_LANE, q.shape)).astype(
            jnp.bfloat16
        )


def attend(q, kn, kf, vn, vf, step=256):
    rows, span = q.shape
    heads = span // PAD
    block = lambda arr: pl.BlockSpec((arr.shape[0], PAD), lambda h: (0, h))
    return pl.pallas_call(
        functools.partial(attend_kernel, step=step),
        grid=(heads,),
        in_specs=[block(a) for a in (q, kn, kf, vn, vf)],
        out_specs=[block(q), block(q)],
        out_shape=[jax.ShapeDtypeStruct(q.shape, jnp.bfloat16)] * 2,
        compiler_params=pltpu.CompilerParams(vmem_limit_bytes=VMEM_LIMIT),
        cost_estimate=pl.CostEstimate(
            flops=4 * rows * (kn.shape[0] + kf.shape[0]) * span, bytes_accessed=2 * (3 * rows * span + 4 * kn.shape[0] * span),
            transcendentals=rows * (kn.shape[0] + kf.shape[0]) * heads,
        ),
    )(q, kn, kf, vn, vf)


def unturn(grad, lin, gain, cosine, front, back):
    turned = rotate(grad, cosine, -front, -back)
    inverse = head_inverse(lin)
    normed = lin * inverse
    gained = turned * gain
    mean = jnp.sum(gained * normed, axis=-1, keepdims=True) * (1.0 / HEAD_DIM)
    return inverse * (gained - normed * mean), jnp.sum(turned * normed, axis=0, keepdims=True)


def pull_kernel(*refs, final):
    if final:
        (ga_ref, mixed_ref, q_ref, kn_ref, kf_ref, vn_ref, vf_ref, wo_ref, squeeze_ref, gain_ref,
         cos_ref, front_ref, back_ref, qlin_ref, klin_ref, acck_ref, accv_ref, near_ref, gains_in_ref,
         out_ref, gains_ref, dk_ref, dv_ref, dq_ref) = refs
    else:
        (ga_ref, mixed_ref, q_ref, kn_ref, kf_ref, vn_ref, vf_ref, wo_ref, squeeze_ref, gain_ref,
         cos_ref, front_ref, back_ref, qlin_ref,
         out_ref, gains_ref, dk_ref, dv_ref) = refs
    heads = q_ref.shape[1] // PAD
    half = kn_ref.shape[0]
    step = pl.program_id(0)
    rows = ga_ref.shape[0]

    @pl.when(step == 0)
    def _():
        if final:
            dk_ref[...] = acck_ref[...]
            dv_ref[...] = accv_ref[...]
            gains_ref[...] = gains_in_ref[...]
        else:
            dk_ref[...] = jnp.zeros_like(dk_ref)
            dv_ref[...] = jnp.zeros_like(dv_ref)
            gains_ref[...] = jnp.zeros_like(gains_ref)

    if final:
        first = pl.multiple_of(half + step * rows, rows)
        table_rows = pl.ds(first, rows)
    else:
        table_rows = slice(None)
    cosine, front, back = cos_ref[table_rows, :], front_ref[table_rows, :], back_ref[table_rows, :]
    grad_mixed = full_dot(ga_ref[...], wo_ref[...], CONTRACT_COLS).astype(jnp.bfloat16)
    gain_sum = jnp.zeros((1, PAD), jnp.float32)
    q_grads = []
    for h in range(heads):
        cols = slice(h * PAD, (h + 1) * PAD)
        grad_low = grad_mixed[:, cols]
        grad_head = grad_low.astype(jnp.float32)
        mixed = mixed_ref[:, cols].astype(jnp.float32)
        row_dot = jnp.sum(grad_head * mixed, axis=-1, keepdims=True)
        grad_aug = (grad_head + split_lanes(-row_dot, DOT_LANE, grad_head.shape)).astype(jnp.bfloat16)
        q = q_ref[:, cols]
        dq = None
        for part, (key_ref, value_ref) in enumerate(((kn_ref, vn_ref), (kf_ref, vf_ref))):
            key, value = key_ref[:, cols], value_ref[:, cols]
            key_rows = slice(part * half, (part + 1) * half)
            probs = jnp.exp2(full_dot(key, q, CONTRACT_COLS) * SCORE_LOG2)
            grad_probs = full_dot(value, grad_aug, CONTRACT_COLS)
            grad_scores = (probs * grad_probs).astype(jnp.bfloat16)
            dv_ref[key_rows, cols] += full_dot(probs.astype(jnp.bfloat16), grad_low)
            dk_ref[key_rows, cols] += full_dot(grad_scores, q)
            term = full_dot(grad_scores, key, CONTRACT_ROWS)
            dq = term if dq is None else dq + term
        lin = qlin_ref[:, cols].astype(jnp.float32)
        grad_lin, gain_term = unturn(dq * INV_ROOT, lin, gain_ref[0:1, :], cosine, front, back)
        gain_sum = gain_sum + gain_term
        q_grads.append(grad_lin.astype(jnp.bfloat16))
    gains_ref[0:1, :] += gain_sum
    q_compact = full_dot(jnp.concatenate(q_grads, axis=1), squeeze_ref[...]).astype(jnp.bfloat16)
    if not final:
        out_ref[...] = q_compact
        return
    dq_ref[pl.ds(pl.multiple_of(step * rows, rows), rows), :] = q_compact

    @pl.when(step == pl.num_programs(0) - 1)
    def _():
        key_gain = jnp.zeros((1, PAD), jnp.float32)
        for block in range(2 * half // rows):
            span = slice(block * rows, (block + 1) * rows)
            k_grads = []
            for h in range(heads):
                cols = slice(h * PAD, (h + 1) * PAD)
                grad_lin, gain_term = unturn(
                    dk_ref[span, cols] * INV_ROOT, klin_ref[span, cols].astype(jnp.float32),
                    gain_ref[1:2, :], cos_ref[span, :], front_ref[span, :], back_ref[span, :],
                )
                key_gain += gain_term
                k_grads.append(grad_lin.astype(jnp.bfloat16))
            k_compact = full_dot(jnp.concatenate(k_grads, axis=1), squeeze_ref[...]).astype(jnp.bfloat16)
            v_compact = full_dot(dv_ref[span, :].astype(jnp.bfloat16), squeeze_ref[...]).astype(jnp.bfloat16)
            if block * rows < half:
                q_part = near_ref[span, :]
            else:
                q_part = dq_ref[block * rows - half : block * rows - half + rows, :]
            out_ref[span, :] = jnp.concatenate([q_part, k_compact, v_compact], axis=1)
        gains_ref[1:2, :] += key_gain


def pull(ga, mixed, qlog, kn, kf, vn, vf, w_out, squeeze, gains, tables, q_lin, k_lin=None, carried=None):
    final = carried is not None
    rows, width = ga.shape
    span = qlog.shape[1]
    half = kn.shape[0]
    compact = squeeze.shape[1]
    block = 256
    row_block = lambda cols: pl.BlockSpec((block, cols), lambda i: (i, 0))
    whole = lambda arr: pl.BlockSpec(arr.shape, lambda i: (0,) * arr.ndim)
    fixed = lambda shape: pl.BlockSpec(shape, lambda i: (0,) * len(shape))
    args = [ga, mixed, qlog, kn, kf, vn, vf, w_out, squeeze, gains, *tables, q_lin]
    specs = [row_block(width), row_block(span), row_block(span)] + [whole(a) for a in (kn, kf, vn, vf, w_out, squeeze, gains)]
    acc = jax.ShapeDtypeStruct((2 * half, span), jnp.float32)
    gain_shape = jax.ShapeDtypeStruct((8, PAD), jnp.float32)
    if final:
        specs += [whole(t) for t in tables] + [row_block(span)]
        near_q, gain_in, acc_k, acc_v = carried
        args += [k_lin, acc_k, acc_v, near_q, gain_in]
        specs += [whole(a) for a in (k_lin, acc_k, acc_v, near_q, gain_in)]
        out_shape = [jax.ShapeDtypeStruct((2 * half, 3 * compact), jnp.bfloat16), gain_shape]
        out_specs = [fixed((2 * half, 3 * compact)), fixed((8, PAD))]
        scratch = [pltpu.VMEM(acc.shape, jnp.float32), pltpu.VMEM(acc.shape, jnp.float32), pltpu.VMEM((rows, compact), jnp.bfloat16)]
    else:
        specs += [row_block(PAD) for t in tables] + [row_block(span)]
        out_shape = [jax.ShapeDtypeStruct((rows, compact), jnp.bfloat16), gain_shape, acc, acc]
        out_specs = [row_block(compact), fixed((8, PAD)), fixed(acc.shape), fixed(acc.shape)]
        scratch = []
    return pl.pallas_call(
        functools.partial(pull_kernel, final=final),
        grid=(rows // block,),
        in_specs=specs, out_specs=out_specs, out_shape=out_shape, scratch_shapes=scratch,
        compiler_params=pltpu.CompilerParams(vmem_limit_bytes=VMEM_LIMIT),
        cost_estimate=pl.CostEstimate(
            flops=10 * rows * 2 * half * span, bytes_accessed=2 * rows * (width + 3 * span) + 16 * half * span,
            transcendentals=rows * 2 * half * span // PAD,
        ),
    )(*args)


def swap(values, axis_name, bit):
    count = lax.axis_size(axis_name)
    return lax.ppermute(values, axis_name, [(i, i ^ bit) for i in range(count)])


def after(values, *earlier):
    return lax.optimization_barrier((values, *earlier))[0]


def bits_of(axis_name):
    count = lax.axis_size(axis_name)
    bits = []
    bit = 1
    while bit < count:
        bits.append(bit)
        bit *= 2
    assert bit == count
    return bits


def gather_dp(values):
    for bit in reversed(bits_of("dp")):
        values = jnp.concatenate([values, swap(values, "dp", bit)], axis=0)
    return values


def reduce_dp(grad, bits, splits, anchors):
    place = lax.axis_index("dp")
    anchors = list(anchors)

    def tied(values):
        return after(values, *anchors.pop(0)) if anchors else values

    low = grad
    for bit in bits:
        half = low.shape[0] // 2
        upper = (place // bit) % 2
        mine = lax.dynamic_slice_in_dim(low, upper * half, half, 0)
        other = lax.dynamic_slice_in_dim(low, (1 - upper) * half, half, 0)
        got = swap(other, "dp", bit)
        mine = tied(mine)
        low = (mine.astype(jnp.float32) + got.astype(jnp.float32)).astype(jnp.bfloat16)
    for bit in reversed(bits):
        upper = (place // bit) % 2
        got = swap(low, "dp", bit)
        low = tied(low)
        if bit == bits[0]:
            break
        low = jnp.where(
            upper == 1,
            jnp.concatenate([got, low], axis=0),
            jnp.concatenate([low, got], axis=0),
        )
    outs = []
    first = 0
    for width in splits:
        one, two = got[:, first : first + width], low[:, first : first + width]
        outs.append(
            jnp.where(
                upper == 1, jnp.concatenate([one, two], axis=0), jnp.concatenate([two, one], axis=0)
            ).astype(jnp.float32)
        )
        first += width
    return outs


def rows_dot(source, weight):
    return jnp.dot(source, weight, preferred_element_type=jnp.float32)


def dot_cols(source, weight):
    return lax.dot_general(source, weight, CONTRACT_COLS, preferred_element_type=jnp.float32)


def dot_rows(left, right):
    return lax.dot_general(
        left, right, CONTRACT_ROWS, preferred_element_type=jnp.float32
    ).astype(jnp.bfloat16)


def gather_halves(own):
    far_own = swap(own, "tensor", 2)
    near = jnp.concatenate([own, swap(own, "tensor", 1)], axis=0)
    far = jnp.concatenate([far_own, swap(far_own, "tensor", 1)], axis=0)
    return near, far


def send_far(far):
    low = far.astype(jnp.bfloat16)
    got = swap(low[SLOT_TOK:], "tensor", 1)
    total = low[:SLOT_TOK].astype(jnp.float32) + got.astype(jnp.float32)
    return swap(total.astype(jnp.bfloat16), "tensor", 2)


def sum_near(near, far_got):
    low = near.astype(jnp.bfloat16)
    got = swap(low[SLOT_TOK:], "tensor", 1)
    return low[:SLOT_TOK].astype(jnp.float32) + got.astype(jnp.float32) + far_got.astype(jnp.float32)


def rope_tables(grid_row, grid_col):
    quarter = HEAD_DIM // 4
    lane = jnp.arange(PAD, dtype=jnp.int32)
    rates = jnp.exp(-math.log(10000.0) * (lane % quarter).astype(jnp.float32) / quarter)
    position = jnp.where(lane[None] < 2 * quarter, grid_row[:, None], grid_col[:, None])
    angles = position.astype(jnp.float32) * rates[None]
    valid = (lane < HEAD_DIM)[None]
    is_front = ((lane % (2 * quarter)) < quarter)[None]
    cosine, sine_v = jnp.cos(angles), jnp.sin(angles)
    return (
        jnp.where(valid, cosine, 0.0),
        jnp.where(valid & is_front, -sine_v, 0.0),
        jnp.where(valid & ~is_front, sine_v, 0.0),
    )


def lane_extras(slot_ids, item_count):
    lane = jnp.arange(PAD, dtype=jnp.int32)
    hot = (lane - ITEM_LANE)[None] == (slot_ids + 1)[:, None]
    item_lane = ((lane >= ITEM_LANE) & (lane <= ITEM_LANE + item_count))[None]
    log_lane = ((lane >= LOG_LANE) & (lane < LOG_LANE + 3))[None]
    for_key = jnp.where(item_lane & ~hot, -FAR_ITEM, 0.0) + jnp.where(log_lane, 1.0, 0.0)
    for_value = jnp.broadcast_to(((lane >= TOTAL_LANE) & (lane < DOT_LANE + 3))[None], hot.shape)
    return jnp.stack([hot.astype(jnp.float32), for_key, for_value.astype(jnp.float32)], axis=1)


def local(
    tokens,
    w_query,
    w_key,
    w_value,
    w_out,
    w_gate,
    w_up,
    w_down,
    w_mod,
    b_mod,
    class_table,
    q_gain,
    k_gain,
    slot_item,
    labels,
    tsteps,
    cotangent,
):
    tensor_count = lax.axis_size("tensor")
    tensor_place = lax.axis_index("tensor")
    slot_count = slot_item.shape[1]
    item_count = labels.shape[1]
    assert tensor_count == 4 and slot_count == 4 and item_count < LOG_LANE - ITEM_LANE
    width = tokens.shape[1]
    head_cols = w_query.shape[1]
    heads = head_cols // HEAD_DIM
    bias_len = b_mod.shape[0]
    slot_ids = slot_item[0]
    half = 2 * SLOT_TOK

    tokens_near, tokens_far = gather_halves(tokens)
    cot_near, cot_far = gather_halves(after(cotangent, tokens_far))

    slots = jnp.arange(slot_count, dtype=jnp.int32)
    rel_hot = (tensor_place ^ slots)[:, None] == slots[None, :]
    rel_int = rel_hot.astype(jnp.int32)
    item_ids = jnp.arange(item_count, dtype=jnp.int32)
    class_ids = jnp.arange(class_table.shape[0], dtype=jnp.int32)

    def condition(label_ids, step_ids):
        label_hot = (label_ids[:, None] == class_ids[None, :]).astype(jnp.float32)
        embedded = rows_dot(label_hot.astype(jnp.bfloat16), class_table)
        cond_pre = embedded + sinusoid(step_ids, tensor_place * head_cols, head_cols)
        return label_hot, cond_pre

    _, cond_own = condition(labels[0], tsteps[0])
    bias_full = lax.dynamic_update_slice_in_dim(
        jnp.zeros((6 * width,), jnp.float32), b_mod, tensor_place * bias_len, 0
    )
    modul = rows_dot(jax.nn.silu(cond_own).astype(jnp.bfloat16), w_mod) + bias_full[None, :]
    modul = modul + swap(modul, "tensor", 1)
    modul = modul + swap(modul, "tensor", 2)
    rel_ids = jnp.sum(rel_int * slot_ids[None, :], axis=1)
    rel_pick = (rel_ids[:, None] == item_ids[None, :]).astype(jnp.float32)
    per_slot = jnp.dot(rel_pick, modul, precision=lax.Precision.HIGHEST)
    shift_a, scale_a, gate_a, shift_m, scale_m, gate_m = jnp.split(per_slot[:1], 6, axis=1)
    gate_m_all = per_slot[:, 5 * width :]

    grid_row, grid_col = grid_positions(slot_ids)

    def rel_tokens(per_token):
        return jnp.sum(rel_int[:, :, None] * per_token.reshape(1, slot_count, SLOT_TOK), axis=1).reshape(-1)

    tables = rope_tables(rel_tokens(grid_row), rel_tokens(grid_col))
    extras = lane_extras(rel_ids, item_count)
    gains = jnp.pad(jnp.stack([q_gain, k_gain]), ((0, 0), (0, PAD - HEAD_DIM)))
    pad_row = jnp.arange(heads * PAD, dtype=jnp.int32)[:, None]
    flat_col = jnp.arange(head_cols, dtype=jnp.int32)[None, :]
    squeeze = (
        (pad_row // PAD == flat_col // HEAD_DIM) & (pad_row % PAD == flat_col % HEAD_DIM)
    ).astype(jnp.bfloat16)
    w_wide = [dot_cols(w, squeeze).astype(jnp.bfloat16) for w in (w_query, w_key, w_value)]
    w_out_wide = rows_dot(squeeze, w_out).astype(jnp.bfloat16)
    w_qkv = jnp.concatenate([w_query, w_key, w_value], axis=1)
    w_gate_up = jnp.concatenate([w_gate, w_up], axis=1)

    mods = per_slot[:, None, : 2 * width]
    near_tables = [t[:half] for t in tables]
    far_tables = [t[half:] for t in tables]
    attn_near, lin_near, q_near, k_near, v_near = prepare(
        tokens_near, mods[:2], w_wide, near_tables, gains, extras[:2]
    )
    attn_far, lin_far, q_far, k_far, v_far = prepare(
        tokens_far, mods[2:], w_wide, far_tables, gains, extras[2:]
    )
    mixed_far, qlog_far = attend(q_far, k_near, k_far, v_near, v_far)
    far_got = send_far(rows_dot(mixed_far, w_out_wide))
    mixed_near, qlog_near = attend(q_near, k_near, k_far, v_near, v_far)
    attn = sum_near(rows_dot(mixed_near, w_out_wide), far_got)

    resid = tokens.astype(jnp.float32)
    middle = resid + gate_a * attn

    def norm_rows(values, shift_by, scale_by):
        return modulated_norm(values[None], shift_by, scale_by)[0]

    normed_two, norm_two_back = jax.vjp(norm_rows, middle, shift_m, scale_m)
    mlp_near, mlp_far = gather_halves(normed_two.astype(jnp.bfloat16))

    def swiglu(gate_part, up_part):
        return jax.nn.silu(gate_part) * up_part

    def mlp_rows(rows, cot_rows, gates):
        gate_lin, up_lin = jnp.split(rows_dot(rows, w_gate_up), 2, axis=1)
        hidden_f, swiglu_back = jax.vjp(swiglu, gate_lin, up_lin)
        grad_branch = (
            (gates[:, None, :] * cot_rows.astype(jnp.float32).reshape(2, SLOT_TOK, width))
            .astype(jnp.bfloat16)
            .reshape(half, width)
        )
        grad_gate, grad_up = swiglu_back(dot_cols(grad_branch, w_down))
        grad_gate_up = jnp.concatenate([grad_gate, grad_up], axis=1).astype(jnp.bfloat16)
        return hidden_f.astype(jnp.bfloat16), grad_branch, grad_gate_up

    hidden_near, branch_grad_near, gu_near = mlp_rows(mlp_near, cot_near, gate_m_all[:2])
    hidden_far, branch_grad_far, gu_far = mlp_rows(mlp_far, cot_far, gate_m_all[2:])
    far_got = send_far(dot_cols(gu_far, w_gate_up))
    grad_normed_mlp = sum_near(dot_cols(gu_near, w_gate_up), far_got)

    grad_out = cotangent.astype(jnp.float32)
    grad_mid_norm, grad_shift_m, grad_scale_m = norm_two_back(grad_normed_mlp)
    grad_middle = grad_out + grad_mid_norm
    grad_gate_a = jnp.sum(attn * grad_middle, axis=0, keepdims=True)
    ga_near, ga_far = gather_halves((gate_a * grad_middle).astype(jnp.bfloat16))
    q_grad_near, gain_near, acc_k, acc_v = pull(
        ga_near, mixed_near, qlog_near, k_near, k_far, v_near, v_far, w_out_wide, squeeze, gains,
        near_tables, lin_near[:, : heads * PAD],
    )
    k_lin = jnp.concatenate([lin_near[:, heads * PAD :], lin_far[:, heads * PAD :]], axis=0)
    grad_qkv, gain_grads = pull(
        ga_far, mixed_far, qlog_far, k_near, k_far, v_near, v_far, w_out_wide, squeeze, gains,
        tables, lin_far[:, : heads * PAD], k_lin, (q_grad_near, gain_near, acc_k, acc_v),
    )
    far_got = send_far(dot_cols(grad_qkv[half:], w_qkv))
    grad_normed_attn = sum_near(dot_cols(grad_qkv[:half], w_qkv), far_got)

    both = lambda near, far: jnp.concatenate([near, far], axis=0)
    attn_all = both(attn_near, attn_far)
    mlp_all = both(mlp_near, mlp_far)
    hidden = both(hidden_near, hidden_far)
    branch_grad = both(branch_grad_near, branch_grad_far)
    bits = bits_of("dp")
    late_first = bits[1:] + bits[:1]
    (grad_w_down,) = reduce_dp(
        dot_rows(hidden, branch_grad), late_first, [width],
        [(q_grad_near,), (grad_qkv,), (grad_qkv,), (grad_normed_attn,)],
    )
    grad_w_gate, grad_w_up = reduce_dp(
        dot_rows(mlp_all, both(gu_near, gu_far)), bits, [w_gate.shape[1], w_up.shape[1]],
        [(grad_qkv,), (grad_normed_attn,)],
    )
    grad_w_out_wide = dot_rows(both(mixed_near, mixed_far), both(ga_near, ga_far))
    grad_w_out_low = grad_w_out_wide.reshape(heads, PAD, width)[:, :HEAD_DIM].reshape(head_cols, width)
    (grad_w_out,) = reduce_dp(grad_w_out_low, bits, [width], [(grad_normed_attn,)])
    grad_w_query, grad_w_key, grad_w_value = reduce_dp(
        dot_rows(attn_all, grad_qkv), bits, [head_cols] * 3, [(grad_normed_attn,)]
    )

    far_got = send_far(rows_dot(after(hidden_far, ga_far), w_down))
    branch = sum_near(rows_dot(after(hidden_near, ga_far), w_down), far_got)
    output = (middle + gate_m * branch).astype(jnp.bfloat16)
    grad_gate_m = jnp.sum(branch * grad_out, axis=0, keepdims=True)

    _, norm_one_back = jax.vjp(norm_rows, resid, shift_a, scale_a)
    grad_resid_norm, grad_shift_a, grad_scale_a = norm_one_back(grad_normed_attn)
    grad_tokens = (grad_middle + grad_resid_norm).astype(jnp.bfloat16)

    grad_slot = jnp.concatenate(
        [
            grad_shift_a,
            grad_scale_a,
            grad_gate_a,
            grad_shift_m,
            grad_scale_m,
            grad_gate_m,
            gain_grads[:1],
            gain_grads[1:2],
        ],
        axis=1,
    )
    pair_slots = jnp.concatenate([grad_slot, swap(grad_slot, "tensor", 2)], axis=0)
    grad_slots = jnp.concatenate([pair_slots, swap(pair_slots, "tensor", 1)], axis=0)
    mod_width = 6 * width
    pick_order = jnp.stack([rel_pick[0], rel_pick[2], rel_pick[1], rel_pick[3]])
    grad_items = lax.dot_general(
        pick_order,
        grad_slots[:, :mod_width],
        CONTRACT_ROWS,
        precision=lax.Precision.HIGHEST,
        preferred_element_type=jnp.float32,
    ).astype(jnp.bfloat16)
    gain_sum = jnp.sum(grad_slots[:, mod_width:], axis=0, keepdims=True)
    gain_rows = jnp.pad(gain_sum, ((0, item_count - 1), (0, 0))).astype(jnp.bfloat16)
    items_all = gather_dp(jnp.concatenate([grad_items, gain_rows], axis=1))
    ids_all = gather_dp(
        jnp.stack([after(labels[0], gate_m), after(tsteps[0], gate_m)], axis=1)
    )
    grad_modul_low = items_all[:, :mod_width]
    gain_total = jnp.sum(items_all[:, mod_width:].astype(jnp.float32), axis=0)
    grad_q_gain = gain_total[:HEAD_DIM]
    grad_k_gain = gain_total[PAD : PAD + HEAD_DIM]
    label_hot, cond_pre = condition(ids_all[:, 0], ids_all[:, 1])
    cond_full, silu_back = jax.vjp(jax.nn.silu, cond_pre)
    grad_w_mod = lax.dot_general(
        cond_full.astype(jnp.bfloat16), grad_modul_low, CONTRACT_ROWS, preferred_element_type=jnp.float32
    )
    grad_bias_full = jnp.sum(grad_modul_low.astype(jnp.float32), axis=0)
    grad_b_mod = lax.dynamic_slice_in_dim(grad_bias_full, tensor_place * bias_len, bias_len, 0)
    grad_cond_pre = silu_back(dot_cols(grad_modul_low, w_mod))[0]
    grad_class_table = lax.dot_general(
        label_hot,
        grad_cond_pre,
        CONTRACT_ROWS,
        precision=lax.Precision.HIGHEST,
        preferred_element_type=jnp.float32,
    )
    return (
        output,
        grad_tokens,
        grad_w_query,
        grad_w_key,
        grad_w_value,
        grad_w_out,
        grad_w_gate,
        grad_w_up,
        grad_w_down,
        grad_w_mod,
        grad_b_mod,
        grad_class_table,
        grad_q_gain,
        grad_k_gain,
    )


def solution(mesh):
    in_specs = (
        P(("dp", "tensor"), None),
        P(None, "tensor"),
        P(None, "tensor"),
        P(None, "tensor"),
        P("tensor", None),
        P(None, "tensor"),
        P(None, "tensor"),
        P("tensor", None),
        P("tensor", None),
        P("tensor"),
        P(None, "tensor"),
        P(),
        P(),
        P("dp", None),
        P("dp", None),
        P("dp", None),
        P(("dp", "tensor"), None),
    )
    out_specs = (
        P(("dp", "tensor"), None),
        P(("dp", "tensor"), None),
        P(None, "tensor"),
        P(None, "tensor"),
        P(None, "tensor"),
        P("tensor", None),
        P(None, "tensor"),
        P(None, "tensor"),
        P("tensor", None),
        P("tensor", None),
        P("tensor"),
        P(None, "tensor"),
        P(),
        P(),
    )
    return jax.shard_map(local, mesh=mesh, in_specs=in_specs, out_specs=out_specs, check_vma=False)
```

```python
import functools
import math

import jax
import jax.numpy as jnp
from jax import lax
from jax.experimental import pallas as pl
from jax.experimental.pallas import tpu as pltpu
from jax.sharding import PartitionSpec as P

D = 1152
HEAD_DIM = 72
PAD = 128
SIDE = 16
SLOT_TOK = 256
EPSILON = 1e-06
SCORE_LOG2 = math.log2(math.e) / math.sqrt(HEAD_DIM)
INV_ROOT = 1.0 / math.sqrt(HEAD_DIM)
BACK_LANE = PAD // 2
TOTAL_LANE = HEAD_DIM // 2
DOT_LANE = TOTAL_LANE + 1
ITEM_LANE = TOTAL_LANE + 4
LOG_LANE = ITEM_LANE + 8
FAR_ITEM = 16384.0
CONTRACT_ROWS = (((0,), (0,)), ((), ()))
CONTRACT_COLS = (((1,), (1,)), ((), ()))
VMEM_LIMIT = 56 * 1024 * 1024


def sinusoid(step_ids, first_col, col_count):
    half_width = D // 2
    feature = first_col + jnp.arange(col_count, dtype=jnp.int32)
    freq_index = (feature % half_width).astype(jnp.float32)
    rates = jnp.exp(-math.log(10000.0) * freq_index / half_width)
    angles = step_ids.astype(jnp.float32)[:, None] * rates[None, :]
    return jnp.where(feature[None, :] < half_width, jnp.cos(angles), jnp.sin(angles))


def grid_positions(slot_ids):
    slot_count = slot_ids.shape[0]
    slot_order = jnp.arange(slot_count, dtype=jnp.int32)
    same_item = (slot_ids[:, None] == slot_ids[None, :]) & (slot_ids[:, None] >= 0)
    members = jnp.sum(same_item.astype(jnp.int32), axis=1)
    first_slot = jnp.min(jnp.where(same_item, slot_order[None, :], slot_count), axis=1)
    first_slot = jnp.where(members > 0, first_slot, slot_order)
    side_len = jnp.where(members > 1, 2 * SIDE, SIDE)
    within = jnp.arange(SLOT_TOK, dtype=jnp.int32)
    place_in = (slot_order - first_slot)[:, None] * SLOT_TOK + within[None, :]
    return ((place_in // side_len[:, None]).reshape(-1), (place_in % side_len[:, None]).reshape(-1))


def modulated_norm(values, shift_by, scale_by):
    normed = values * lax.rsqrt(jnp.mean(values * values, axis=-1, keepdims=True) + EPSILON)
    return normed * (1.0 + scale_by[:, None, :]) + shift_by[:, None, :]


def full_dot(left, right, dims=(((1,), (0,)), ((), ()))):
    return lax.dot_general(left, right, dims, preferred_element_type=jnp.float32)


def rotate(values, cosine, sine):
    return values * cosine + pltpu.roll(values, BACK_LANE, 1) * sine


def lane_sum(values, on_mxu):
    if on_mxu:
        return full_dot(values.astype(jnp.bfloat16), jnp.ones((PAD, PAD), jnp.bfloat16))
    return jnp.sum(values, axis=-1, keepdims=True)


def head_inverse(lin, on_mxu):
    return lax.rsqrt(lane_sum(lin * lin, on_mxu) * (1.0 / HEAD_DIM) + EPSILON)


def table_parts(table_ref):
    return table_ref[:, :PAD], table_ref[:, PAD:]


def whole(array):
    return pl.BlockSpec(array.shape, lambda i: (0,) * array.ndim)


def pick_rows(first_ref, second_ref):
    return jnp.where(pl.program_id(0) == 0, first_ref[...], second_ref[...])


def slot_rows(cols, first):
    return pl.BlockSpec((SLOT_TOK, cols), lambda i: (i + first, 0))


def call_kernel(body, grid, args, in_specs, out_shape, out_specs, carried, flops, exps=0, first_carried=0):
    carried = [] if carried is None else list(carried)
    count = len(args)
    moved = sum(a.size * a.dtype.itemsize for a in args)

    def wrapped(*refs):
        body(*refs[:count], *refs[count + len(carried) :])

    return pl.pallas_call(
        wrapped,
        grid=grid,
        in_specs=list(in_specs) + [pl.BlockSpec(memory_space=pl.ANY)] * len(carried),
        out_shape=out_shape,
        out_specs=out_specs,
        input_output_aliases={count + i: first_carried + i for i in range(len(carried))},
        compiler_params=pltpu.CompilerParams(vmem_limit_bytes=VMEM_LIMIT),
        cost_estimate=pl.CostEstimate(flops=flops, bytes_accessed=moved, transcendentals=exps),
    )(*args, *carried)


def prepare_kernel(
    own_ref, other_ref, mod_ref, wq_ref, wk_ref, wv_ref, table_ref, gain_ref, extra_ref,
    normed_ref, lin_ref, q_ref, k_ref, v_ref,
):
    heads = q_ref.shape[1] // PAD
    span = heads * PAD
    width = own_ref.shape[1]
    x = pick_rows(own_ref, other_ref).astype(jnp.float32)
    rms = lax.rsqrt(jnp.mean(x * x, axis=-1, keepdims=True) + EPSILON)
    shift_by = mod_ref[0, :, :width]
    scale_by = mod_ref[0, :, width:]
    normed = (x * rms * (1.0 + scale_by) + shift_by).astype(jnp.bfloat16)
    normed_ref[...] = normed
    cosine, sine = table_parts(table_ref)
    for part, w_ref in enumerate((wq_ref, wk_ref, wv_ref)):
        lin = full_dot(normed, w_ref[...])
        for h in range(heads):
            cols = slice(h * PAD, (h + 1) * PAD)
            piece = lin[:, cols]
            extra = extra_ref[0, part : part + 1, :]
            if part == 2:
                v_ref[:, cols] = (piece + extra).astype(jnp.bfloat16)
                continue
            lin_ref[:, part * span + h * PAD : part * span + (h + 1) * PAD] = piece.astype(jnp.bfloat16)
            gain = gain_ref[part : part + 1, :]
            turned = rotate(piece * head_inverse(piece, True) * gain, cosine, sine)
            out_ref = q_ref if part == 0 else k_ref
            out_ref[:, cols] = (turned + extra).astype(jnp.bfloat16)


def prepare(pair, per_slot, weights, table, gains, extras, first, carried=None):
    rows, width = 2 * SLOT_TOK, pair[0].shape[1]
    span = weights[0].shape[1]
    all_rows = table.shape[0]
    sizes = (width, 2 * span, span, span, span)
    return call_kernel(
        prepare_kernel,
        (rows // SLOT_TOK,),
        [*pair, per_slot, *weights, table, gains, extras],
        [
            *(whole(rows_in) for rows_in in pair),
            pl.BlockSpec((1, 1, 2 * width), lambda i: (i + first, 0, 0)),
            *(whole(w) for w in weights),
            slot_rows(2 * PAD, first),
            whole(gains),
            pl.BlockSpec((1, 3, PAD), lambda i: (i + first, 0, 0)),
        ],
        [jax.ShapeDtypeStruct((all_rows, cols), jnp.bfloat16) for cols in sizes],
        [slot_rows(cols, first) for cols in sizes],
        carried,
        6 * rows * width * span,
    )


def split_lanes(values, first_lane, shape):
    lane = lax.broadcasted_iota(jnp.int32, shape, 1)
    high = values.astype(jnp.bfloat16).astype(jnp.float32)
    rest = values - high
    mid = rest.astype(jnp.bfloat16).astype(jnp.float32)
    low = rest - mid
    return jnp.where(
        lane == first_lane,
        high,
        jnp.where(lane == first_lane + 1, mid, jnp.where(lane == first_lane + 2, low, 0.0)),
    )


def attend_kernel(q_ref, key_ref, value_ref, mixed_ref, qlog_ref):
    half = key_ref.shape[0] // 2
    for first in range(0, q_ref.shape[0], SLOT_TOK):
        rows = slice(first, first + SLOT_TOK)
        q = q_ref[rows, :]
        total = None
        for start in (0, half):
            keys = slice(start, start + half)
            weight = jnp.exp2(full_dot(q, key_ref[keys, :], CONTRACT_COLS) * SCORE_LOG2)
            term = full_dot(weight.astype(jnp.bfloat16), value_ref[keys, :])
            total = term if total is None else total + term
        row_sum = total[:, TOTAL_LANE : TOTAL_LANE + 1]
        mixed_ref[rows, :] = (total * (1.0 / row_sum)).astype(jnp.bfloat16)
        log_sum = jnp.log2(row_sum) * (-1.0 / SCORE_LOG2)
        qlog_ref[rows, :] = (q.astype(jnp.float32) + split_lanes(log_sum, LOG_LANE, q.shape)).astype(
            jnp.bfloat16
        )


def attend(q, k, v, part, carried=None):
    all_rows, span = q.shape
    rows = all_rows // 2
    heads = span // PAD
    mine = pl.BlockSpec((rows, PAD), lambda h: (part, h))
    every = pl.BlockSpec((all_rows, PAD), lambda h: (0, h))
    return call_kernel(
        attend_kernel,
        (heads,),
        [q, k, v],
        [mine, every, every],
        [jax.ShapeDtypeStruct(q.shape, jnp.bfloat16)] * 2,
        [mine, mine],
        carried,
        4 * rows * all_rows * span,
        rows * all_rows * heads,
    )


def unturn(grad, lin, gain, cosine, sine, on_mxu):
    turned = rotate(grad, cosine, -sine)
    inverse = head_inverse(lin, on_mxu)
    normed = lin * inverse
    gained = turned * gain
    mean = lane_sum(gained * normed, on_mxu) * (1.0 / HEAD_DIM)
    return inverse * (gained - normed * mean), jnp.sum(turned * normed, axis=0, keepdims=True)


def pull_kernel(
    own_ref, other_ref, mixed_ref, q_ref, key_ref, value_ref, wo_ref, squeeze_ref, gain_ref, table_ref, lin_ref,
    *rest,
):
    *before, ga_ref, dq_ref, wide_ref, gains_ref, dk_ref, dv_ref = rest
    heads = q_ref.shape[1] // PAD
    half = key_ref.shape[0] // 2

    @pl.when(pl.program_id(0) == 0)
    def _():
        if before:
            gains_before, dk_before, dv_before = before
            gains_ref[...] = gains_before[...]
            dk_ref[...] = dk_before[...]
            dv_ref[...] = dv_before[...]
        else:
            gains_ref[...] = jnp.zeros_like(gains_ref)
            dk_ref[...] = jnp.zeros_like(dk_ref)
            dv_ref[...] = jnp.zeros_like(dv_ref)

    cosine, sine = table_parts(table_ref)
    grad_attn = pick_rows(own_ref, other_ref)
    ga_ref[...] = grad_attn
    grad_mixed = full_dot(grad_attn, wo_ref[...], CONTRACT_COLS).astype(jnp.bfloat16)
    gain_sum = jnp.zeros((1, PAD), jnp.float32)
    for h in range(heads):
        cols = slice(h * PAD, (h + 1) * PAD)
        grad_low = grad_mixed[:, cols]
        grad_head = grad_low.astype(jnp.float32)
        mixed = mixed_ref[:, cols].astype(jnp.float32)
        row_dot = jnp.sum(grad_head * mixed, axis=-1, keepdims=True)
        grad_aug = (grad_head + split_lanes(-row_dot, DOT_LANE, grad_head.shape)).astype(jnp.bfloat16)
        q = q_ref[:, cols]
        dq = None
        for start in (0, half):
            key_rows = slice(start, start + half)
            key, value = key_ref[key_rows, cols], value_ref[key_rows, cols]
            probs = jnp.exp2(full_dot(key, q, CONTRACT_COLS) * SCORE_LOG2)
            grad_probs = full_dot(value, grad_aug, CONTRACT_COLS)
            grad_scores = (probs * grad_probs).astype(jnp.bfloat16)
            dv_ref[key_rows, cols] += full_dot(probs.astype(jnp.bfloat16), grad_low)
            dk_ref[key_rows, cols] += full_dot(grad_scores, q)
            term = full_dot(grad_scores, key, CONTRACT_ROWS)
            dq = term if dq is None else dq + term
        lin = lin_ref[:, cols].astype(jnp.float32)
        grad_lin, gain_term = unturn(dq * INV_ROOT, lin, gain_ref[0:1, :], cosine, sine, False)
        gain_sum = gain_sum + gain_term
        wide_ref[:, cols] = grad_lin.astype(jnp.bfloat16)
    gains_ref[0:1, :] += gain_sum
    dq_ref[...] = full_dot(wide_ref[...], squeeze_ref[...]).astype(jnp.bfloat16)


def pull(pair, mixed, qlog, k, v, w_out, squeeze, gains, table, lin, first, carried=None, earlier=None):
    rows, width = 2 * SLOT_TOK, pair[0].shape[1]
    all_rows, span = qlog.shape
    compact = squeeze.shape[1]
    args = [*pair, mixed, qlog, k, v, w_out, squeeze, gains, table, lin]
    specs = [*(whole(a) for a in pair), slot_rows(span, first), slot_rows(span, first)]
    specs += [whole(a) for a in (k, v, w_out, squeeze, gains)]
    specs += [slot_rows(2 * PAD, first), slot_rows(span, first)]
    sums = [jax.ShapeDtypeStruct(shape, jnp.float32) for shape in ((8, PAD), (all_rows, span), (all_rows, span))]
    if earlier is not None:
        args += earlier
        specs += [whole(a) for a in earlier]
    kept = [jax.ShapeDtypeStruct((all_rows, cols), jnp.bfloat16) for cols in (width, compact, span)]
    return call_kernel(
        pull_kernel,
        (rows // SLOT_TOK,),
        args,
        specs,
        kept + sums,
        [slot_rows(a.shape[1], first) for a in kept] + [whole(a) for a in sums],
        carried,
        10 * rows * all_rows * span,
        rows * all_rows * span // PAD,
    )


def finish_kernel(
    dq_ref, dk_ref, dv_ref, lin_ref, squeeze_ref, gain_ref, table_ref, wq_ref, wk_ref, wv_ref,
    part_ref, gains_ref, kc_ref, vc_ref,
):
    @pl.when(pl.program_id(0) == 0)
    def _():
        gains_ref[...] = jnp.zeros_like(gains_ref)

    cosine, sine = table_parts(table_ref)
    gain_sum = jnp.zeros((1, PAD), jnp.float32)
    k_grads = []
    for h in range(dk_ref.shape[1] // PAD):
        cols = slice(h * PAD, (h + 1) * PAD)
        grad_lin, gain_term = unturn(
            dk_ref[:, cols] * INV_ROOT, lin_ref[:, cols].astype(jnp.float32), gain_ref[1:2, :], cosine, sine, True
        )
        gain_sum = gain_sum + gain_term
        k_grads.append(grad_lin.astype(jnp.bfloat16))
    gains_ref[0:1, :] += gain_sum
    k_wide = jnp.concatenate(k_grads, axis=1)
    v_wide = dv_ref[...].astype(jnp.bfloat16)
    kc_ref[...] = full_dot(k_wide, squeeze_ref[...]).astype(jnp.bfloat16)
    vc_ref[...] = full_dot(v_wide, squeeze_ref[...]).astype(jnp.bfloat16)
    part_ref[...] = (
        full_dot(dq_ref[...], wq_ref[...], CONTRACT_COLS)
        + full_dot(k_wide, wk_ref[...], CONTRACT_COLS)
        + full_dot(v_wide, wv_ref[...], CONTRACT_COLS)
    ).astype(jnp.bfloat16)


def finish(dq, dk, dv, lin, squeeze, gains, table, weights, first, carried=None):
    all_rows, span = dk.shape
    rows = all_rows // 2
    width, compact = weights[0].shape[0], squeeze.shape[1]
    kept = [jax.ShapeDtypeStruct((all_rows, compact), jnp.bfloat16)] * 2
    fresh = [jax.ShapeDtypeStruct((rows, width), jnp.bfloat16), jax.ShapeDtypeStruct((8, PAD), jnp.float32)]
    return call_kernel(
        finish_kernel,
        (rows // SLOT_TOK,),
        [dq, dk, dv, lin, squeeze, gains, table, *weights],
        [
            slot_rows(span, first),
            slot_rows(span, first),
            slot_rows(span, first),
            pl.BlockSpec((SLOT_TOK, span), lambda i: (i + first, 1)),
            whole(squeeze),
            whole(gains),
            slot_rows(2 * PAD, first),
            *(whole(w) for w in weights),
        ],
        fresh + kept,
        [slot_rows(width, 0), whole(fresh[1])] + [slot_rows(compact, first)] * 2,
        carried,
        6 * rows * span * width,
        first_carried=2,
    )


def mlp_kernel(own_ref, other_ref, gh_ref, wg_ref, wu_ref, part_ref, rows_ref, hidden_ref, gate_ref, up_ref):
    rows = pick_rows(own_ref, other_ref)
    rows_ref[...] = rows
    gate_lin = full_dot(rows, wg_ref[...])
    up_lin = full_dot(rows, wu_ref[...])
    grad_hidden = gh_ref[...]
    sigmoid = 1.0 / (1.0 + jnp.exp(-gate_lin))
    silu = gate_lin * sigmoid
    hidden_ref[...] = (silu * up_lin).astype(jnp.bfloat16)
    grad_up = (grad_hidden * silu).astype(jnp.bfloat16)
    grad_gate = (grad_hidden * up_lin * (sigmoid + silu * (1.0 - sigmoid))).astype(jnp.bfloat16)
    up_ref[...] = grad_up
    gate_ref[...] = grad_gate
    part_ref[...] = (
        full_dot(grad_gate, wg_ref[...], CONTRACT_COLS) + full_dot(grad_up, wu_ref[...], CONTRACT_COLS)
    ).astype(jnp.bfloat16)


def mlp(pair, grad_hidden, w_gate, w_up, first, carried=None):
    rows, width = 2 * SLOT_TOK, pair[0].shape[1]
    all_rows, units = grad_hidden.shape
    kept = [jax.ShapeDtypeStruct((all_rows, cols), jnp.bfloat16) for cols in (width, units, units, units)]
    return call_kernel(
        mlp_kernel,
        (rows // SLOT_TOK,),
        [*pair, grad_hidden, w_gate, w_up],
        [*(whole(a) for a in pair), slot_rows(units, first), whole(w_gate), whole(w_up)],
        [jax.ShapeDtypeStruct((rows, width), jnp.bfloat16), *kept],
        [slot_rows(width, 0)] + [slot_rows(a.shape[1], first) for a in kept],
        carried,
        8 * rows * width * units,
        rows * units,
        first_carried=1,
    )


TAIL_ORDER = (
    "down", "up", "gate", "key", "out", "query", "value", "gate",
    "key", "out", "query", "value", "up", "key", "out", "down",
    "query", "value", "key", "out", "up", "query", "value", "gate",
    "key", "out", "query", "value", "down", "up", "out", "key",
    "query", "value",
)


def swap(values, axis_name, bit):
    count = lax.axis_size(axis_name)
    return lax.ppermute(values, axis_name, [(i, i ^ bit) for i in range(count)])


def after(values, *earlier):
    return lax.optimization_barrier((values, *earlier))[0]


def bits_of(axis_name):
    count = lax.axis_size(axis_name)
    bits = []
    bit = 1
    while bit < count:
        bits.append(bit)
        bit *= 2
    assert bit == count
    return bits


def gather_dp(values):
    for bit in reversed(bits_of("dp")):
        values = jnp.concatenate([values, swap(values, "dp", bit)], axis=0)
    return values


def dp_steps(grad, bits):
    place = lax.axis_index("dp")
    low = grad
    for bit in bits:
        half = low.shape[0] // 2
        upper = (place // bit) % 2
        other = lax.dynamic_slice_in_dim(low, (1 - upper) * half, half, 0)
        got = swap(other, "dp", bit)
        earlier = yield other
        mine = lax.dynamic_slice_in_dim(after(low, *earlier), upper * half, half, 0)
        low = (mine.astype(jnp.float32) + got.astype(jnp.float32)).astype(jnp.bfloat16)
    for bit in reversed(bits):
        upper = (place // bit) % 2
        got = swap(low, "dp", bit)
        earlier = yield low
        low = after(low, *earlier)
        low = jnp.where(
            upper == 1, jnp.concatenate([got, low], axis=0), jnp.concatenate([low, got], axis=0)
        )
        if bit == bits[0]:
            low = low.astype(jnp.float32)
    yield low


class DpSums:
    def __init__(self):
        self.steps = {}
        self.newest = {}
        self.left = {}

    def start(self, name, grad, bits):
        self.steps[name] = dp_steps(grad, bits)
        self.newest[name] = next(self.steps[name])
        self.left[name] = 2 * len(bits)
        return self.newest[name]

    def step(self, name, *earlier):
        self.newest[name] = self.steps[name].send(earlier)
        self.left[name] -= 1
        return self.newest[name]

    def finish(self, order, tick):
        while any(self.left.values()):
            for name in order:
                if self.left[name]:
                    tick = self.step(name, tick)
        return self.newest


def rows_dot(source, weight):
    return jnp.dot(source, weight, preferred_element_type=jnp.float32)


def dot_cols(source, weight):
    return lax.dot_general(source, weight, CONTRACT_COLS, preferred_element_type=jnp.float32)


def dot_rows(left, right):
    return lax.dot_general(
        left, right, CONTRACT_ROWS, preferred_element_type=jnp.float32
    ).astype(jnp.bfloat16)


def pair_sum(part):
    low = part.astype(jnp.bfloat16)
    got = swap(low[SLOT_TOK:], "tensor", 1)
    return low[:SLOT_TOK].astype(jnp.float32) + got.astype(jnp.float32)


def lane_of(dims):
    quarter = HEAD_DIM // 4
    pair, rest = dims // (2 * quarter), dims % (2 * quarter)
    return pair * quarter + jnp.where(rest < quarter, rest, BACK_LANE + rest - quarter)


def head_order(values):
    quarter = HEAD_DIM // 4
    return jnp.concatenate(
        [values[:, first : first + quarter] for first in (0, BACK_LANE, quarter, BACK_LANE + quarter)], axis=1
    )


def rope_table(grid_row, grid_col):
    quarter = HEAD_DIM // 4
    lane = jnp.arange(2 * PAD, dtype=jnp.int32)
    dim = lane % BACK_LANE
    rates = jnp.exp(-math.log(10000.0) * (dim % quarter).astype(jnp.float32) / quarter)
    position = jnp.where(dim[None] < quarter, grid_row[:, None], grid_col[:, None])
    angles = position.astype(jnp.float32) * rates[None]
    sine_v = jnp.where((lane % PAD < BACK_LANE)[None], -jnp.sin(angles), jnp.sin(angles))
    return jnp.where((dim < 2 * quarter)[None], jnp.where((lane < PAD)[None], jnp.cos(angles), sine_v), 0.0)


def lane_extras(slot_ids, item_count):
    lane = jnp.arange(PAD, dtype=jnp.int32)
    hot = (lane - ITEM_LANE)[None] == (slot_ids + 1)[:, None]
    item_lane = ((lane >= ITEM_LANE) & (lane <= ITEM_LANE + item_count))[None]
    log_lane = ((lane >= LOG_LANE) & (lane < LOG_LANE + 3))[None]
    for_key = jnp.where(item_lane & ~hot, -FAR_ITEM, 0.0) + jnp.where(log_lane, 1.0, 0.0)
    for_value = jnp.broadcast_to(((lane >= TOTAL_LANE) & (lane < DOT_LANE + 3))[None], hot.shape)
    return jnp.stack([hot.astype(jnp.float32), for_key, for_value.astype(jnp.float32)], axis=1)


def local(
    tokens,
    w_query,
    w_key,
    w_value,
    w_out,
    w_gate,
    w_up,
    w_down,
    w_mod,
    b_mod,
    class_table,
    q_gain,
    k_gain,
    slot_item,
    labels,
    tsteps,
    cotangent,
):
    tensor_count = lax.axis_size("tensor")
    tensor_place = lax.axis_index("tensor")
    slot_count = slot_item.shape[1]
    item_count = labels.shape[1]
    assert tensor_count == 4 and slot_count == 4 and item_count < LOG_LANE - ITEM_LANE
    width = tokens.shape[1]
    head_cols = w_query.shape[1]
    heads = head_cols // HEAD_DIM
    bias_len = b_mod.shape[0]
    slot_ids = slot_item[0]
    half = 2 * SLOT_TOK

    far_tokens = swap(tokens, "tensor", 2)
    near_tokens = swap(tokens, "tensor", 1)

    slots = jnp.arange(slot_count, dtype=jnp.int32)
    rel_hot = (tensor_place ^ slots)[:, None] == slots[None, :]
    rel_int = rel_hot.astype(jnp.int32)
    item_ids = jnp.arange(item_count, dtype=jnp.int32)
    class_ids = jnp.arange(class_table.shape[0], dtype=jnp.int32)

    def condition(label_ids, step_ids):
        label_hot = (label_ids[:, None] == class_ids[None, :]).astype(jnp.float32)
        embedded = rows_dot(label_hot.astype(jnp.bfloat16), class_table)
        cond_pre = embedded + sinusoid(step_ids, tensor_place * head_cols, head_cols)
        return label_hot, cond_pre

    _, cond_own = condition(labels[0], tsteps[0])
    bias_full = lax.dynamic_update_slice_in_dim(
        jnp.zeros((6 * width,), jnp.float32), b_mod, tensor_place * bias_len, 0
    )
    modul = rows_dot(jax.nn.silu(cond_own).astype(jnp.bfloat16), w_mod) + bias_full[None, :]
    modul = modul + swap(modul, "tensor", 1)
    modul_pair = modul
    modul = modul + swap(modul, "tensor", 2)
    pad_row = jnp.arange(heads * PAD, dtype=jnp.int32)[:, None]
    flat_col = jnp.arange(head_cols, dtype=jnp.int32)[None, :]
    squeeze = (
        (pad_row // PAD == flat_col // HEAD_DIM) & (pad_row % PAD == lane_of(flat_col % HEAD_DIM))
    ).astype(jnp.bfloat16)
    w_wide = [dot_cols(after(w, modul_pair), squeeze).astype(jnp.bfloat16) for w in (w_query, w_key, w_value)]
    w_out_wide = rows_dot(squeeze, after(w_out, modul_pair)).astype(jnp.bfloat16)
    rel_ids = jnp.sum(rel_int * slot_ids[None, :], axis=1)
    rel_pick = (rel_ids[:, None] == item_ids[None, :]).astype(jnp.float32)
    grid_row, grid_col = grid_positions(slot_ids)

    def rel_tokens(per_token):
        return jnp.sum(rel_int[:, :, None] * per_token.reshape(1, slot_count, SLOT_TOK), axis=1).reshape(-1)

    table = rope_table(*(after(rel_tokens(g), modul_pair) for g in (grid_row, grid_col)))
    extras = lane_extras(rel_ids, item_count)
    gain_lane = lane_of(jnp.arange(HEAD_DIM, dtype=jnp.int32))[:, None] == jnp.arange(PAD)[None, :]
    gains = jnp.dot(
        jnp.stack([q_gain, k_gain]), gain_lane.astype(jnp.float32), precision=lax.Precision.HIGHEST
    )

    per_slot = jnp.dot(rel_pick, modul, precision=lax.Precision.HIGHEST)
    shift_a, scale_a, gate_a, shift_m, scale_m, gate_m = jnp.split(per_slot[:1], 6, axis=1)
    cot_now = after(cotangent, modul)
    far_cot = swap(cot_now, "tensor", 2)
    near_cot = swap(cot_now, "tensor", 1)

    slot_mods = per_slot[:, None, :]
    near_set = prepare((tokens, near_tokens), slot_mods, w_wide, table, gains, extras, 0)
    far_tokens = after(far_tokens, near_set[2])
    attn_all, lin, q, k, v = prepare(
        (far_tokens, swap(far_tokens, "tensor", 1)), slot_mods, w_wide, table, gains, extras, 2, near_set
    )
    far_mixed, far_qlog = attend(q, k, v, 1)
    far_sum = pair_sum(rows_dot(far_mixed[half:], w_out_wide)).astype(jnp.bfloat16)
    far_got = swap(far_sum, "tensor", 2)
    far_cot = after(far_cot, far_mixed)
    cot_all = jnp.concatenate([cotangent, near_cot, far_cot, swap(far_cot, "tensor", 1)], axis=0)
    mixed, qlog = attend(after(q, far_sum), k, v, 0, (far_mixed, far_qlog))
    near_sum = pair_sum(rows_dot(mixed[:half], w_out_wide))
    branch_grad = (
        (per_slot[:, None, 5 * width :] * after(cot_all, mixed).astype(jnp.float32).reshape(4, SLOT_TOK, width))
        .astype(jnp.bfloat16)
        .reshape(2 * half, width)
    )
    grad_hidden = dot_cols(branch_grad, w_down)
    mixed_low = rows_dot(mixed, squeeze).astype(jnp.bfloat16)
    attn = near_sum + after(far_got, grad_hidden, mixed_low).astype(jnp.float32)

    resid = tokens.astype(jnp.float32)
    middle = resid + gate_a * attn

    def norm_rows(values, shift_by, scale_by):
        return modulated_norm(values[None], shift_by, scale_by)[0]

    normed_two, norm_two_back = jax.vjp(norm_rows, middle, shift_m, scale_m)
    normed_mlp = normed_two.astype(jnp.bfloat16)
    far_normed = swap(normed_mlp, "tensor", 2)
    near_part, *near_mlp = mlp((normed_mlp, swap(normed_mlp, "tensor", 1)), grad_hidden, w_gate, w_up, 0)
    far_normed = after(far_normed, near_part)
    far_part, mlp_all, hidden, gate_grad, up_grad = mlp(
        (far_normed, swap(far_normed, "tensor", 1)), grad_hidden, w_gate, w_up, 2, near_mlp
    )
    sums = DpSums()
    bits = bits_of("dp")
    late_first = bits[1:] + bits[:1]
    down_term = dot_rows(hidden, branch_grad)
    sums.start("down", down_term, late_first)
    far_sum = pair_sum(far_part).astype(jnp.bfloat16)
    far_got = swap(far_sum, "tensor", 2)
    gate_term = dot_rows(after(mlp_all, far_sum), gate_grad)
    sums.start("gate", gate_term, bits)
    up_term = dot_rows(after(mlp_all, gate_term), up_grad)
    sums.start("up", up_term, bits)
    near_sum = pair_sum(after(near_part, up_term))
    branch_far = pair_sum(rows_dot(after(hidden, near_sum)[half:], w_down)).astype(jnp.bfloat16)
    branch_near = pair_sum(rows_dot(after(hidden, near_sum)[:half], w_down))
    grad_normed_mlp = near_sum + after(far_got, branch_near).astype(jnp.float32)

    grad_out = cotangent.astype(jnp.float32)
    grad_mid_norm, grad_shift_m, grad_scale_m = norm_two_back(grad_normed_mlp)
    grad_middle = grad_out + grad_mid_norm
    grad_gate_a = jnp.sum(attn * grad_middle, axis=0, keepdims=True)
    grad_attn = (gate_a * grad_middle).astype(jnp.bfloat16)
    far_ga = swap(grad_attn, "tensor", 2)
    near_pull = pull(
        (grad_attn, swap(grad_attn, "tensor", 1)), mixed, qlog, k, v, w_out_wide, squeeze, gains, table, lin, 0
    )
    far_ga = after(far_ga, near_pull[0])
    branch_got = swap(after(branch_far, far_ga), "tensor", 2)
    tick = sums.step("down", near_pull[0])
    tick = sums.step("gate", near_pull[0], tick)
    ga_all, q_low, q_wide, gain_q, sum_k, sum_v = pull(
        (far_ga, after(swap(far_ga, "tensor", 1), tick)), mixed, qlog, k, v, w_out_wide, squeeze, gains, table, lin,
        2, near_pull[:3], near_pull[3:],
    )
    tick = sums.step("gate", q_low)
    tick = sums.step("up", q_low, tick)
    far_part, gain_far, *far_low = finish(
        after(q_wide, tick), sum_k, sum_v, lin, squeeze, gains, table, w_wide, 2
    )
    tick = sums.step("down", far_part)
    far_sum = pair_sum(after(far_part, tick)).astype(jnp.bfloat16)
    far_got = swap(far_sum, "tensor", 2)
    near_part, gain_near, k_low, v_low = finish(
        after(q_wide, far_sum), sum_k, sum_v, lin, squeeze, gains, table, w_wide, 0, far_low
    )
    query_term = dot_rows(after(attn_all, near_part), q_low)
    sums.start("query", query_term, bits)
    key_term = dot_rows(after(attn_all, query_term), k_low)
    sums.start("key", key_term, late_first)
    value_term = dot_rows(after(attn_all, key_term), v_low)
    sums.start("value", value_term, bits)
    tick = sums.step("down", value_term)
    tick = sums.step("gate", value_term, tick)
    tick = sums.step("up", value_term, tick)
    out_term = dot_rows(after(mixed_low, tick), ga_all)
    sums.start("out", out_term, late_first)
    near_sum = pair_sum(after(near_part, tick))
    grad_normed_attn = near_sum + after(far_got, tick).astype(jnp.float32)
    gain_grads = head_order(jnp.concatenate([gain_q[:1], gain_far[:1] + gain_near[:1]], axis=0))

    branch = branch_near + after(branch_got, far_part).astype(jnp.float32)
    output = (middle + gate_m * branch).astype(jnp.bfloat16)
    grad_gate_m = jnp.sum(branch * grad_out, axis=0, keepdims=True)

    _, norm_one_back = jax.vjp(norm_rows, resid, shift_a, scale_a)
    grad_resid_norm, grad_shift_a, grad_scale_a = norm_one_back(grad_normed_attn)
    grad_tokens = (grad_middle + grad_resid_norm).astype(jnp.bfloat16)

    grad_slot = jnp.concatenate(
        [
            grad_shift_a,
            grad_scale_a,
            grad_gate_a,
            grad_shift_m,
            grad_scale_m,
            grad_gate_m,
            gain_grads[:1],
            gain_grads[1:],
        ],
        axis=1,
    )
    pair_slots = jnp.concatenate([grad_slot, swap(grad_slot, "tensor", 2)], axis=0)
    grad_slots = jnp.concatenate([pair_slots, swap(pair_slots, "tensor", 1)], axis=0)
    mod_width = 6 * width
    pick_order = jnp.stack([rel_pick[0], rel_pick[2], rel_pick[1], rel_pick[3]])
    grad_items = lax.dot_general(
        pick_order,
        grad_slots[:, :mod_width],
        CONTRACT_ROWS,
        precision=lax.Precision.HIGHEST,
        preferred_element_type=jnp.float32,
    ).astype(jnp.bfloat16)
    gain_sum = jnp.sum(grad_slots[:, mod_width:], axis=0, keepdims=True)
    gain_rows = jnp.pad(gain_sum, ((0, item_count - 1), (0, 0)))
    ids = jnp.stack([labels[0] // 32, labels[0] % 32, tsteps[0] // 32, tsteps[0] % 32], axis=1)
    item_rows = jnp.concatenate([gain_rows, ids.astype(jnp.float32)], axis=1).astype(jnp.bfloat16)
    items_all = gather_dp(jnp.concatenate([grad_items, item_rows], axis=1))
    grad_modul_low = items_all[:, :mod_width]
    gains_end = mod_width + 2 * HEAD_DIM
    gain_total = jnp.sum(items_all[:, mod_width:gains_end].astype(jnp.float32), axis=0)
    grad_q_gain = gain_total[:HEAD_DIM]
    grad_k_gain = gain_total[HEAD_DIM:]
    ids = items_all[:, gains_end:].astype(jnp.int32)
    label_hot, cond_pre = condition(ids[:, 0] * 32 + ids[:, 1], ids[:, 2] * 32 + ids[:, 3])
    cond_full, silu_back = jax.vjp(jax.nn.silu, cond_pre)
    grad_w_mod = lax.dot_general(
        cond_full.astype(jnp.bfloat16), grad_modul_low, CONTRACT_ROWS, preferred_element_type=jnp.float32
    )
    grad_bias_full = jnp.sum(grad_modul_low.astype(jnp.float32), axis=0)
    grad_b_mod = lax.dynamic_slice_in_dim(grad_bias_full, tensor_place * bias_len, bias_len, 0)
    grad_cond_pre = silu_back(dot_cols(grad_modul_low, w_mod))[0]
    grad_class_table = lax.dot_general(
        label_hot,
        grad_cond_pre,
        CONTRACT_ROWS,
        precision=lax.Precision.HIGHEST,
        preferred_element_type=jnp.float32,
    )
    grad_w = sums.finish(TAIL_ORDER, grad_normed_attn)
    return (
        output,
        grad_tokens,
        grad_w["query"],
        grad_w["key"],
        grad_w["value"],
        grad_w["out"],
        grad_w["gate"],
        grad_w["up"],
        grad_w["down"],
        grad_w_mod,
        grad_b_mod,
        grad_class_table,
        grad_q_gain,
        grad_k_gain,
    )


def solution(mesh):
    in_specs = (
        P(("dp", "tensor"), None),
        P(None, "tensor"),
        P(None, "tensor"),
        P(None, "tensor"),
        P("tensor", None),
        P(None, "tensor"),
        P(None, "tensor"),
        P("tensor", None),
        P("tensor", None),
        P("tensor"),
        P(None, "tensor"),
        P(),
        P(),
        P("dp", None),
        P("dp", None),
        P("dp", None),
        P(("dp", "tensor"), None),
    )
    out_specs = (
        P(("dp", "tensor"), None),
        P(("dp", "tensor"), None),
        P(None, "tensor"),
        P(None, "tensor"),
        P(None, "tensor"),
        P("tensor", None),
        P(None, "tensor"),
        P(None, "tensor"),
        P("tensor", None),
        P("tensor", None),
        P("tensor"),
        P(None, "tensor"),
        P(),
        P(),
    )
    return jax.shard_map(local, mesh=mesh, in_specs=in_specs, out_specs=out_specs, check_vma=False)
```

```python
import functools
import math

import jax
import jax.numpy as jnp
from jax import lax
from jax.experimental import pallas as pl
from jax.experimental.pallas import tpu as pltpu
from jax.sharding import PartitionSpec as P

D = 1152
HEAD_DIM = 72
PAD = 128
SIDE = 16
SLOT_TOK = 256
EPSILON = 1e-06
SCORE_LOG2 = math.log2(math.e) / math.sqrt(HEAD_DIM)
INV_ROOT = 1.0 / math.sqrt(HEAD_DIM)
BACK_LANE = PAD // 2
TOTAL_LANE = HEAD_DIM // 2
DOT_LANE = TOTAL_LANE + 1
ITEM_LANE = TOTAL_LANE + 4
LOG_LANE = ITEM_LANE + 8
FAR_ITEM = 16384.0
CONTRACT_ROWS = (((0,), (0,)), ((), ()))
CONTRACT_COLS = (((1,), (1,)), ((), ()))
VMEM_LIMIT = 28 * 1024 * 1024


def sinusoid(step_ids, first_col, col_count):
    half_width = D // 2
    feature = first_col + jnp.arange(col_count, dtype=jnp.int32)
    freq_index = (feature % half_width).astype(jnp.float32)
    rates = jnp.exp(-math.log(10000.0) * freq_index / half_width)
    angles = step_ids.astype(jnp.float32)[:, None] * rates[None, :]
    return jnp.where(feature[None, :] < half_width, jnp.cos(angles), jnp.sin(angles))


def grid_positions(slot_ids):
    slot_count = slot_ids.shape[0]
    slot_order = jnp.arange(slot_count, dtype=jnp.int32)
    same_item = (slot_ids[:, None] == slot_ids[None, :]) & (slot_ids[:, None] >= 0)
    members = jnp.sum(same_item.astype(jnp.int32), axis=1)
    first_slot = jnp.min(jnp.where(same_item, slot_order[None, :], slot_count), axis=1)
    first_slot = jnp.where(members > 0, first_slot, slot_order)
    side_len = jnp.where(members > 1, 2 * SIDE, SIDE)
    within = jnp.arange(SLOT_TOK, dtype=jnp.int32)
    place_in = (slot_order - first_slot)[:, None] * SLOT_TOK + within[None, :]
    return ((place_in // side_len[:, None]).reshape(-1), (place_in % side_len[:, None]).reshape(-1))


def modulated_norm(values, shift_by, scale_by):
    normed = values * lax.rsqrt(jnp.mean(values * values, axis=-1, keepdims=True) + EPSILON)
    return normed * (1.0 + scale_by[:, None, :]) + shift_by[:, None, :]


def full_dot(left, right, dims=(((1,), (0,)), ((), ()))):
    return lax.dot_general(left, right, dims, preferred_element_type=jnp.float32)


def rotate(values, cosine, sine):
    return values * cosine + pltpu.roll(values, BACK_LANE, 1) * sine


def lane_sum(values, on_mxu):
    if on_mxu:
        return full_dot(values.astype(jnp.bfloat16), jnp.ones((PAD, PAD), jnp.bfloat16))
    return jnp.sum(values, axis=-1, keepdims=True)


def head_inverse(lin, on_mxu):
    return lax.rsqrt(lane_sum(lin * lin, on_mxu) * (1.0 / HEAD_DIM) + EPSILON)


def table_parts(table_ref):
    return table_ref[:, :PAD], table_ref[:, PAD:]


def whole(array):
    return pl.BlockSpec(array.shape, lambda i: (0,) * array.ndim)


def pick_rows(first_ref, second_ref):
    return jnp.where(pl.program_id(0) == 0, first_ref[...], second_ref[...])


def slot_rows(cols, first):
    return pl.BlockSpec((SLOT_TOK, cols), lambda i: (i + first, 0))


def call_kernel(body, grid, args, in_specs, out_shape, out_specs, carried, flops, exps=0, first_carried=0):
    carried = [] if carried is None else list(carried)
    count = len(args)
    moved = sum(a.size * a.dtype.itemsize for a in args)

    def wrapped(*refs):
        body(*refs[:count], *refs[count + len(carried) :])

    return pl.pallas_call(
        wrapped,
        grid=grid,
        in_specs=list(in_specs) + [pl.BlockSpec(memory_space=pl.ANY)] * len(carried),
        out_shape=out_shape,
        out_specs=out_specs,
        input_output_aliases={count + i: first_carried + i for i in range(len(carried))},
        compiler_params=pltpu.CompilerParams(vmem_limit_bytes=VMEM_LIMIT),
        cost_estimate=pl.CostEstimate(flops=flops, bytes_accessed=moved, transcendentals=exps),
    )(*args, *carried)


def prepare_kernel(
    own_ref, other_ref, mod_ref, wq_ref, wk_ref, wv_ref, table_ref, gain_ref, extra_ref,
    normed_ref, lin_ref, q_ref, k_ref, v_ref,
):
    heads = q_ref.shape[1] // PAD
    span = heads * PAD
    width = own_ref.shape[1]
    for slot, rows_ref in enumerate((own_ref, other_ref)):
        x = rows_ref[...].astype(jnp.float32)
        rms = lax.rsqrt(jnp.mean(x * x, axis=-1, keepdims=True) + EPSILON)
        shift_by = mod_ref[slot, :, :width]
        scale_by = mod_ref[slot, :, width:]
        normed_ref[slot * SLOT_TOK : (slot + 1) * SLOT_TOK, :] = (
            x * rms * (1.0 + scale_by) + shift_by
        ).astype(jnp.bfloat16)
    normed = normed_ref[...]
    in_first = lax.broadcasted_iota(jnp.int32, (2 * SLOT_TOK, PAD), 0) < SLOT_TOK
    cosine, sine = table_parts(table_ref)
    for part, w_ref in enumerate((wq_ref, wk_ref, wv_ref)):
        lin = full_dot(normed, w_ref[...])
        for h in range(heads):
            cols = slice(h * PAD, (h + 1) * PAD)
            piece = lin[:, cols]
            extra = jnp.where(in_first, extra_ref[0, part : part + 1, :], extra_ref[1, part : part + 1, :])
            if part == 2:
                v_ref[:, cols] = (piece + extra).astype(jnp.bfloat16)
                continue
            lin_ref[:, part * span + h * PAD : part * span + (h + 1) * PAD] = piece.astype(jnp.bfloat16)
            gain = gain_ref[part : part + 1, :]
            turned = rotate(piece * head_inverse(piece, True) * gain, cosine, sine)
            out_ref = q_ref if part == 0 else k_ref
            out_ref[:, cols] = (turned + extra).astype(jnp.bfloat16)


def prepare(pair, per_slot, weights, table, gains, extras, part, carried=None):
    rows, width = 2 * SLOT_TOK, pair[0].shape[1]
    span = weights[0].shape[1]
    all_rows = table.shape[0]
    sizes = (width, 2 * span, span, span, span)
    half_rows = lambda cols: pl.BlockSpec((rows, cols), lambda i: (part, 0))
    return call_kernel(
        prepare_kernel,
        (1,),
        [*pair, per_slot, *weights, table, gains, extras],
        [
            *(whole(rows_in) for rows_in in pair),
            pl.BlockSpec((2, 1, 2 * width), lambda i: (part, 0, 0)),
            *(whole(w) for w in weights),
            half_rows(2 * PAD),
            whole(gains),
            pl.BlockSpec((2, 3, PAD), lambda i: (part, 0, 0)),
        ],
        [jax.ShapeDtypeStruct((all_rows, cols), jnp.bfloat16) for cols in sizes],
        [half_rows(cols) for cols in sizes],
        carried,
        6 * rows * width * span,
    )


def split_lanes(values, first_lane, shape):
    lane = lax.broadcasted_iota(jnp.int32, shape, 1)
    high = values.astype(jnp.bfloat16).astype(jnp.float32)
    rest = values - high
    mid = rest.astype(jnp.bfloat16).astype(jnp.float32)
    low = rest - mid
    return jnp.where(
        lane == first_lane,
        high,
        jnp.where(lane == first_lane + 1, mid, jnp.where(lane == first_lane + 2, low, 0.0)),
    )


def attend_kernel(q_ref, key_ref, value_ref, mixed_ref, qlog_ref):
    half = key_ref.shape[0] // 2
    for first in range(0, q_ref.shape[0], SLOT_TOK):
        rows = slice(first, first + SLOT_TOK)
        q = q_ref[rows, :]
        total = None
        for start in (0, half):
            keys = slice(start, start + half)
            weight = jnp.exp2(full_dot(q, key_ref[keys, :], CONTRACT_COLS) * SCORE_LOG2)
            term = full_dot(weight.astype(jnp.bfloat16), value_ref[keys, :])
            total = term if total is None else total + term
        row_sum = total[:, TOTAL_LANE : TOTAL_LANE + 1]
        mixed_ref[rows, :] = (total * (1.0 / row_sum)).astype(jnp.bfloat16)
        log_sum = jnp.log2(row_sum) * (-1.0 / SCORE_LOG2)
        qlog_ref[rows, :] = (q.astype(jnp.float32) + split_lanes(log_sum, LOG_LANE, q.shape)).astype(
            jnp.bfloat16
        )


def attend(q, k, v, part, carried=None):
    all_rows, span = q.shape
    rows = all_rows // 2
    heads = span // PAD
    mine = pl.BlockSpec((rows, PAD), lambda h: (part, h))
    every = pl.BlockSpec((all_rows, PAD), lambda h: (0, h))
    return call_kernel(
        attend_kernel,
        (heads,),
        [q, k, v],
        [mine, every, every],
        [jax.ShapeDtypeStruct(q.shape, jnp.bfloat16)] * 2,
        [mine, mine],
        carried,
        4 * rows * all_rows * span,
        rows * all_rows * heads,
    )


def unturn(grad, lin, gain, cosine, sine, on_mxu):
    turned = rotate(grad, cosine, -sine)
    inverse = head_inverse(lin, on_mxu)
    normed = lin * inverse
    gained = turned * gain
    mean = lane_sum(gained * normed, on_mxu) * (1.0 / HEAD_DIM)
    return inverse * (gained - normed * mean), jnp.sum(turned * normed, axis=0, keepdims=True)


def pull_kernel(
    own_ref, other_ref, mixed_ref, q_ref, key_ref, value_ref, wo_ref, squeeze_ref, gain_ref, table_ref, lin_ref,
    *rest,
):
    *before, ga_ref, dq_ref, wide_ref, gains_ref, dk_ref, dv_ref = rest
    heads = q_ref.shape[1] // PAD
    half = key_ref.shape[0] // 2

    @pl.when(pl.program_id(0) == 0)
    def _():
        if before:
            gains_before, dk_before, dv_before = before
            gains_ref[...] = gains_before[...]
            dk_ref[...] = dk_before[...]
            dv_ref[...] = dv_before[...]
        else:
            gains_ref[...] = jnp.zeros_like(gains_ref)
            dk_ref[...] = jnp.zeros_like(dk_ref)
            dv_ref[...] = jnp.zeros_like(dv_ref)

    cosine, sine = table_parts(table_ref)
    grad_attn = pick_rows(own_ref, other_ref)
    ga_ref[...] = grad_attn
    grad_mixed = full_dot(grad_attn, wo_ref[...], CONTRACT_COLS).astype(jnp.bfloat16)
    gain_sum = jnp.zeros((1, PAD), jnp.float32)
    for h in range(heads):
        cols = slice(h * PAD, (h + 1) * PAD)
        grad_low = grad_mixed[:, cols]
        grad_head = grad_low.astype(jnp.float32)
        mixed = mixed_ref[:, cols].astype(jnp.float32)
        row_dot = jnp.sum(grad_head * mixed, axis=-1, keepdims=True)
        grad_aug = (grad_head + split_lanes(-row_dot, DOT_LANE, grad_head.shape)).astype(jnp.bfloat16)
        q = q_ref[:, cols]
        dq = None
        for start in (0, half):
            key_rows = slice(start, start + half)
            key, value = key_ref[key_rows, cols], value_ref[key_rows, cols]
            probs = jnp.exp2(full_dot(key, q, CONTRACT_COLS) * SCORE_LOG2)
            grad_probs = full_dot(value, grad_aug, CONTRACT_COLS)
            grad_scores = (probs * grad_probs).astype(jnp.bfloat16)
            dv_ref[key_rows, cols] += full_dot(probs.astype(jnp.bfloat16), grad_low)
            dk_ref[key_rows, cols] += full_dot(grad_scores, q)
            term = full_dot(grad_scores, key, CONTRACT_ROWS)
            dq = term if dq is None else dq + term
        lin = lin_ref[:, cols].astype(jnp.float32)
        grad_lin, gain_term = unturn(dq * INV_ROOT, lin, gain_ref[0:1, :], cosine, sine, False)
        gain_sum = gain_sum + gain_term
        wide_ref[:, cols] = grad_lin.astype(jnp.bfloat16)
    gains_ref[0:1, :] += gain_sum
    dq_ref[...] = full_dot(wide_ref[...], squeeze_ref[...]).astype(jnp.bfloat16)


def pull(pair, mixed, qlog, k, v, w_out, squeeze, gains, table, lin, first, carried=None, earlier=None):
    rows, width = 2 * SLOT_TOK, pair[0].shape[1]
    all_rows, span = qlog.shape
    compact = squeeze.shape[1]
    args = [*pair, mixed, qlog, k, v, w_out, squeeze, gains, table, lin]
    specs = [*(whole(a) for a in pair), slot_rows(span, first), slot_rows(span, first)]
    specs += [whole(a) for a in (k, v, w_out, squeeze, gains)]
    specs += [slot_rows(2 * PAD, first), slot_rows(span, first)]
    sums = [jax.ShapeDtypeStruct(shape, jnp.float32) for shape in ((8, PAD), (all_rows, span), (all_rows, span))]
    if earlier is not None:
        args += earlier
        specs += [whole(a) for a in earlier]
    kept = [jax.ShapeDtypeStruct((all_rows, cols), jnp.bfloat16) for cols in (width, compact, span)]
    return call_kernel(
        pull_kernel,
        (rows // SLOT_TOK,),
        args,
        specs,
        kept + sums,
        [slot_rows(a.shape[1], first) for a in kept] + [whole(a) for a in sums],
        carried,
        10 * rows * all_rows * span,
        rows * all_rows * span // PAD,
    )


def finish_kernel(
    dq_ref, dk_ref, dv_ref, lin_ref, squeeze_ref, gain_ref, table_ref, wq_ref, wk_ref, wv_ref,
    part_ref, gains_ref, kc_ref, vc_ref,
):
    @pl.when(pl.program_id(0) == 0)
    def _():
        gains_ref[...] = jnp.zeros_like(gains_ref)

    cosine, sine = table_parts(table_ref)
    gain_sum = jnp.zeros((1, PAD), jnp.float32)
    k_grads = []
    for h in range(dk_ref.shape[1] // PAD):
        cols = slice(h * PAD, (h + 1) * PAD)
        grad_lin, gain_term = unturn(
            dk_ref[:, cols] * INV_ROOT, lin_ref[:, cols].astype(jnp.float32), gain_ref[1:2, :], cosine, sine, True
        )
        gain_sum = gain_sum + gain_term
        k_grads.append(grad_lin.astype(jnp.bfloat16))
    gains_ref[0:1, :] += gain_sum
    k_wide = jnp.concatenate(k_grads, axis=1)
    v_wide = dv_ref[...].astype(jnp.bfloat16)
    kc_ref[...] = full_dot(k_wide, squeeze_ref[...]).astype(jnp.bfloat16)
    vc_ref[...] = full_dot(v_wide, squeeze_ref[...]).astype(jnp.bfloat16)
    part_ref[...] = (
        full_dot(dq_ref[...], wq_ref[...], CONTRACT_COLS)
        + full_dot(k_wide, wk_ref[...], CONTRACT_COLS)
        + full_dot(v_wide, wv_ref[...], CONTRACT_COLS)
    ).astype(jnp.bfloat16)


def finish(dq, dk, dv, lin, squeeze, gains, table, weights, first, carried=None):
    all_rows, span = dk.shape
    rows = all_rows // 2
    width, compact = weights[0].shape[0], squeeze.shape[1]
    kept = [jax.ShapeDtypeStruct((all_rows, compact), jnp.bfloat16)] * 2
    fresh = [jax.ShapeDtypeStruct((rows, width), jnp.bfloat16), jax.ShapeDtypeStruct((8, PAD), jnp.float32)]
    return call_kernel(
        finish_kernel,
        (rows // SLOT_TOK,),
        [dq, dk, dv, lin, squeeze, gains, table, *weights],
        [
            slot_rows(span, first),
            slot_rows(span, first),
            slot_rows(span, first),
            pl.BlockSpec((SLOT_TOK, span), lambda i: (i + first, 1)),
            whole(squeeze),
            whole(gains),
            slot_rows(2 * PAD, first),
            *(whole(w) for w in weights),
        ],
        fresh + kept,
        [slot_rows(width, 0), whole(fresh[1])] + [slot_rows(compact, first)] * 2,
        carried,
        6 * rows * span * width,
        first_carried=2,
    )


def mlp_kernel(own_ref, other_ref, gh_ref, wg_ref, wu_ref, part_ref, rows_ref, hidden_ref, grad_ref):
    rows = pick_rows(own_ref, other_ref)
    rows_ref[...] = rows
    gate_lin = full_dot(rows, wg_ref[...])
    up_lin = full_dot(rows, wu_ref[...])
    grad_hidden = gh_ref[...]
    sigmoid = 1.0 / (1.0 + jnp.exp(-gate_lin))
    silu = gate_lin * sigmoid
    hidden_ref[...] = (silu * up_lin).astype(jnp.bfloat16)
    grad_up = (grad_hidden * silu).astype(jnp.bfloat16)
    grad_gate = (grad_hidden * up_lin * (sigmoid + silu * (1.0 - sigmoid))).astype(jnp.bfloat16)
    units = wg_ref.shape[1]
    grad_ref[:, :units] = grad_gate
    grad_ref[:, units:] = grad_up
    part_ref[...] = (
        full_dot(grad_gate, wg_ref[...], CONTRACT_COLS) + full_dot(grad_up, wu_ref[...], CONTRACT_COLS)
    ).astype(jnp.bfloat16)


def mlp(pair, grad_hidden, w_gate, w_up, first, carried=None):
    rows, width = 2 * SLOT_TOK, pair[0].shape[1]
    all_rows, units = grad_hidden.shape
    kept = [jax.ShapeDtypeStruct((all_rows, cols), jnp.bfloat16) for cols in (width, units, 2 * units)]
    return call_kernel(
        mlp_kernel,
        (rows // SLOT_TOK,),
        [*pair, grad_hidden, w_gate, w_up],
        [*(whole(a) for a in pair), slot_rows(units, first), whole(w_gate), whole(w_up)],
        [jax.ShapeDtypeStruct((rows, width), jnp.bfloat16), *kept],
        [slot_rows(width, 0)] + [slot_rows(a.shape[1], first) for a in kept],
        carried,
        8 * rows * width * units,
        rows * units,
        first_carried=1,
    )


PLAN = {
    "down": ("down",),
    "terms": ("early",),
    "near": ("down",),
    "middle": ("early", "late"),
    "pulled": ("down", "early", "late"),
    "pulled_far": ("down", "early", "late"),
    "finished_far": ("down", "early", "late"),
    "query": ("early", "query", "late"),
    "key": ("key", "down", "late"),
    "tail": (
        "query", "key", "early", "query", "key", "late", "items", "query", "key", "items", "query", "key", "down",
        "items", "query", "key", "items",
    ),
}


def swap(values, axis_name, bit):
    count = lax.axis_size(axis_name)
    return lax.ppermute(values, axis_name, [(i, i ^ bit) for i in range(count)])


def after(values, *earlier):
    return lax.optimization_barrier((values, *earlier))[0]


def bits_of(axis_name):
    count = lax.axis_size(axis_name)
    bits = []
    bit = 1
    while bit < count:
        bits.append(bit)
        bit *= 2
    assert bit == count
    return bits


def halving_steps(first, second, bits, earlier):
    place = lax.axis_index("dp")
    upper = (place // bits[0]) % 2 == 1
    first = after(first, *earlier)
    send = jnp.where(upper, first, second)
    got = swap(send, "dp", bits[0])
    earlier = yield send
    low = after(jnp.where(upper, second, first), *earlier)
    low = (low.astype(jnp.float32) + got.astype(jnp.float32)).astype(jnp.bfloat16)
    for bit in bits[1:]:
        half = low.shape[0] // 2
        part = (place // bit) % 2
        send = lax.dynamic_slice_in_dim(low, (1 - part) * half, half, 0)
        got = swap(send, "dp", bit)
        earlier = yield send
        mine = lax.dynamic_slice_in_dim(after(low, *earlier), part * half, half, 0)
        low = (mine.astype(jnp.float32) + got.astype(jnp.float32)).astype(jnp.bfloat16)
    for bit in reversed(bits[1:]):
        got = swap(low, "dp", bit)
        earlier = yield low
        low = after(low, *earlier)
        low = jnp.where(
            (place // bit) % 2 == 1, jnp.concatenate([got, low], axis=0), jnp.concatenate([low, got], axis=0)
        )
    got = swap(low, "dp", bits[0])
    earlier = yield low
    low = after(low, *earlier)
    yield jnp.where(upper, got, low), jnp.where(upper, low, got)


def gather_steps(values, earlier):
    values = after(values, *earlier)
    for bit in reversed(bits_of("dp")):
        got = swap(values, "dp", bit)
        earlier = yield values
        values = jnp.concatenate([after(values, *earlier), got], axis=0)
    yield (values,)


class DpSums:
    def __init__(self):
        self.steps = {}
        self.newest = {}

    def offer(self, name, steps):
        self.steps[name] = steps
        self.newest[name] = None

    def step(self, name, *earlier):
        if self.newest[name] is None:
            self.steps[name] = self.steps[name](earlier)
            self.newest[name] = next(self.steps[name])
        elif not isinstance(self.newest[name], tuple):
            self.newest[name] = self.steps[name].send(earlier)
        newest = self.newest[name]
        return newest[0] if isinstance(newest, tuple) else newest

    def at(self, point, tick):
        for name in PLAN[point]:
            tick = self.step(name, tick)
        return tick

    def finish(self, tick):
        tick = self.at("tail", tick)
        while not all(isinstance(newest, tuple) for newest in self.newest.values()):
            for name in self.newest:
                tick = self.step(name, tick)
        return self.newest


def rows_dot(source, weight):
    return jnp.dot(source, weight, preferred_element_type=jnp.float32)


def dot_cols(source, weight):
    return lax.dot_general(source, weight, CONTRACT_COLS, preferred_element_type=jnp.float32)


def dot_rows(left, right):
    return lax.dot_general(
        left, right, CONTRACT_ROWS, preferred_element_type=jnp.float32
    ).astype(jnp.bfloat16)


def pair_sum(part):
    low = part.astype(jnp.bfloat16)
    got = swap(low[SLOT_TOK:], "tensor", 1)
    return low[:SLOT_TOK].astype(jnp.float32) + got.astype(jnp.float32)


def lane_of(dims):
    quarter = HEAD_DIM // 4
    pair, rest = dims // (2 * quarter), dims % (2 * quarter)
    return pair * quarter + jnp.where(rest < quarter, rest, BACK_LANE + rest - quarter)


def head_order(values):
    quarter = HEAD_DIM // 4
    return jnp.concatenate(
        [values[:, first : first + quarter] for first in (0, BACK_LANE, quarter, BACK_LANE + quarter)], axis=1
    )


def rope_table(grid_row, grid_col):
    quarter = HEAD_DIM // 4
    lane = jnp.arange(2 * PAD, dtype=jnp.int32)
    dim = lane % BACK_LANE
    rates = jnp.exp(-math.log(10000.0) * (dim % quarter).astype(jnp.float32) / quarter)
    places = jnp.arange(2 * SIDE, dtype=jnp.int32)
    angles = places.astype(jnp.float32)[:, None] * rates[None]
    sine_v = jnp.where((lane % PAD < BACK_LANE)[None], -jnp.sin(angles), jnp.sin(angles))
    values = jnp.where((lane < PAD)[None], jnp.cos(angles), sine_v)
    by_row = jnp.where((dim < quarter)[None], values, 0.0)
    by_col = jnp.where(((dim >= quarter) & (dim < 2 * quarter))[None], values, 0.0)
    hot = jnp.concatenate([grid[:, None] == places[None] for grid in (grid_row, grid_col)], axis=1)
    return jnp.dot(
        hot.astype(jnp.float32), jnp.concatenate([by_row, by_col], axis=0), precision=lax.Precision.HIGHEST
    )


def lane_extras(slot_ids, item_count):
    lane = jnp.arange(PAD, dtype=jnp.int32)
    hot = (lane - ITEM_LANE)[None] == (slot_ids + 1)[:, None]
    item_lane = ((lane >= ITEM_LANE) & (lane <= ITEM_LANE + item_count))[None]
    log_lane = ((lane >= LOG_LANE) & (lane < LOG_LANE + 3))[None]
    for_key = jnp.where(item_lane & ~hot, -FAR_ITEM, 0.0) + jnp.where(log_lane, 1.0, 0.0)
    for_value = jnp.broadcast_to(((lane >= TOTAL_LANE) & (lane < DOT_LANE + 3))[None], hot.shape)
    return jnp.stack([hot.astype(jnp.float32), for_key, for_value.astype(jnp.float32)], axis=1)


def local(
    tokens,
    w_query,
    w_key,
    w_value,
    w_out,
    w_gate,
    w_up,
    w_down,
    w_mod,
    b_mod,
    class_table,
    q_gain,
    k_gain,
    slot_item,
    labels,
    tsteps,
    cotangent,
):
    tensor_count = lax.axis_size("tensor")
    tensor_place = lax.axis_index("tensor")
    slot_count = slot_item.shape[1]
    item_count = labels.shape[1]
    assert tensor_count == 4 and slot_count == 4 and item_count < LOG_LANE - ITEM_LANE
    width = tokens.shape[1]
    head_cols = w_query.shape[1]
    heads = head_cols // HEAD_DIM
    bias_len = b_mod.shape[0]
    slot_ids = slot_item[0]
    half = 2 * SLOT_TOK

    far_tokens = swap(tokens, "tensor", 2)
    near_tokens = swap(tokens, "tensor", 1)

    slots = jnp.arange(slot_count, dtype=jnp.int32)
    rel_hot = (tensor_place ^ slots)[:, None] == slots[None, :]
    rel_int = rel_hot.astype(jnp.int32)
    item_ids = jnp.arange(item_count, dtype=jnp.int32)
    class_ids = jnp.arange(class_table.shape[0], dtype=jnp.int32)

    def condition(label_ids, step_ids):
        label_hot = (label_ids[:, None] == class_ids[None, :]).astype(jnp.float32)
        embedded = rows_dot(label_hot.astype(jnp.bfloat16), class_table)
        cond_pre = embedded + sinusoid(step_ids, tensor_place * head_cols, head_cols)
        return label_hot, cond_pre

    _, cond_own = condition(labels[0], tsteps[0])
    bias_full = lax.dynamic_update_slice_in_dim(
        jnp.zeros((6 * width,), jnp.float32), b_mod, tensor_place * bias_len, 0
    )
    modul = rows_dot(jax.nn.silu(cond_own).astype(jnp.bfloat16), w_mod) + bias_full[None, :]
    modul = modul + swap(modul, "tensor", 1)
    modul_pair = modul
    modul = modul + swap(modul, "tensor", 2)
    pad_row = jnp.arange(heads * PAD, dtype=jnp.int32)[:, None]
    flat_col = jnp.arange(head_cols, dtype=jnp.int32)[None, :]
    squeeze = (
        (pad_row // PAD == flat_col // HEAD_DIM) & (pad_row % PAD == lane_of(flat_col % HEAD_DIM))
    ).astype(jnp.bfloat16)
    w_wide = [dot_cols(after(w, modul_pair), squeeze).astype(jnp.bfloat16) for w in (w_query, w_key, w_value)]
    w_out_wide = rows_dot(squeeze, after(w_out, modul_pair)).astype(jnp.bfloat16)
    rel_ids = jnp.sum(rel_int * slot_ids[None, :], axis=1)
    rel_pick = (rel_ids[:, None] == item_ids[None, :]).astype(jnp.float32)
    grid_row, grid_col = grid_positions(slot_ids)

    def rel_tokens(per_token):
        return jnp.sum(rel_int[:, :, None] * per_token.reshape(1, slot_count, SLOT_TOK), axis=1).reshape(-1)

    table = rope_table(*(after(rel_tokens(g), modul_pair) for g in (grid_row, grid_col)))
    extras = lane_extras(rel_ids, item_count)
    gain_lane = lane_of(jnp.arange(HEAD_DIM, dtype=jnp.int32))[:, None] == jnp.arange(PAD)[None, :]
    gains = jnp.dot(
        jnp.stack([q_gain, k_gain]), gain_lane.astype(jnp.float32), precision=lax.Precision.HIGHEST
    )

    per_slot = jnp.dot(rel_pick, modul, precision=lax.Precision.HIGHEST)
    shift_a, scale_a, gate_a, shift_m, scale_m, gate_m = jnp.split(per_slot[:1], 6, axis=1)
    cot_now = after(cotangent, modul)
    far_cot = swap(cot_now, "tensor", 2)
    near_cot = swap(cot_now, "tensor", 1)

    slot_mods = per_slot[:, None, :]
    near_set = prepare((tokens, near_tokens), slot_mods, w_wide, table, gains, extras, 0)
    far_tokens = after(far_tokens, near_set[2])
    attn_all, lin, q, k, v = prepare(
        (far_tokens, swap(far_tokens, "tensor", 1)), slot_mods, w_wide, table, gains, extras, 1, near_set
    )
    far_mixed, far_qlog = attend(q, k, v, 1)
    far_sum = pair_sum(rows_dot(far_mixed[half:], w_out_wide)).astype(jnp.bfloat16)
    far_got = swap(far_sum, "tensor", 2)
    far_cot = after(far_cot, far_mixed)
    cot_all = jnp.concatenate([cotangent, near_cot, far_cot, swap(far_cot, "tensor", 1)], axis=0)
    mixed, qlog = attend(after(q, far_sum), k, v, 0, (far_mixed, far_qlog))
    near_sum = pair_sum(rows_dot(mixed[:half], w_out_wide))
    branch_grad = (
        (per_slot[:, None, 5 * width :] * after(cot_all, mixed).astype(jnp.float32).reshape(4, SLOT_TOK, width))
        .astype(jnp.bfloat16)
        .reshape(2 * half, width)
    )
    grad_hidden = dot_cols(branch_grad, w_down)
    mixed_low = rows_dot(mixed, squeeze).astype(jnp.bfloat16)
    attn = near_sum + after(far_got, grad_hidden, mixed_low).astype(jnp.float32)

    resid = tokens.astype(jnp.float32)
    middle = resid + gate_a * attn

    def norm_rows(values, shift_by, scale_by):
        return modulated_norm(values[None], shift_by, scale_by)[0]

    normed_two, norm_two_back = jax.vjp(norm_rows, middle, shift_m, scale_m)
    normed_mlp = normed_two.astype(jnp.bfloat16)
    far_normed = swap(normed_mlp, "tensor", 2)
    near_part, *near_mlp = mlp((normed_mlp, swap(normed_mlp, "tensor", 1)), grad_hidden, w_gate, w_up, 0)
    far_normed = after(far_normed, near_part)
    far_part, mlp_all, hidden, gate_up_grad = mlp(
        (far_normed, swap(far_normed, "tensor", 1)), grad_hidden, w_gate, w_up, 2, near_mlp
    )
    sums = DpSums()
    bits = bits_of("dp")
    late_first = bits[1:] + bits[:1]
    half_width = width // 2
    down_term = dot_rows(hidden, branch_grad)
    half_units = down_term.shape[0] // 2
    sums.offer("down", functools.partial(halving_steps, down_term[:half_units], down_term[half_units:], late_first))
    tick = sums.at("down", down_term)
    far_sum = pair_sum(after(far_part, tick)).astype(jnp.bfloat16)
    far_got = swap(far_sum, "tensor", 2)
    units = w_gate.shape[1]
    gate_term = dot_rows(after(mlp_all, far_sum), gate_up_grad[:, :units])
    up_term = dot_rows(after(mlp_all, gate_term), gate_up_grad[:, units:])
    half_width = width // 2
    sums.offer("early", functools.partial(halving_steps, gate_term[:half_width], up_term[:half_width], bits))
    sums.offer("late", functools.partial(halving_steps, gate_term[half_width:], up_term[half_width:], bits))
    tick = sums.at("terms", up_term)
    near_sum = pair_sum(after(near_part, tick))
    branch_far = pair_sum(rows_dot(after(hidden, near_sum)[half:], w_down)).astype(jnp.bfloat16)
    branch_near = pair_sum(rows_dot(after(hidden, near_sum)[:half], w_down))
    tick = sums.at("near", branch_near)
    grad_normed_mlp = near_sum + after(far_got, tick).astype(jnp.float32)

    grad_out = cotangent.astype(jnp.float32)
    grad_mid_norm, grad_shift_m, grad_scale_m = norm_two_back(grad_normed_mlp)
    grad_middle = grad_out + grad_mid_norm
    grad_gate_a = jnp.sum(attn * grad_middle, axis=0, keepdims=True)
    grad_attn = (gate_a * grad_middle).astype(jnp.bfloat16)
    far_ga = swap(grad_attn, "tensor", 2)
    near_ga = swap(grad_attn, "tensor", 1)
    tick = sums.at("middle", grad_attn)
    near_pull = pull(
        (grad_attn, after(near_ga, tick)), mixed, qlog, k, v, w_out_wide, squeeze, gains, table, lin, 0
    )
    far_ga = after(far_ga, near_pull[0])
    diag_ga = swap(far_ga, "tensor", 1)
    tick = sums.at("pulled", near_pull[0])
    ga_all, q_low, q_wide, gain_q, sum_k, sum_v = pull(
        (far_ga, after(diag_ga, tick)), mixed, qlog, k, v, w_out_wide, squeeze, gains, table, lin,
        2, near_pull[:3], near_pull[3:],
    )
    branch_got = swap(after(branch_far, q_low), "tensor", 2)
    tick = sums.at("pulled_far", q_low)
    far_part, gain_far, *far_low = finish(
        after(q_wide, tick), sum_k, sum_v, lin, squeeze, gains, table, w_wide, 2
    )
    far_sum = pair_sum(far_part).astype(jnp.bfloat16)
    far_got = swap(far_sum, "tensor", 2)
    tick = sums.at("finished_far", far_sum)
    near_part, gain_near, k_low, v_low = finish(
        after(q_wide, tick), sum_k, sum_v, lin, squeeze, gains, table, w_wide, 0, far_low
    )
    query_term = dot_rows(after(attn_all, near_part), q_low)
    value_term = dot_rows(after(attn_all, query_term), v_low)
    sums.offer("query", functools.partial(halving_steps, query_term, value_term, bits))
    tick = sums.at("query", value_term)
    key_term = dot_rows(after(k_low, tick), attn_all)
    out_term = dot_rows(mixed_low, after(ga_all, key_term))
    sums.offer("key", functools.partial(halving_steps, key_term, out_term, late_first))
    tick = sums.at("key", out_term)
    near_sum = pair_sum(after(near_part, tick))
    grad_normed_attn = near_sum + after(far_got, tick).astype(jnp.float32)
    gain_grads = head_order(jnp.concatenate([gain_q[:1], gain_far[:1] + gain_near[:1]], axis=0))

    branch = branch_near + after(branch_got, near_part).astype(jnp.float32)
    output = (middle + gate_m * branch).astype(jnp.bfloat16)
    grad_gate_m = jnp.sum(branch * grad_out, axis=0, keepdims=True)

    _, norm_one_back = jax.vjp(norm_rows, resid, shift_a, scale_a)
    grad_resid_norm, grad_shift_a, grad_scale_a = norm_one_back(grad_normed_attn)
    grad_tokens = (grad_middle + grad_resid_norm).astype(jnp.bfloat16)

    grad_slot = jnp.concatenate(
        [
            grad_shift_a,
            grad_scale_a,
            grad_gate_a,
            grad_shift_m,
            grad_scale_m,
            grad_gate_m,
            gain_grads[:1],
            gain_grads[1:],
        ],
        axis=1,
    )
    pair_slots = jnp.concatenate([grad_slot, swap(grad_slot, "tensor", 2)], axis=0)
    grad_slots = jnp.concatenate([pair_slots, swap(pair_slots, "tensor", 1)], axis=0)
    mod_width = 6 * width
    pick_order = jnp.stack([rel_pick[0], rel_pick[2], rel_pick[1], rel_pick[3]])
    grad_items = lax.dot_general(
        pick_order,
        grad_slots[:, :mod_width],
        CONTRACT_ROWS,
        precision=lax.Precision.HIGHEST,
        preferred_element_type=jnp.float32,
    ).astype(jnp.bfloat16)
    gain_sum = jnp.sum(grad_slots[:, mod_width:], axis=0, keepdims=True)
    gain_rows = jnp.pad(gain_sum, ((0, item_count - 1), (0, 0)))
    ids = jnp.stack([labels[0] // 32, labels[0] % 32, tsteps[0] // 32, tsteps[0] % 32], axis=1)
    item_rows = jnp.concatenate([gain_rows, ids.astype(jnp.float32)], axis=1).astype(jnp.bfloat16)
    sums.offer("items", functools.partial(gather_steps, jnp.concatenate([grad_items, item_rows], axis=1)))
    grad_w = sums.finish(near_part)
    items_all = grad_w["items"][0]
    grad_modul_low = items_all[:, :mod_width]
    gains_end = mod_width + 2 * HEAD_DIM
    gain_total = jnp.sum(items_all[:, mod_width:gains_end].astype(jnp.float32), axis=0)
    grad_q_gain = gain_total[:HEAD_DIM]
    grad_k_gain = gain_total[HEAD_DIM:]
    ids = items_all[:, gains_end:].astype(jnp.int32)
    label_hot, cond_pre = condition(ids[:, 0] * 32 + ids[:, 1], ids[:, 2] * 32 + ids[:, 3])
    cond_full, silu_back = jax.vjp(jax.nn.silu, cond_pre)
    grad_w_mod = lax.dot_general(
        cond_full.astype(jnp.bfloat16), grad_modul_low, CONTRACT_ROWS, preferred_element_type=jnp.float32
    )
    grad_bias_full = jnp.sum(grad_modul_low.astype(jnp.float32), axis=0)
    grad_b_mod = lax.dynamic_slice_in_dim(grad_bias_full, tensor_place * bias_len, bias_len, 0)
    grad_cond_pre = silu_back(dot_cols(grad_modul_low, w_mod))[0]
    grad_class_table = lax.dot_general(
        label_hot,
        grad_cond_pre,
        CONTRACT_ROWS,
        precision=lax.Precision.HIGHEST,
        preferred_element_type=jnp.float32,
    )
    wide_rows = lambda parts: jnp.concatenate(parts, axis=0).astype(jnp.float32)
    return (
        output,
        grad_tokens,
        grad_w["query"][0].astype(jnp.float32),
        grad_w["key"][0].T.astype(jnp.float32),
        grad_w["query"][1].astype(jnp.float32),
        grad_w["key"][1].astype(jnp.float32),
        wide_rows([grad_w["early"][0], grad_w["late"][0]]),
        wide_rows([grad_w["early"][1], grad_w["late"][1]]),
        wide_rows(grad_w["down"]),
        grad_w_mod,
        grad_b_mod,
        grad_class_table,
        grad_q_gain,
        grad_k_gain,
    )


def solution(mesh):
    in_specs = (
        P(("dp", "tensor"), None),
        P(None, "tensor"),
        P(None, "tensor"),
        P(None, "tensor"),
        P("tensor", None),
        P(None, "tensor"),
        P(None, "tensor"),
        P("tensor", None),
        P("tensor", None),
        P("tensor"),
        P(None, "tensor"),
        P(),
        P(),
        P("dp", None),
        P("dp", None),
        P("dp", None),
        P(("dp", "tensor"), None),
    )
    out_specs = (
        P(("dp", "tensor"), None),
        P(("dp", "tensor"), None),
        P(None, "tensor"),
        P(None, "tensor"),
        P(None, "tensor"),
        P("tensor", None),
        P(None, "tensor"),
        P(None, "tensor"),
        P("tensor", None),
        P("tensor", None),
        P("tensor"),
        P(None, "tensor"),
        P(),
        P(),
    )
    return jax.shard_map(local, mesh=mesh, in_specs=in_specs, out_specs=out_specs, check_vma=False)
```

```python
import functools
import math

import jax
import jax.numpy as jnp
from jax import lax
from jax.experimental import pallas as pl
from jax.experimental.pallas import tpu as pltpu
from jax.sharding import PartitionSpec as P

D = 1152
HEAD_DIM = 72
PAD = 128
SIDE = 16
SLOT_TOK = 256
EPSILON = 1e-06
SCORE_LOG2 = math.log2(math.e) / math.sqrt(HEAD_DIM)
INV_ROOT = 1.0 / math.sqrt(HEAD_DIM)
BACK_LANE = PAD // 2
TOTAL_LANE = HEAD_DIM // 2
DOT_LANE = TOTAL_LANE + 1
ITEM_LANE = TOTAL_LANE + 4
LOG_LANE = ITEM_LANE + 8
FAR_ITEM = 16384.0
CONTRACT_ROWS = (((0,), (0,)), ((), ()))
CONTRACT_COLS = (((1,), (1,)), ((), ()))
VMEM_LIMIT = 28 * 1024 * 1024


def sinusoid(step_ids, first_col, col_count):
    half_width = D // 2
    feature = first_col + jnp.arange(col_count, dtype=jnp.int32)
    freq_index = (feature % half_width).astype(jnp.float32)
    rates = jnp.exp(-math.log(10000.0) * freq_index / half_width)
    angles = step_ids.astype(jnp.float32)[:, None] * rates[None, :]
    return jnp.where(feature[None, :] < half_width, jnp.cos(angles), jnp.sin(angles))


def grid_positions(slot_ids):
    slot_count = slot_ids.shape[0]
    slot_order = jnp.arange(slot_count, dtype=jnp.int32)
    same_item = (slot_ids[:, None] == slot_ids[None, :]) & (slot_ids[:, None] >= 0)
    members = jnp.sum(same_item.astype(jnp.int32), axis=1)
    first_slot = jnp.min(jnp.where(same_item, slot_order[None, :], slot_count), axis=1)
    first_slot = jnp.where(members > 0, first_slot, slot_order)
    side_len = jnp.where(members > 1, 2 * SIDE, SIDE)
    within = jnp.arange(SLOT_TOK, dtype=jnp.int32)
    place_in = (slot_order - first_slot)[:, None] * SLOT_TOK + within[None, :]
    return ((place_in // side_len[:, None]).reshape(-1), (place_in % side_len[:, None]).reshape(-1))


def modulated_norm(values, shift_by, scale_by):
    normed = values * lax.rsqrt(jnp.mean(values * values, axis=-1, keepdims=True) + EPSILON)
    return normed * (1.0 + scale_by[:, None, :]) + shift_by[:, None, :]


def full_dot(left, right, dims=(((1,), (0,)), ((), ()))):
    return lax.dot_general(left, right, dims, preferred_element_type=jnp.float32)


def rotate(values, cosine, sine):
    return values * cosine + pltpu.roll(values, BACK_LANE, 1) * sine


def lane_sum(values, on_mxu):
    if on_mxu:
        return full_dot(values.astype(jnp.bfloat16), jnp.ones((PAD, PAD), jnp.bfloat16))
    return jnp.sum(values, axis=-1, keepdims=True)


def head_inverse(lin, on_mxu):
    return lax.rsqrt(lane_sum(lin * lin, on_mxu) * (1.0 / HEAD_DIM) + EPSILON)


def table_parts(table_ref):
    return table_ref[:, :PAD], table_ref[:, PAD:]


def whole(array):
    return pl.BlockSpec(array.shape, lambda i: (0,) * array.ndim)


def pick_rows(first_ref, second_ref):
    return jnp.where(pl.program_id(0) == 0, first_ref[...], second_ref[...])


def slot_rows(cols, first):
    return pl.BlockSpec((SLOT_TOK, cols), lambda i: (i + first, 0))


def call_kernel(body, grid, args, in_specs, out_shape, out_specs, carried, flops, exps=0, first_carried=0, vmem=VMEM_LIMIT):
    carried = [] if carried is None else list(carried)
    count = len(args)
    moved = sum(a.size * a.dtype.itemsize for a in args)

    def wrapped(*refs):
        body(*refs[:count], *refs[count + len(carried) :])

    return pl.pallas_call(
        wrapped,
        grid=grid,
        in_specs=list(in_specs) + [pl.BlockSpec(memory_space=pl.ANY)] * len(carried),
        out_shape=out_shape,
        out_specs=out_specs,
        input_output_aliases={count + i: first_carried + i for i in range(len(carried))},
        compiler_params=pltpu.CompilerParams(vmem_limit_bytes=vmem),
        cost_estimate=pl.CostEstimate(flops=flops, bytes_accessed=moved, transcendentals=exps),
    )(*args, *carried)


def prepare_kernel(
    own_ref, other_ref, mod_ref, wq_ref, wk_ref, wv_ref, table_ref, gain_ref, extra_ref,
    normed_ref, lin_ref, q_ref, k_ref, v_ref,
):
    heads = q_ref.shape[1] // PAD
    span = heads * PAD
    width = own_ref.shape[1]
    for slot, rows_ref in enumerate((own_ref, other_ref)):
        x = rows_ref[...].astype(jnp.float32)
        rms = lax.rsqrt(jnp.mean(x * x, axis=-1, keepdims=True) + EPSILON)
        shift_by = mod_ref[slot, :, :width]
        scale_by = mod_ref[slot, :, width:]
        normed_ref[slot * SLOT_TOK : (slot + 1) * SLOT_TOK, :] = (
            x * rms * (1.0 + scale_by) + shift_by
        ).astype(jnp.bfloat16)
    normed = normed_ref[...]
    in_first = lax.broadcasted_iota(jnp.int32, (2 * SLOT_TOK, PAD), 0) < SLOT_TOK
    cosine, sine = table_parts(table_ref)
    for part, w_ref in enumerate((wq_ref, wk_ref, wv_ref)):
        lin = full_dot(normed, w_ref[...])
        for h in range(heads):
            cols = slice(h * PAD, (h + 1) * PAD)
            piece = lin[:, cols]
            extra = jnp.where(in_first, extra_ref[0, part : part + 1, :], extra_ref[1, part : part + 1, :])
            if part == 2:
                v_ref[:, cols] = (piece + extra).astype(jnp.bfloat16)
                continue
            lin_ref[:, part * span + h * PAD : part * span + (h + 1) * PAD] = piece.astype(jnp.bfloat16)
            gain = gain_ref[part : part + 1, :]
            turned = rotate(piece * head_inverse(piece, True) * gain, cosine, sine)
            out_ref = q_ref if part == 0 else k_ref
            out_ref[:, cols] = (turned + extra).astype(jnp.bfloat16)


def prepare(pair, per_slot, weights, table, gains, extras, part, carried=None):
    rows, width = 2 * SLOT_TOK, pair[0].shape[1]
    span = weights[0].shape[1]
    all_rows = table.shape[0]
    sizes = (width, 2 * span, span, span, span)
    half_rows = lambda cols: pl.BlockSpec((rows, cols), lambda i: (part, 0))
    return call_kernel(
        prepare_kernel,
        (1,),
        [*pair, per_slot, *weights, table, gains, extras],
        [
            *(whole(rows_in) for rows_in in pair),
            pl.BlockSpec((2, 1, 2 * width), lambda i: (part, 0, 0)),
            *(whole(w) for w in weights),
            half_rows(2 * PAD),
            whole(gains),
            pl.BlockSpec((2, 3, PAD), lambda i: (part, 0, 0)),
        ],
        [jax.ShapeDtypeStruct((all_rows, cols), jnp.bfloat16) for cols in sizes],
        [half_rows(cols) for cols in sizes],
        carried,
        6 * rows * width * span,
    )


def split_lanes(values, first_lane, shape):
    lane = lax.broadcasted_iota(jnp.int32, shape, 1)
    high = values.astype(jnp.bfloat16).astype(jnp.float32)
    rest = values - high
    mid = rest.astype(jnp.bfloat16).astype(jnp.float32)
    low = rest - mid
    return jnp.where(
        lane == first_lane,
        high,
        jnp.where(lane == first_lane + 1, mid, jnp.where(lane == first_lane + 2, low, 0.0)),
    )


def attend_kernel(q_ref, key_ref, value_ref, mixed_ref, qlog_ref):
    half = key_ref.shape[0] // 2
    for first in range(0, q_ref.shape[0], SLOT_TOK):
        rows = slice(first, first + SLOT_TOK)
        q = q_ref[rows, :]
        total = None
        for start in (0, half):
            keys = slice(start, start + half)
            weight = jnp.exp2(full_dot(q, key_ref[keys, :], CONTRACT_COLS) * SCORE_LOG2)
            term = full_dot(weight.astype(jnp.bfloat16), value_ref[keys, :])
            total = term if total is None else total + term
        row_sum = total[:, TOTAL_LANE : TOTAL_LANE + 1]
        mixed_ref[rows, :] = (total * (1.0 / row_sum)).astype(jnp.bfloat16)
        log_sum = jnp.log2(row_sum) * (-1.0 / SCORE_LOG2)
        qlog_ref[rows, :] = (q.astype(jnp.float32) + split_lanes(log_sum, LOG_LANE, q.shape)).astype(
            jnp.bfloat16
        )


def attend(q, k, v, part, carried=None):
    all_rows, span = q.shape
    rows = all_rows // 2
    heads = span // PAD
    mine = pl.BlockSpec((rows, PAD), lambda h: (part, h))
    every = pl.BlockSpec((all_rows, PAD), lambda h: (0, h))
    return call_kernel(
        attend_kernel,
        (heads,),
        [q, k, v],
        [mine, every, every],
        [jax.ShapeDtypeStruct(q.shape, jnp.bfloat16)] * 2,
        [mine, mine],
        carried,
        4 * rows * all_rows * span,
        rows * all_rows * heads,
    )


def unturn(grad, lin, gain, cosine, sine, on_mxu):
    turned = rotate(grad, cosine, -sine)
    inverse = head_inverse(lin, on_mxu)
    normed = lin * inverse
    gained = turned * gain
    mean = lane_sum(gained * normed, on_mxu) * (1.0 / HEAD_DIM)
    return inverse * (gained - normed * mean), jnp.sum(turned * normed, axis=0, keepdims=True)


def pull_kernel(
    own_ref, other_ref, mixed_ref, q_ref, key_ref, value_ref, wo_ref, squeeze_ref, gain_ref, table_ref, lin_ref,
    *rest,
):
    *before, ga_ref, dq_ref, wide_ref, gains_ref, dk_ref, dv_ref = rest
    heads = q_ref.shape[1] // PAD
    half = key_ref.shape[0] // 2

    @pl.when(pl.program_id(0) == 0)
    def _():
        if before:
            gains_before, dk_before, dv_before = before
            gains_ref[...] = gains_before[...]
            dk_ref[...] = dk_before[...]
            dv_ref[...] = dv_before[...]
        else:
            gains_ref[...] = jnp.zeros_like(gains_ref)
            dk_ref[...] = jnp.zeros_like(dk_ref)
            dv_ref[...] = jnp.zeros_like(dv_ref)

    cosine, sine = table_parts(table_ref)
    grad_attn = pick_rows(own_ref, other_ref)
    ga_ref[...] = grad_attn
    grad_mixed = full_dot(grad_attn, wo_ref[...], CONTRACT_COLS).astype(jnp.bfloat16)
    gain_sum = jnp.zeros((1, PAD), jnp.float32)
    for h in range(heads):
        cols = slice(h * PAD, (h + 1) * PAD)
        grad_low = grad_mixed[:, cols]
        grad_head = grad_low.astype(jnp.float32)
        mixed = mixed_ref[:, cols].astype(jnp.float32)
        row_dot = jnp.sum(grad_head * mixed, axis=-1, keepdims=True)
        grad_aug = (grad_head + split_lanes(-row_dot, DOT_LANE, grad_head.shape)).astype(jnp.bfloat16)
        q = q_ref[:, cols]
        dq = None
        for start in (0, half):
            key_rows = slice(start, start + half)
            key, value = key_ref[key_rows, cols], value_ref[key_rows, cols]
            probs = jnp.exp2(full_dot(key, q, CONTRACT_COLS) * SCORE_LOG2)
            grad_probs = full_dot(value, grad_aug, CONTRACT_COLS)
            grad_scores = (probs * grad_probs).astype(jnp.bfloat16)
            dv_ref[key_rows, cols] += full_dot(probs.astype(jnp.bfloat16), grad_low)
            dk_ref[key_rows, cols] += full_dot(grad_scores, q)
            term = full_dot(grad_scores, key, CONTRACT_ROWS)
            dq = term if dq is None else dq + term
        lin = lin_ref[:, cols].astype(jnp.float32)
        grad_lin, gain_term = unturn(dq * INV_ROOT, lin, gain_ref[0:1, :], cosine, sine, False)
        gain_sum = gain_sum + gain_term
        wide_ref[:, cols] = grad_lin.astype(jnp.bfloat16)
    gains_ref[0:1, :] += gain_sum
    dq_ref[...] = full_dot(wide_ref[...], squeeze_ref[...]).astype(jnp.bfloat16)


def pull(pair, mixed, qlog, k, v, w_out, squeeze, gains, table, lin, first, carried=None, earlier=None):
    rows, width = 2 * SLOT_TOK, pair[0].shape[1]
    all_rows, span = qlog.shape
    compact = squeeze.shape[1]
    args = [*pair, mixed, qlog, k, v, w_out, squeeze, gains, table, lin]
    specs = [*(whole(a) for a in pair), slot_rows(span, first), slot_rows(span, first)]
    specs += [whole(a) for a in (k, v, w_out, squeeze, gains)]
    specs += [slot_rows(2 * PAD, first), slot_rows(span, first)]
    sums = [jax.ShapeDtypeStruct(shape, jnp.float32) for shape in ((8, PAD), (all_rows, span), (all_rows, span))]
    if earlier is not None:
        args += earlier
        specs += [whole(a) for a in earlier]
    kept = [jax.ShapeDtypeStruct((all_rows, cols), jnp.bfloat16) for cols in (width, compact, span)]
    return call_kernel(
        pull_kernel,
        (rows // SLOT_TOK,),
        args,
        specs,
        kept + sums,
        [slot_rows(a.shape[1], first) for a in kept] + [whole(a) for a in sums],
        carried,
        10 * rows * all_rows * span,
        rows * all_rows * span // PAD,
    )


def finish_kernel(
    dq_ref, dk_ref, dv_ref, lin_ref, squeeze_ref, gain_ref, table_ref, wq_ref, wk_ref, wv_ref,
    part_ref, gains_ref, kc_ref, vc_ref,
):
    @pl.when(pl.program_id(0) == 0)
    def _():
        gains_ref[...] = jnp.zeros_like(gains_ref)

    cosine, sine = table_parts(table_ref)
    gain_sum = jnp.zeros((1, PAD), jnp.float32)
    k_grads = []
    for h in range(dk_ref.shape[1] // PAD):
        cols = slice(h * PAD, (h + 1) * PAD)
        grad_lin, gain_term = unturn(
            dk_ref[:, cols] * INV_ROOT, lin_ref[:, cols].astype(jnp.float32), gain_ref[1:2, :], cosine, sine, True
        )
        gain_sum = gain_sum + gain_term
        k_grads.append(grad_lin.astype(jnp.bfloat16))
    gains_ref[0:1, :] += gain_sum
    k_wide = jnp.concatenate(k_grads, axis=1)
    v_wide = dv_ref[...].astype(jnp.bfloat16)
    kc_ref[...] = full_dot(k_wide, squeeze_ref[...]).astype(jnp.bfloat16)
    vc_ref[...] = full_dot(v_wide, squeeze_ref[...]).astype(jnp.bfloat16)
    part_ref[...] = (
        full_dot(dq_ref[...], wq_ref[...], CONTRACT_COLS)
        + full_dot(k_wide, wk_ref[...], CONTRACT_COLS)
        + full_dot(v_wide, wv_ref[...], CONTRACT_COLS)
    ).astype(jnp.bfloat16)


def finish(dq, dk, dv, lin, squeeze, gains, table, weights, first, carried=None):
    all_rows, span = dk.shape
    rows = all_rows // 2
    width, compact = weights[0].shape[0], squeeze.shape[1]
    kept = [jax.ShapeDtypeStruct((all_rows, compact), jnp.bfloat16)] * 2
    fresh = [jax.ShapeDtypeStruct((rows, width), jnp.bfloat16), jax.ShapeDtypeStruct((8, PAD), jnp.float32)]
    return call_kernel(
        finish_kernel,
        (rows // SLOT_TOK,),
        [dq, dk, dv, lin, squeeze, gains, table, *weights],
        [
            slot_rows(span, first),
            slot_rows(span, first),
            slot_rows(span, first),
            pl.BlockSpec((SLOT_TOK, span), lambda i: (i + first, 1)),
            whole(squeeze),
            whole(gains),
            slot_rows(2 * PAD, first),
            *(whole(w) for w in weights),
        ],
        fresh + kept,
        [slot_rows(width, 0), whole(fresh[1])] + [slot_rows(compact, first)] * 2,
        carried,
        6 * rows * span * width,
        first_carried=2,
    )


def mlp_kernel(own_ref, other_ref, gh_ref, wg_ref, wu_ref, part_ref, rows_ref, hidden_ref, grad_ref):
    rows = pick_rows(own_ref, other_ref)
    rows_ref[...] = rows
    gate_lin = full_dot(rows, wg_ref[...])
    up_lin = full_dot(rows, wu_ref[...])
    grad_hidden = gh_ref[...]
    sigmoid = 1.0 / (1.0 + jnp.exp(-gate_lin))
    silu = gate_lin * sigmoid
    hidden_ref[...] = (silu * up_lin).astype(jnp.bfloat16)
    grad_up = (grad_hidden * silu).astype(jnp.bfloat16)
    grad_gate = (grad_hidden * up_lin * (sigmoid + silu * (1.0 - sigmoid))).astype(jnp.bfloat16)
    units = wg_ref.shape[1]
    grad_ref[:, :units] = grad_gate
    grad_ref[:, units:] = grad_up
    part_ref[...] = (
        full_dot(grad_gate, wg_ref[...], CONTRACT_COLS) + full_dot(grad_up, wu_ref[...], CONTRACT_COLS)
    ).astype(jnp.bfloat16)


def mlp(pair, grad_hidden, w_gate, w_up, first, carried=None):
    rows, width = 2 * SLOT_TOK, pair[0].shape[1]
    all_rows, units = grad_hidden.shape
    kept = [jax.ShapeDtypeStruct((all_rows, cols), jnp.bfloat16) for cols in (width, units, 2 * units)]
    return call_kernel(
        mlp_kernel,
        (rows // SLOT_TOK,),
        [*pair, grad_hidden, w_gate, w_up],
        [*(whole(a) for a in pair), slot_rows(units, first), whole(w_gate), whole(w_up)],
        [jax.ShapeDtypeStruct((rows, width), jnp.bfloat16), *kept],
        [slot_rows(width, 0)] + [slot_rows(a.shape[1], first) for a in kept],
        carried,
        8 * rows * width * units,
        rows * units,
        first_carried=1,
        vmem=2 * VMEM_LIMIT,
    )


PLAN = {
    "down": ("down",),
    "terms": ("early",),
    "near": ("down",),
    "middle": ("early", "late"),
    "pulled": ("down", "early", "late"),
    "pulled_far": ("down", "early", "late"),
    "finished_far": ("down", "early", "late"),
    "query": ("query",),
    "key": ("early", "key", "late"),
    "tail": (
        "query", "key", "late", "early", "query", "key", "query", "key", "late", "query", "items", "key", "items", "query",
        "down", "key", "items", "items", "query", "key", "down",
    ),
}


def swap(values, axis_name, bit):
    count = lax.axis_size(axis_name)
    return lax.ppermute(values, axis_name, [(i, i ^ bit) for i in range(count)])


def after(values, *earlier):
    return lax.optimization_barrier((values, *earlier))[0]


def bits_of(axis_name):
    count = lax.axis_size(axis_name)
    bits = []
    bit = 1
    while bit < count:
        bits.append(bit)
        bit *= 2
    assert bit == count
    return bits


def halving_steps(first, second, bits, earlier):
    place = lax.axis_index("dp")
    upper = (place // bits[0]) % 2 == 1
    first = after(first, *earlier)
    send = jnp.where(upper, first, second)
    got = swap(send, "dp", bits[0])
    earlier = yield send
    low = after(jnp.where(upper, second, first), *earlier)
    low = (low.astype(jnp.float32) + got.astype(jnp.float32)).astype(jnp.bfloat16)
    for bit in bits[1:]:
        half = low.shape[0] // 2
        part = (place // bit) % 2
        send = lax.dynamic_slice_in_dim(low, (1 - part) * half, half, 0)
        got = swap(send, "dp", bit)
        earlier = yield send
        mine = lax.dynamic_slice_in_dim(after(low, *earlier), part * half, half, 0)
        low = (mine.astype(jnp.float32) + got.astype(jnp.float32)).astype(jnp.bfloat16)
    for bit in reversed(bits[1:]):
        got = swap(low, "dp", bit)
        earlier = yield low
        low = after(low, *earlier)
        low = jnp.where(
            (place // bit) % 2 == 1, jnp.concatenate([got, low], axis=0), jnp.concatenate([low, got], axis=0)
        )
    got = swap(low, "dp", bits[0])
    earlier = yield low
    low = after(low, *earlier)
    yield jnp.where(upper, got, low), jnp.where(upper, low, got)


def gather_steps(values, earlier):
    values = after(values, *earlier)
    for bit in reversed(bits_of("dp")):
        got = swap(values, "dp", bit)
        earlier = yield values
        values = jnp.concatenate([after(values, *earlier), got], axis=0)
    yield (values,)


def tree_steps(first, second, earlier):
    place = lax.axis_index("dp")
    if lax.axis_size("dp") != 8:
        yield from halving_steps(first, second, bits_of("dp"), earlier)
        return
    upper = place % 2 == 1
    is_end = (place // 2 == 0) | (place // 2 == 3)

    def along(values, pairs):
        return lax.ppermute(values, "dp", [(2 * a + y, 2 * b + y) for a, b in pairs for y in range(2)])

    def plus(values, got):
        return (values.astype(jnp.float32) + got.astype(jnp.float32)).astype(jnp.bfloat16)

    first = after(first, *earlier)
    send = jnp.where(upper, first, second)
    got = swap(send, "dp", 1)
    earlier = yield send
    low = plus(after(jnp.where(upper, second, first), *earlier), got)
    got = along(low, [(0, 1), (3, 2)])
    earlier = yield low
    low = plus(after(low, *earlier), got)
    got = along(low, [(1, 2), (2, 1)])
    earlier = yield low
    low = plus(after(low, *earlier), got)
    got = along(low, [(1, 0), (2, 3)])
    earlier = yield low
    low = jnp.where(is_end, got, after(low, *earlier))
    got = swap(low, "dp", 1)
    earlier = yield low
    low = after(low, *earlier)
    yield jnp.where(upper, got, low), jnp.where(upper, low, got)


class DpSums:
    def __init__(self):
        self.steps = {}
        self.newest = {}

    def offer(self, name, steps):
        self.steps[name] = steps
        self.newest[name] = None

    def step(self, name, *earlier):
        if self.newest[name] is None:
            self.steps[name] = self.steps[name](earlier)
            self.newest[name] = next(self.steps[name])
        elif not isinstance(self.newest[name], tuple):
            self.newest[name] = self.steps[name].send(earlier)
        newest = self.newest[name]
        return newest[0] if isinstance(newest, tuple) else newest

    def at(self, point, tick):
        for name in PLAN[point]:
            tick = self.step(name, tick)
        return tick

    def finish(self, tick):
        tick = self.at("tail", tick)
        while not all(isinstance(newest, tuple) for newest in self.newest.values()):
            for name in self.newest:
                tick = self.step(name, tick)
        return self.newest


def rows_dot(source, weight):
    return jnp.dot(source, weight, preferred_element_type=jnp.float32)


def dot_cols(source, weight):
    return lax.dot_general(source, weight, CONTRACT_COLS, preferred_element_type=jnp.float32)


def dot_rows(left, right):
    return lax.dot_general(
        left, right, CONTRACT_ROWS, preferred_element_type=jnp.float32
    ).astype(jnp.bfloat16)


def pair_sum(part):
    low = part.astype(jnp.bfloat16)
    got = swap(low[SLOT_TOK:], "tensor", 1)
    return low[:SLOT_TOK].astype(jnp.float32) + got.astype(jnp.float32)


def lane_of(dims):
    quarter = HEAD_DIM // 4
    pair, rest = dims // (2 * quarter), dims % (2 * quarter)
    return pair * quarter + jnp.where(rest < quarter, rest, BACK_LANE + rest - quarter)


def head_order(values):
    quarter = HEAD_DIM // 4
    return jnp.concatenate(
        [values[:, first : first + quarter] for first in (0, BACK_LANE, quarter, BACK_LANE + quarter)], axis=1
    )


def rope_table(grid_row, grid_col):
    quarter = HEAD_DIM // 4
    lane = jnp.arange(2 * PAD, dtype=jnp.int32)
    dim = lane % BACK_LANE
    rates = jnp.exp(-math.log(10000.0) * (dim % quarter).astype(jnp.float32) / quarter)
    places = jnp.arange(2 * SIDE, dtype=jnp.int32)
    angles = places.astype(jnp.float32)[:, None] * rates[None]
    sine_v = jnp.where((lane % PAD < BACK_LANE)[None], -jnp.sin(angles), jnp.sin(angles))
    values = jnp.where((lane < PAD)[None], jnp.cos(angles), sine_v)
    by_row = jnp.where((dim < quarter)[None], values, 0.0)
    by_col = jnp.where(((dim >= quarter) & (dim < 2 * quarter))[None], values, 0.0)
    hot = jnp.concatenate([grid[:, None] == places[None] for grid in (grid_row, grid_col)], axis=1)
    return jnp.dot(
        hot.astype(jnp.float32), jnp.concatenate([by_row, by_col], axis=0), precision=lax.Precision.HIGHEST
    )


def lane_extras(slot_ids, item_count):
    lane = jnp.arange(PAD, dtype=jnp.int32)
    hot = (lane - ITEM_LANE)[None] == (slot_ids + 1)[:, None]
    item_lane = ((lane >= ITEM_LANE) & (lane <= ITEM_LANE + item_count))[None]
    log_lane = ((lane >= LOG_LANE) & (lane < LOG_LANE + 3))[None]
    for_key = jnp.where(item_lane & ~hot, -FAR_ITEM, 0.0) + jnp.where(log_lane, 1.0, 0.0)
    for_value = jnp.broadcast_to(((lane >= TOTAL_LANE) & (lane < DOT_LANE + 3))[None], hot.shape)
    return jnp.stack([hot.astype(jnp.float32), for_key, for_value.astype(jnp.float32)], axis=1)


def local(
    tokens,
    w_query,
    w_key,
    w_value,
    w_out,
    w_gate,
    w_up,
    w_down,
    w_mod,
    b_mod,
    class_table,
    q_gain,
    k_gain,
    slot_item,
    labels,
    tsteps,
    cotangent,
):
    tensor_count = lax.axis_size("tensor")
    tensor_place = lax.axis_index("tensor")
    slot_count = slot_item.shape[1]
    item_count = labels.shape[1]
    assert tensor_count == 4 and slot_count == 4 and item_count < LOG_LANE - ITEM_LANE
    width = tokens.shape[1]
    head_cols = w_query.shape[1]
    heads = head_cols // HEAD_DIM
    bias_len = b_mod.shape[0]
    slot_ids = slot_item[0]
    half = 2 * SLOT_TOK

    far_tokens = swap(tokens, "tensor", 2)
    near_tokens = swap(tokens, "tensor", 1)

    slots = jnp.arange(slot_count, dtype=jnp.int32)
    rel_hot = (tensor_place ^ slots)[:, None] == slots[None, :]
    rel_int = rel_hot.astype(jnp.int32)
    item_ids = jnp.arange(item_count, dtype=jnp.int32)
    class_ids = jnp.arange(class_table.shape[0], dtype=jnp.int32)

    def condition(label_ids, step_ids):
        label_hot = (label_ids[:, None] == class_ids[None, :]).astype(jnp.float32)
        embedded = rows_dot(label_hot.astype(jnp.bfloat16), class_table)
        cond_pre = embedded + sinusoid(step_ids, tensor_place * head_cols, head_cols)
        return label_hot, cond_pre

    _, cond_own = condition(labels[0], tsteps[0])
    bias_full = lax.dynamic_update_slice_in_dim(
        jnp.zeros((6 * width,), jnp.float32), b_mod, tensor_place * bias_len, 0
    )
    modul = rows_dot(jax.nn.silu(cond_own).astype(jnp.bfloat16), w_mod) + bias_full[None, :]
    modul = modul + swap(modul, "tensor", 1)
    modul_pair = modul
    modul = modul + swap(modul, "tensor", 2)
    pad_row = jnp.arange(heads * PAD, dtype=jnp.int32)[:, None]
    flat_col = jnp.arange(head_cols, dtype=jnp.int32)[None, :]
    squeeze = (
        (pad_row // PAD == flat_col // HEAD_DIM) & (pad_row % PAD == lane_of(flat_col % HEAD_DIM))
    ).astype(jnp.bfloat16)
    w_wide = [dot_cols(after(w, modul_pair), squeeze).astype(jnp.bfloat16) for w in (w_query, w_key, w_value)]
    w_out_wide = rows_dot(squeeze, after(w_out, modul_pair)).astype(jnp.bfloat16)
    rel_ids = jnp.sum(rel_int * slot_ids[None, :], axis=1)
    rel_pick = (rel_ids[:, None] == item_ids[None, :]).astype(jnp.float32)
    grid_row, grid_col = grid_positions(slot_ids)

    def rel_tokens(per_token):
        return jnp.sum(rel_int[:, :, None] * per_token.reshape(1, slot_count, SLOT_TOK), axis=1).reshape(-1)

    table = rope_table(*(after(rel_tokens(g), modul_pair) for g in (grid_row, grid_col)))
    extras = lane_extras(rel_ids, item_count)
    gain_lane = lane_of(jnp.arange(HEAD_DIM, dtype=jnp.int32))[:, None] == jnp.arange(PAD)[None, :]
    gains = jnp.dot(
        jnp.stack([q_gain, k_gain]), gain_lane.astype(jnp.float32), precision=lax.Precision.HIGHEST
    )

    per_slot = jnp.dot(rel_pick, modul, precision=lax.Precision.HIGHEST)
    shift_a, scale_a, gate_a, shift_m, scale_m, gate_m = jnp.split(per_slot[:1], 6, axis=1)
    cot_now = after(cotangent, modul)
    far_cot = swap(cot_now, "tensor", 2)
    near_cot = swap(cot_now, "tensor", 1)

    slot_mods = per_slot[:, None, :]
    near_set = prepare((tokens, near_tokens), slot_mods, w_wide, table, gains, extras, 0)
    far_tokens = after(far_tokens, near_set[2])
    attn_all, lin, q, k, v = prepare(
        (far_tokens, swap(far_tokens, "tensor", 1)), slot_mods, w_wide, table, gains, extras, 1, near_set
    )
    far_mixed, far_qlog = attend(q, k, v, 1)
    far_sum = pair_sum(rows_dot(far_mixed[half:], w_out_wide)).astype(jnp.bfloat16)
    far_got = swap(far_sum, "tensor", 2)
    far_cot = after(far_cot, far_mixed)
    cot_all = jnp.concatenate([cotangent, near_cot, far_cot, swap(far_cot, "tensor", 1)], axis=0)
    mixed, qlog = attend(after(q, far_sum), k, v, 0, (far_mixed, far_qlog))
    near_sum = pair_sum(rows_dot(mixed[:half], w_out_wide))
    branch_grad = (
        (per_slot[:, None, 5 * width :] * after(cot_all, mixed).astype(jnp.float32).reshape(4, SLOT_TOK, width))
        .astype(jnp.bfloat16)
        .reshape(2 * half, width)
    )
    grad_hidden = dot_cols(branch_grad, w_down)
    mixed_low = rows_dot(mixed, squeeze).astype(jnp.bfloat16)
    attn = near_sum + after(far_got, grad_hidden, mixed_low).astype(jnp.float32)

    resid = tokens.astype(jnp.float32)
    middle = resid + gate_a * attn

    def norm_rows(values, shift_by, scale_by):
        return modulated_norm(values[None], shift_by, scale_by)[0]

    normed_two, norm_two_back = jax.vjp(norm_rows, middle, shift_m, scale_m)
    normed_mlp = normed_two.astype(jnp.bfloat16)
    far_normed = swap(normed_mlp, "tensor", 2)
    near_part, *near_mlp = mlp((normed_mlp, swap(normed_mlp, "tensor", 1)), grad_hidden, w_gate, w_up, 0)
    far_normed = after(far_normed, near_part)
    far_part, mlp_all, hidden, gate_up_grad = mlp(
        (far_normed, swap(far_normed, "tensor", 1)), grad_hidden, w_gate, w_up, 2, near_mlp
    )
    sums = DpSums()
    bits = bits_of("dp")
    late_first = bits[1:] + bits[:1]
    half_width = width // 2
    down_term = dot_rows(hidden, branch_grad)
    half_units = down_term.shape[0] // 2
    sums.offer("down", functools.partial(halving_steps, down_term[:half_units], down_term[half_units:], late_first))
    far_sum = pair_sum(far_part).astype(jnp.bfloat16)
    far_got = swap(far_sum, "tensor", 2)
    tick = sums.at("down", far_sum)
    units = w_gate.shape[1]
    gate_term = dot_rows(after(mlp_all, tick), gate_up_grad[:, :units])
    up_term = dot_rows(after(mlp_all, gate_term), gate_up_grad[:, units:])
    half_width = width // 2
    sums.offer("early", functools.partial(halving_steps, gate_term[:half_width], up_term[:half_width], bits))
    sums.offer("late", functools.partial(halving_steps, gate_term[half_width:], up_term[half_width:], bits))
    tick = sums.at("terms", up_term)
    near_sum = pair_sum(after(near_part, tick))
    tick = sums.at("near", near_sum)
    grad_normed_mlp = near_sum + after(far_got, tick).astype(jnp.float32)

    grad_out = cotangent.astype(jnp.float32)
    grad_mid_norm, grad_shift_m, grad_scale_m = norm_two_back(grad_normed_mlp)
    grad_middle = grad_out + grad_mid_norm
    grad_gate_a = jnp.sum(attn * grad_middle, axis=0, keepdims=True)
    grad_attn = (gate_a * grad_middle).astype(jnp.bfloat16)
    far_ga = swap(grad_attn, "tensor", 2)
    near_ga = swap(grad_attn, "tensor", 1)
    tick = sums.at("middle", grad_attn)
    near_pull = pull(
        (grad_attn, after(near_ga, tick)), mixed, qlog, k, v, w_out_wide, squeeze, gains, table, lin, 0
    )
    far_ga = after(far_ga, near_pull[0])
    diag_ga = swap(far_ga, "tensor", 1)
    tick = sums.at("pulled", near_pull[0])
    ga_all, q_low, q_wide, gain_q, sum_k, sum_v = pull(
        (far_ga, after(diag_ga, tick)), mixed, qlog, k, v, w_out_wide, squeeze, gains, table, lin,
        2, near_pull[:3], near_pull[3:],
    )
    tick = sums.at("pulled_far", q_low)
    far_part, gain_far, *far_low = finish(
        after(q_wide, tick), sum_k, sum_v, lin, squeeze, gains, table, w_wide, 2
    )
    far_sum = pair_sum(far_part).astype(jnp.bfloat16)
    far_got = swap(far_sum, "tensor", 2)
    branch_far = pair_sum(rows_dot(after(hidden, far_sum)[half:], w_down)).astype(jnp.bfloat16)
    branch_near = pair_sum(rows_dot(after(hidden, branch_far)[:half], w_down))
    tick = sums.at("finished_far", branch_near)
    near_part, gain_near, k_low, v_low = finish(
        after(q_wide, tick), sum_k, sum_v, lin, squeeze, gains, table, w_wide, 0, far_low
    )
    query_term = dot_rows(after(attn_all, near_part), q_low)
    value_term = dot_rows(after(attn_all, query_term), v_low)
    sums.offer("query", functools.partial(halving_steps, query_term, value_term, bits))
    tick = sums.at("query", value_term)
    key_term = dot_rows(after(k_low, tick), attn_all)
    out_term = dot_rows(mixed_low, after(ga_all, key_term))
    sums.offer("key", functools.partial(halving_steps, key_term, out_term, bits))
    tick = sums.at("key", out_term)
    near_sum = pair_sum(after(near_part, tick))
    grad_normed_attn = near_sum + after(far_got, tick).astype(jnp.float32)
    gain_grads = head_order(jnp.concatenate([gain_q[:1], gain_far[:1] + gain_near[:1]], axis=0))

    branch_got = swap(after(branch_far, out_term), "tensor", 2)
    branch = branch_near + branch_got.astype(jnp.float32)
    output = (middle + gate_m * branch).astype(jnp.bfloat16)
    grad_gate_m = jnp.sum(branch * grad_out, axis=0, keepdims=True)

    _, norm_one_back = jax.vjp(norm_rows, resid, shift_a, scale_a)
    grad_resid_norm, grad_shift_a, grad_scale_a = norm_one_back(grad_normed_attn)
    grad_tokens = (grad_middle + grad_resid_norm).astype(jnp.bfloat16)

    grad_slot = jnp.concatenate(
        [
            grad_shift_a,
            grad_scale_a,
            grad_gate_a,
            grad_shift_m,
            grad_scale_m,
            grad_gate_m,
            gain_grads[:1],
            gain_grads[1:],
        ],
        axis=1,
    )
    pair_slots = jnp.concatenate([grad_slot, swap(grad_slot, "tensor", 2)], axis=0)
    grad_slots = jnp.concatenate([pair_slots, swap(pair_slots, "tensor", 1)], axis=0)
    mod_width = 6 * width
    pick_order = jnp.stack([rel_pick[0], rel_pick[2], rel_pick[1], rel_pick[3]])
    grad_items = lax.dot_general(
        pick_order,
        grad_slots[:, :mod_width],
        CONTRACT_ROWS,
        precision=lax.Precision.HIGHEST,
        preferred_element_type=jnp.float32,
    ).astype(jnp.bfloat16)
    gain_sum = jnp.sum(grad_slots[:, mod_width:], axis=0, keepdims=True)
    gain_rows = jnp.pad(gain_sum, ((0, item_count - 1), (0, 0)))
    ids = jnp.stack([labels[0] // 32, labels[0] % 32, tsteps[0] // 32, tsteps[0] % 32], axis=1)
    item_rows = jnp.concatenate([gain_rows, ids.astype(jnp.float32)], axis=1).astype(jnp.bfloat16)
    sums.offer("items", functools.partial(gather_steps, jnp.concatenate([grad_items, item_rows], axis=1)))
    grad_w = sums.finish(near_part)
    items_all = grad_w["items"][0]
    grad_modul_low = items_all[:, :mod_width]
    gains_end = mod_width + 2 * HEAD_DIM
    gain_total = jnp.sum(items_all[:, mod_width:gains_end].astype(jnp.float32), axis=0)
    grad_q_gain = gain_total[:HEAD_DIM]
    grad_k_gain = gain_total[HEAD_DIM:]
    ids = items_all[:, gains_end:].astype(jnp.int32)
    label_hot, cond_pre = condition(ids[:, 0] * 32 + ids[:, 1], ids[:, 2] * 32 + ids[:, 3])
    cond_full, silu_back = jax.vjp(jax.nn.silu, cond_pre)
    grad_w_mod = lax.dot_general(
        cond_full.astype(jnp.bfloat16), grad_modul_low, CONTRACT_ROWS, preferred_element_type=jnp.float32
    )
    grad_bias_full = jnp.sum(grad_modul_low.astype(jnp.float32), axis=0)
    grad_b_mod = lax.dynamic_slice_in_dim(grad_bias_full, tensor_place * bias_len, bias_len, 0)
    grad_cond_pre = silu_back(dot_cols(grad_modul_low, w_mod))[0]
    grad_class_table = lax.dot_general(
        label_hot,
        grad_cond_pre,
        CONTRACT_ROWS,
        precision=lax.Precision.HIGHEST,
        preferred_element_type=jnp.float32,
    )
    wide_rows = lambda parts: jnp.concatenate(parts, axis=0).astype(jnp.float32)
    return (
        output,
        grad_tokens,
        grad_w["query"][0].astype(jnp.float32),
        grad_w["key"][0].T.astype(jnp.float32),
        grad_w["query"][1].astype(jnp.float32),
        grad_w["key"][1].astype(jnp.float32),
        wide_rows([grad_w["early"][0], grad_w["late"][0]]),
        wide_rows([grad_w["early"][1], grad_w["late"][1]]),
        wide_rows(grad_w["down"]),
        grad_w_mod,
        grad_b_mod,
        grad_class_table,
        grad_q_gain,
        grad_k_gain,
    )


def solution(mesh):
    in_specs = (
        P(("dp", "tensor"), None),
        P(None, "tensor"),
        P(None, "tensor"),
        P(None, "tensor"),
        P("tensor", None),
        P(None, "tensor"),
        P(None, "tensor"),
        P("tensor", None),
        P("tensor", None),
        P("tensor"),
        P(None, "tensor"),
        P(),
        P(),
        P("dp", None),
        P("dp", None),
        P("dp", None),
        P(("dp", "tensor"), None),
    )
    out_specs = (
        P(("dp", "tensor"), None),
        P(("dp", "tensor"), None),
        P(None, "tensor"),
        P(None, "tensor"),
        P(None, "tensor"),
        P("tensor", None),
        P(None, "tensor"),
        P(None, "tensor"),
        P("tensor", None),
        P("tensor", None),
        P("tensor"),
        P(None, "tensor"),
        P(),
        P(),
    )
    return jax.shard_map(local, mesh=mesh, in_specs=in_specs, out_specs=out_specs, check_vma=False)
```

```python
import functools
import math

import jax
import jax.numpy as jnp
from jax import lax
from jax.experimental import pallas as pl
from jax.experimental.pallas import tpu as pltpu
from jax.sharding import PartitionSpec as P

D = 1152
HEAD_DIM = 72
PAD = 128
SIDE = 16
SLOT_TOK = 256
EPSILON = 1e-06
SCORE_LOG2 = math.log2(math.e) / math.sqrt(HEAD_DIM)
INV_ROOT = 1.0 / math.sqrt(HEAD_DIM)
BACK_LANE = PAD // 2
TOTAL_LANE = HEAD_DIM // 2
DOT_LANE = TOTAL_LANE + 1
ITEM_LANE = TOTAL_LANE + 4
LOG_LANE = ITEM_LANE + 8
FAR_ITEM = 16384.0
CONTRACT_ROWS = (((0,), (0,)), ((), ()))
CONTRACT_COLS = (((1,), (1,)), ((), ()))
VMEM_LIMIT = 28 * 1024 * 1024


def sinusoid(step_ids, first_col, col_count):
    half_width = D // 2
    feature = first_col + jnp.arange(col_count, dtype=jnp.int32)
    freq_index = (feature % half_width).astype(jnp.float32)
    rates = jnp.exp(-math.log(10000.0) * freq_index / half_width)
    angles = step_ids.astype(jnp.float32)[:, None] * rates[None, :]
    return jnp.where(feature[None, :] < half_width, jnp.cos(angles), jnp.sin(angles))


def grid_positions(slot_ids):
    slot_count = slot_ids.shape[0]
    slot_order = jnp.arange(slot_count, dtype=jnp.int32)
    same_item = (slot_ids[:, None] == slot_ids[None, :]) & (slot_ids[:, None] >= 0)
    members = jnp.sum(same_item.astype(jnp.int32), axis=1)
    first_slot = jnp.min(jnp.where(same_item, slot_order[None, :], slot_count), axis=1)
    first_slot = jnp.where(members > 0, first_slot, slot_order)
    side_len = jnp.where(members > 1, 2 * SIDE, SIDE)
    within = jnp.arange(SLOT_TOK, dtype=jnp.int32)
    place_in = (slot_order - first_slot)[:, None] * SLOT_TOK + within[None, :]
    return ((place_in // side_len[:, None]).reshape(-1), (place_in % side_len[:, None]).reshape(-1))


def modulated_norm(values, shift_by, scale_by):
    normed = values * lax.rsqrt(jnp.mean(values * values, axis=-1, keepdims=True) + EPSILON)
    return normed * (1.0 + scale_by[:, None, :]) + shift_by[:, None, :]


def full_dot(left, right, dims=(((1,), (0,)), ((), ()))):
    return lax.dot_general(left, right, dims, preferred_element_type=jnp.float32)


def rotate(values, cosine, sine):
    return values * cosine + pltpu.roll(values, BACK_LANE, 1) * sine


def lane_sum(values, on_mxu):
    if on_mxu:
        return full_dot(values.astype(jnp.bfloat16), jnp.ones((PAD, PAD), jnp.bfloat16))
    return jnp.sum(values, axis=-1, keepdims=True)


def head_inverse(lin, on_mxu):
    return lax.rsqrt(lane_sum(lin * lin, on_mxu) * (1.0 / HEAD_DIM) + EPSILON)


def table_parts(table_ref):
    return table_ref[:, :PAD], table_ref[:, PAD:]


def whole(array):
    return pl.BlockSpec(array.shape, lambda i: (0,) * array.ndim)


def pick_rows(first_ref, second_ref):
    return jnp.where(pl.program_id(0) == 0, first_ref[...], second_ref[...])


def slot_rows(cols, first):
    return pl.BlockSpec((SLOT_TOK, cols), lambda i: (i + first, 0))


def call_kernel(body, grid, args, in_specs, out_shape, out_specs, carried, flops, exps=0, first_carried=0, vmem=VMEM_LIMIT):
    carried = [] if carried is None else list(carried)
    count = len(args)
    moved = sum(a.size * a.dtype.itemsize for a in args)

    def wrapped(*refs):
        body(*refs[:count], *refs[count + len(carried) :])

    return pl.pallas_call(
        wrapped,
        grid=grid,
        in_specs=list(in_specs) + [pl.BlockSpec(memory_space=pl.ANY)] * len(carried),
        out_shape=out_shape,
        out_specs=out_specs,
        input_output_aliases={count + i: first_carried + i for i in range(len(carried))},
        compiler_params=pltpu.CompilerParams(vmem_limit_bytes=vmem),
        cost_estimate=pl.CostEstimate(flops=flops, bytes_accessed=moved, transcendentals=exps),
    )(*args, *carried)


def prepare_kernel(
    own_ref, other_ref, mod_ref, wq_ref, wk_ref, wv_ref, table_ref, gain_ref, extra_ref,
    normed_ref, lin_ref, q_ref, k_ref, v_ref,
):
    heads = q_ref.shape[1] // PAD
    span = heads * PAD
    width = own_ref.shape[1]
    for slot, rows_ref in enumerate((own_ref, other_ref)):
        x = rows_ref[...].astype(jnp.float32)
        rms = lax.rsqrt(jnp.mean(x * x, axis=-1, keepdims=True) + EPSILON)
        shift_by = mod_ref[slot, :, :width]
        scale_by = mod_ref[slot, :, width:]
        normed_ref[slot * SLOT_TOK : (slot + 1) * SLOT_TOK, :] = (
            x * rms * (1.0 + scale_by) + shift_by
        ).astype(jnp.bfloat16)
    normed = normed_ref[...]
    in_first = lax.broadcasted_iota(jnp.int32, (2 * SLOT_TOK, PAD), 0) < SLOT_TOK
    cosine, sine = table_parts(table_ref)
    for part, w_ref in enumerate((wq_ref, wk_ref, wv_ref)):
        lin = full_dot(normed, w_ref[...])
        for h in range(heads):
            cols = slice(h * PAD, (h + 1) * PAD)
            piece = lin[:, cols]
            extra = jnp.where(in_first, extra_ref[0, part : part + 1, :], extra_ref[1, part : part + 1, :])
            if part == 2:
                v_ref[:, cols] = (piece + extra).astype(jnp.bfloat16)
                continue
            lin_ref[:, part * span + h * PAD : part * span + (h + 1) * PAD] = piece.astype(jnp.bfloat16)
            gain = gain_ref[part : part + 1, :]
            turned = rotate(piece * head_inverse(piece, True) * gain, cosine, sine)
            out_ref = q_ref if part == 0 else k_ref
            out_ref[:, cols] = (turned + extra).astype(jnp.bfloat16)


def prepare(pair, per_slot, weights, table, gains, extras, part, carried=None):
    rows, width = 2 * SLOT_TOK, pair[0].shape[1]
    span = weights[0].shape[1]
    all_rows = table.shape[0]
    sizes = (width, 2 * span, span, span, span)
    half_rows = lambda cols: pl.BlockSpec((rows, cols), lambda i: (part, 0))
    return call_kernel(
        prepare_kernel,
        (1,),
        [*pair, per_slot, *weights, table, gains, extras],
        [
            *(whole(rows_in) for rows_in in pair),
            pl.BlockSpec((2, 1, 2 * width), lambda i: (part, 0, 0)),
            *(whole(w) for w in weights),
            half_rows(2 * PAD),
            whole(gains),
            pl.BlockSpec((2, 3, PAD), lambda i: (part, 0, 0)),
        ],
        [jax.ShapeDtypeStruct((all_rows, cols), jnp.bfloat16) for cols in sizes],
        [half_rows(cols) for cols in sizes],
        carried,
        6 * rows * width * span,
    )


def split_lanes(values, first_lane, shape):
    lane = lax.broadcasted_iota(jnp.int32, shape, 1)
    high = values.astype(jnp.bfloat16).astype(jnp.float32)
    rest = values - high
    mid = rest.astype(jnp.bfloat16).astype(jnp.float32)
    low = rest - mid
    return jnp.where(
        lane == first_lane,
        high,
        jnp.where(lane == first_lane + 1, mid, jnp.where(lane == first_lane + 2, low, 0.0)),
    )


def attend_kernel(q_ref, key_ref, value_ref, mixed_ref, qlog_ref):
    half = key_ref.shape[0] // 2
    for first in range(0, q_ref.shape[0], SLOT_TOK):
        rows = slice(first, first + SLOT_TOK)
        q = q_ref[rows, :]
        total = None
        for start in (0, half):
            keys = slice(start, start + half)
            weight = jnp.exp2(full_dot(q, key_ref[keys, :], CONTRACT_COLS) * SCORE_LOG2)
            term = full_dot(weight.astype(jnp.bfloat16), value_ref[keys, :])
            total = term if total is None else total + term
        row_sum = total[:, TOTAL_LANE : TOTAL_LANE + 1]
        mixed_ref[rows, :] = (total * (1.0 / row_sum)).astype(jnp.bfloat16)
        log_sum = jnp.log2(row_sum) * (-1.0 / SCORE_LOG2)
        qlog_ref[rows, :] = (q.astype(jnp.float32) + split_lanes(log_sum, LOG_LANE, q.shape)).astype(
            jnp.bfloat16
        )


def attend(q, k, v, part, carried=None):
    all_rows, span = q.shape
    rows = all_rows // 2
    heads = span // PAD
    mine = pl.BlockSpec((rows, PAD), lambda h: (part, h))
    every = pl.BlockSpec((all_rows, PAD), lambda h: (0, h))
    return call_kernel(
        attend_kernel,
        (heads,),
        [q, k, v],
        [mine, every, every],
        [jax.ShapeDtypeStruct(q.shape, jnp.bfloat16)] * 2,
        [mine, mine],
        carried,
        4 * rows * all_rows * span,
        rows * all_rows * heads,
    )


def unturn(grad, lin, gain, cosine, sine, on_mxu):
    turned = rotate(grad, cosine, -sine)
    inverse = head_inverse(lin, on_mxu)
    normed = lin * inverse
    gained = turned * gain
    mean = lane_sum(gained * normed, on_mxu) * (1.0 / HEAD_DIM)
    return inverse * (gained - normed * mean), jnp.sum(turned * normed, axis=0, keepdims=True)


def pull_kernel(
    own_ref, other_ref, mixed_ref, q_ref, key_ref, value_ref, wo_ref, squeeze_ref, gain_ref, table_ref, lin_ref,
    *rest,
):
    *before, ga_ref, dq_ref, wide_ref, gains_ref, dk_ref, dv_ref = rest
    heads = q_ref.shape[1] // PAD
    half = key_ref.shape[0] // 2

    @pl.when(pl.program_id(0) == 0)
    def _():
        if before:
            gains_before, dk_before, dv_before = before
            gains_ref[...] = gains_before[...]
            dk_ref[...] = dk_before[...]
            dv_ref[...] = dv_before[...]
        else:
            gains_ref[...] = jnp.zeros_like(gains_ref)
            dk_ref[...] = jnp.zeros_like(dk_ref)
            dv_ref[...] = jnp.zeros_like(dv_ref)

    cosine, sine = table_parts(table_ref)
    grad_attn = pick_rows(own_ref, other_ref)
    ga_ref[...] = grad_attn
    grad_mixed = full_dot(grad_attn, wo_ref[...], CONTRACT_COLS).astype(jnp.bfloat16)
    gain_sum = jnp.zeros((1, PAD), jnp.float32)
    for h in range(heads):
        cols = slice(h * PAD, (h + 1) * PAD)
        grad_low = grad_mixed[:, cols]
        grad_head = grad_low.astype(jnp.float32)
        mixed = mixed_ref[:, cols].astype(jnp.float32)
        row_dot = jnp.sum(grad_head * mixed, axis=-1, keepdims=True)
        grad_aug = (grad_head + split_lanes(-row_dot, DOT_LANE, grad_head.shape)).astype(jnp.bfloat16)
        q = q_ref[:, cols]
        dq = None
        for start in (0, half):
            key_rows = slice(start, start + half)
            key, value = key_ref[key_rows, cols], value_ref[key_rows, cols]
            probs = jnp.exp2(full_dot(key, q, CONTRACT_COLS) * SCORE_LOG2)
            grad_probs = full_dot(value, grad_aug, CONTRACT_COLS)
            grad_scores = (probs * grad_probs).astype(jnp.bfloat16)
            dv_ref[key_rows, cols] += full_dot(probs.astype(jnp.bfloat16), grad_low)
            dk_ref[key_rows, cols] += full_dot(grad_scores, q)
            term = full_dot(grad_scores, key, CONTRACT_ROWS)
            dq = term if dq is None else dq + term
        lin = lin_ref[:, cols].astype(jnp.float32)
        grad_lin, gain_term = unturn(dq * INV_ROOT, lin, gain_ref[0:1, :], cosine, sine, False)
        gain_sum = gain_sum + gain_term
        wide_ref[:, cols] = grad_lin.astype(jnp.bfloat16)
    gains_ref[0:1, :] += gain_sum
    dq_ref[...] = full_dot(wide_ref[...], squeeze_ref[...]).astype(jnp.bfloat16)


def pull(pair, mixed, qlog, k, v, w_out, squeeze, gains, table, lin, first, carried=None, earlier=None):
    rows, width = 2 * SLOT_TOK, pair[0].shape[1]
    all_rows, span = qlog.shape
    compact = squeeze.shape[1]
    args = [*pair, mixed, qlog, k, v, w_out, squeeze, gains, table, lin]
    specs = [*(whole(a) for a in pair), slot_rows(span, first), slot_rows(span, first)]
    specs += [whole(a) for a in (k, v, w_out, squeeze, gains)]
    specs += [slot_rows(2 * PAD, first), slot_rows(span, first)]
    sums = [jax.ShapeDtypeStruct(shape, jnp.float32) for shape in ((8, PAD), (all_rows, span), (all_rows, span))]
    if earlier is not None:
        args += earlier
        specs += [whole(a) for a in earlier]
    kept = [jax.ShapeDtypeStruct((all_rows, cols), jnp.bfloat16) for cols in (width, compact, span)]
    return call_kernel(
        pull_kernel,
        (rows // SLOT_TOK,),
        args,
        specs,
        kept + sums,
        [slot_rows(a.shape[1], first) for a in kept] + [whole(a) for a in sums],
        carried,
        10 * rows * all_rows * span,
        rows * all_rows * span // PAD,
    )


def finish_kernel(
    dq_ref, dk_ref, dv_ref, lin_ref, squeeze_ref, gain_ref, table_ref, wq_ref, wk_ref, wv_ref,
    part_ref, gains_ref, kc_ref, vc_ref,
):
    @pl.when(pl.program_id(0) == 0)
    def _():
        gains_ref[...] = jnp.zeros_like(gains_ref)

    cosine, sine = table_parts(table_ref)
    gain_sum = jnp.zeros((1, PAD), jnp.float32)
    k_grads = []
    for h in range(dk_ref.shape[1] // PAD):
        cols = slice(h * PAD, (h + 1) * PAD)
        grad_lin, gain_term = unturn(
            dk_ref[:, cols] * INV_ROOT, lin_ref[:, cols].astype(jnp.float32), gain_ref[1:2, :], cosine, sine, True
        )
        gain_sum = gain_sum + gain_term
        k_grads.append(grad_lin.astype(jnp.bfloat16))
    gains_ref[0:1, :] += gain_sum
    k_wide = jnp.concatenate(k_grads, axis=1)
    v_wide = dv_ref[...].astype(jnp.bfloat16)
    kc_ref[...] = full_dot(k_wide, squeeze_ref[...]).astype(jnp.bfloat16)
    vc_ref[...] = full_dot(v_wide, squeeze_ref[...]).astype(jnp.bfloat16)
    part_ref[...] = (
        full_dot(dq_ref[...], wq_ref[...], CONTRACT_COLS)
        + full_dot(k_wide, wk_ref[...], CONTRACT_COLS)
        + full_dot(v_wide, wv_ref[...], CONTRACT_COLS)
    ).astype(jnp.bfloat16)


def finish(dq, dk, dv, lin, squeeze, gains, table, weights, first, carried=None):
    all_rows, span = dk.shape
    rows = all_rows // 2
    width, compact = weights[0].shape[0], squeeze.shape[1]
    kept = [jax.ShapeDtypeStruct((all_rows, compact), jnp.bfloat16)] * 2
    fresh = [jax.ShapeDtypeStruct((rows, width), jnp.bfloat16), jax.ShapeDtypeStruct((8, PAD), jnp.float32)]
    return call_kernel(
        finish_kernel,
        (rows // SLOT_TOK,),
        [dq, dk, dv, lin, squeeze, gains, table, *weights],
        [
            slot_rows(span, first),
            slot_rows(span, first),
            slot_rows(span, first),
            pl.BlockSpec((SLOT_TOK, span), lambda i: (i + first, 1)),
            whole(squeeze),
            whole(gains),
            slot_rows(2 * PAD, first),
            *(whole(w) for w in weights),
        ],
        fresh + kept,
        [slot_rows(width, 0), whole(fresh[1])] + [slot_rows(compact, first)] * 2,
        carried,
        6 * rows * span * width,
        first_carried=2,
    )


def mlp_kernel(own_ref, other_ref, gh_ref, wg_ref, wu_ref, part_ref, rows_ref, hidden_ref, grad_ref):
    rows = pick_rows(own_ref, other_ref)
    rows_ref[...] = rows
    gate_lin = full_dot(rows, wg_ref[...])
    up_lin = full_dot(rows, wu_ref[...])
    grad_hidden = gh_ref[...]
    sigmoid = 1.0 / (1.0 + jnp.exp(-gate_lin))
    silu = gate_lin * sigmoid
    hidden_ref[...] = (silu * up_lin).astype(jnp.bfloat16)
    grad_up = (grad_hidden * silu).astype(jnp.bfloat16)
    grad_gate = (grad_hidden * up_lin * (sigmoid + silu * (1.0 - sigmoid))).astype(jnp.bfloat16)
    units = wg_ref.shape[1]
    grad_ref[:, :units] = grad_gate
    grad_ref[:, units:] = grad_up
    part_ref[...] = (
        full_dot(grad_gate, wg_ref[...], CONTRACT_COLS) + full_dot(grad_up, wu_ref[...], CONTRACT_COLS)
    ).astype(jnp.bfloat16)


def mlp(pair, grad_hidden, w_gate, w_up, first, carried=None):
    rows, width = 2 * SLOT_TOK, pair[0].shape[1]
    all_rows, units = grad_hidden.shape
    kept = [jax.ShapeDtypeStruct((all_rows, cols), jnp.bfloat16) for cols in (width, units, 2 * units)]
    return call_kernel(
        mlp_kernel,
        (rows // SLOT_TOK,),
        [*pair, grad_hidden, w_gate, w_up],
        [*(whole(a) for a in pair), slot_rows(units, first), whole(w_gate), whole(w_up)],
        [jax.ShapeDtypeStruct((rows, width), jnp.bfloat16), *kept],
        [slot_rows(width, 0)] + [slot_rows(a.shape[1], first) for a in kept],
        carried,
        8 * rows * width * units,
        rows * units,
        first_carried=1,
        vmem=2 * VMEM_LIMIT,
    )


PLAN = {
    "down": ("down",),
    "terms": ("early",),
    "near": ("down",),
    "middle": ("early", "late"),
    "pulled": ("down", "early", "late"),
    "pulled_far": ("down", "early", "late"),
    "finished_far": ("down", "early", "late"),
    "query": ("query",),
    "key": ("key", "early", "late"),
    "tail": (
        "query", "late", "key", "early", "query", "key", "query", "late", "key",
        "query", "items", "key", "down", "items", "query", "items", "key", "items",
        "query", "down", "key",
    ),
}


def swap(values, axis_name, bit):
    count = lax.axis_size(axis_name)
    return lax.ppermute(values, axis_name, [(i, i ^ bit) for i in range(count)])


def after(values, *earlier):
    return lax.optimization_barrier((values, *earlier))[0]


def bits_of(axis_name):
    count = lax.axis_size(axis_name)
    bits = []
    bit = 1
    while bit < count:
        bits.append(bit)
        bit *= 2
    assert bit == count
    return bits


def halving_steps(first, second, bits, earlier):
    place = lax.axis_index("dp")
    upper = (place // bits[0]) % 2 == 1
    first = after(first, *earlier)
    send = jnp.where(upper, first, second)
    got = swap(send, "dp", bits[0])
    earlier = yield send
    low = after(jnp.where(upper, second, first), *earlier)
    low = (low.astype(jnp.float32) + got.astype(jnp.float32)).astype(jnp.bfloat16)
    for bit in bits[1:]:
        half = low.shape[0] // 2
        part = (place // bit) % 2
        send = lax.dynamic_slice_in_dim(low, (1 - part) * half, half, 0)
        got = swap(send, "dp", bit)
        earlier = yield send
        mine = lax.dynamic_slice_in_dim(after(low, *earlier), part * half, half, 0)
        low = (mine.astype(jnp.float32) + got.astype(jnp.float32)).astype(jnp.bfloat16)
    for bit in reversed(bits[1:]):
        got = swap(low, "dp", bit)
        earlier = yield low
        low = after(low, *earlier)
        low = jnp.where(
            (place // bit) % 2 == 1, jnp.concatenate([got, low], axis=0), jnp.concatenate([low, got], axis=0)
        )
    got = swap(low, "dp", bits[0])
    earlier = yield low
    low = after(low, *earlier)
    yield jnp.where(upper, got, low), jnp.where(upper, low, got)


def gather_steps(values, earlier):
    values = after(values, *earlier)
    for bit in reversed(bits_of("dp")):
        got = swap(values, "dp", bit)
        earlier = yield values
        values = jnp.concatenate([after(values, *earlier), got], axis=0)
    yield (values,)


def tree_steps(first, second, earlier):
    place = lax.axis_index("dp")
    if lax.axis_size("dp") != 8:
        yield from halving_steps(first, second, bits_of("dp"), earlier)
        return
    upper = place % 2 == 1
    is_end = (place // 2 == 0) | (place // 2 == 3)

    def along(values, pairs):
        return lax.ppermute(values, "dp", [(2 * a + y, 2 * b + y) for a, b in pairs for y in range(2)])

    def plus(values, got):
        return (values.astype(jnp.float32) + got.astype(jnp.float32)).astype(jnp.bfloat16)

    first = after(first, *earlier)
    send = jnp.where(upper, first, second)
    got = swap(send, "dp", 1)
    earlier = yield send
    low = plus(after(jnp.where(upper, second, first), *earlier), got)
    got = along(low, [(0, 1), (3, 2)])
    earlier = yield low
    low = plus(after(low, *earlier), got)
    got = along(low, [(1, 2), (2, 1)])
    earlier = yield low
    low = plus(after(low, *earlier), got)
    got = along(low, [(1, 0), (2, 3)])
    earlier = yield low
    low = jnp.where(is_end, got, after(low, *earlier))
    got = swap(low, "dp", 1)
    earlier = yield low
    low = after(low, *earlier)
    yield jnp.where(upper, got, low), jnp.where(upper, low, got)


class DpSums:
    def __init__(self):
        self.steps = {}
        self.newest = {}

    def offer(self, name, steps):
        self.steps[name] = steps
        self.newest[name] = None

    def step(self, name, *earlier):
        if self.newest[name] is None:
            self.steps[name] = self.steps[name](earlier)
            self.newest[name] = next(self.steps[name])
        elif not isinstance(self.newest[name], tuple):
            self.newest[name] = self.steps[name].send(earlier)
        newest = self.newest[name]
        return newest[0] if isinstance(newest, tuple) else newest

    def at(self, point, tick):
        for name in PLAN[point]:
            tick = self.step(name, tick)
        return tick

    def finish(self, tick):
        tick = self.at("tail", tick)
        while not all(isinstance(newest, tuple) for newest in self.newest.values()):
            for name in self.newest:
                tick = self.step(name, tick)
        return self.newest


def rows_dot(source, weight):
    return jnp.dot(source, weight, preferred_element_type=jnp.float32)


def dot_cols(source, weight):
    return lax.dot_general(source, weight, CONTRACT_COLS, preferred_element_type=jnp.float32)


def dot_rows(left, right):
    return lax.dot_general(
        left, right, CONTRACT_ROWS, preferred_element_type=jnp.float32
    ).astype(jnp.bfloat16)


def pair_sum(part):
    low = part.astype(jnp.bfloat16)
    got = swap(low[SLOT_TOK:], "tensor", 1)
    return low[:SLOT_TOK].astype(jnp.float32) + got.astype(jnp.float32)


def lane_of(dims):
    quarter = HEAD_DIM // 4
    pair, rest = dims // (2 * quarter), dims % (2 * quarter)
    return pair * quarter + jnp.where(rest < quarter, rest, BACK_LANE + rest - quarter)


def head_order(values):
    quarter = HEAD_DIM // 4
    return jnp.concatenate(
        [values[:, first : first + quarter] for first in (0, BACK_LANE, quarter, BACK_LANE + quarter)], axis=1
    )


def rope_table(grid_row, grid_col):
    quarter = HEAD_DIM // 4
    lane = jnp.arange(2 * PAD, dtype=jnp.int32)
    dim = lane % BACK_LANE
    rates = jnp.exp(-math.log(10000.0) * (dim % quarter).astype(jnp.float32) / quarter)
    places = jnp.arange(2 * SIDE, dtype=jnp.int32)
    angles = places.astype(jnp.float32)[:, None] * rates[None]
    sine_v = jnp.where((lane % PAD < BACK_LANE)[None], -jnp.sin(angles), jnp.sin(angles))
    values = jnp.where((lane < PAD)[None], jnp.cos(angles), sine_v)
    by_row = jnp.where((dim < quarter)[None], values, 0.0)
    by_col = jnp.where(((dim >= quarter) & (dim < 2 * quarter))[None], values, 0.0)
    hot = jnp.concatenate([grid[:, None] == places[None] for grid in (grid_row, grid_col)], axis=1)
    return jnp.dot(
        hot.astype(jnp.float32), jnp.concatenate([by_row, by_col], axis=0), precision=lax.Precision.HIGHEST
    )


def lane_extras(slot_ids, item_count):
    lane = jnp.arange(PAD, dtype=jnp.int32)
    hot = (lane - ITEM_LANE)[None] == (slot_ids + 1)[:, None]
    item_lane = ((lane >= ITEM_LANE) & (lane <= ITEM_LANE + item_count))[None]
    log_lane = ((lane >= LOG_LANE) & (lane < LOG_LANE + 3))[None]
    for_key = jnp.where(item_lane & ~hot, -FAR_ITEM, 0.0) + jnp.where(log_lane, 1.0, 0.0)
    for_value = jnp.broadcast_to(((lane >= TOTAL_LANE) & (lane < DOT_LANE + 3))[None], hot.shape)
    return jnp.stack([hot.astype(jnp.float32), for_key, for_value.astype(jnp.float32)], axis=1)


def local(
    tokens,
    w_query,
    w_key,
    w_value,
    w_out,
    w_gate,
    w_up,
    w_down,
    w_mod,
    b_mod,
    class_table,
    q_gain,
    k_gain,
    slot_item,
    labels,
    tsteps,
    cotangent,
):
    tensor_count = lax.axis_size("tensor")
    tensor_place = lax.axis_index("tensor")
    slot_count = slot_item.shape[1]
    item_count = labels.shape[1]
    assert tensor_count == 4 and slot_count == 4 and item_count < LOG_LANE - ITEM_LANE
    width = tokens.shape[1]
    head_cols = w_query.shape[1]
    heads = head_cols // HEAD_DIM
    bias_len = b_mod.shape[0]
    slot_ids = slot_item[0]
    half = 2 * SLOT_TOK

    far_tokens = swap(tokens, "tensor", 2)
    near_tokens = swap(tokens, "tensor", 1)

    slots = jnp.arange(slot_count, dtype=jnp.int32)
    rel_hot = (tensor_place ^ slots)[:, None] == slots[None, :]
    rel_int = rel_hot.astype(jnp.int32)
    item_ids = jnp.arange(item_count, dtype=jnp.int32)
    class_ids = jnp.arange(class_table.shape[0], dtype=jnp.int32)

    def condition(label_ids, step_ids):
        label_hot = (label_ids[:, None] == class_ids[None, :]).astype(jnp.float32)
        embedded = rows_dot(label_hot.astype(jnp.bfloat16), class_table)
        cond_pre = embedded + sinusoid(step_ids, tensor_place * head_cols, head_cols)
        return label_hot, cond_pre

    _, cond_own = condition(labels[0], tsteps[0])
    bias_full = lax.dynamic_update_slice_in_dim(
        jnp.zeros((6 * width,), jnp.float32), b_mod, tensor_place * bias_len, 0
    )
    modul = rows_dot(jax.nn.silu(cond_own).astype(jnp.bfloat16), w_mod) + bias_full[None, :]
    modul = modul + swap(modul, "tensor", 1)
    modul_pair = modul
    modul = modul + swap(modul, "tensor", 2)
    pad_row = jnp.arange(heads * PAD, dtype=jnp.int32)[:, None]
    flat_col = jnp.arange(head_cols, dtype=jnp.int32)[None, :]
    squeeze = (
        (pad_row // PAD == flat_col // HEAD_DIM) & (pad_row % PAD == lane_of(flat_col % HEAD_DIM))
    ).astype(jnp.bfloat16)
    w_wide = [dot_cols(after(w, modul_pair), squeeze).astype(jnp.bfloat16) for w in (w_query, w_key, w_value)]
    w_out_wide = rows_dot(squeeze, after(w_out, modul_pair)).astype(jnp.bfloat16)
    rel_ids = jnp.sum(rel_int * slot_ids[None, :], axis=1)
    rel_pick = (rel_ids[:, None] == item_ids[None, :]).astype(jnp.float32)
    grid_row, grid_col = grid_positions(slot_ids)

    def rel_tokens(per_token):
        return jnp.sum(rel_int[:, :, None] * per_token.reshape(1, slot_count, SLOT_TOK), axis=1).reshape(-1)

    table = rope_table(*(after(rel_tokens(g), modul_pair) for g in (grid_row, grid_col)))
    extras = lane_extras(rel_ids, item_count)
    gain_lane = lane_of(jnp.arange(HEAD_DIM, dtype=jnp.int32))[:, None] == jnp.arange(PAD)[None, :]
    gains = jnp.dot(
        jnp.stack([q_gain, k_gain]), gain_lane.astype(jnp.float32), precision=lax.Precision.HIGHEST
    )

    per_slot = jnp.dot(rel_pick, modul, precision=lax.Precision.HIGHEST)
    shift_a, scale_a, gate_a, shift_m, scale_m, gate_m = jnp.split(per_slot[:1], 6, axis=1)
    cot_now = after(cotangent, modul)
    far_cot = swap(cot_now, "tensor", 2)
    near_cot = swap(cot_now, "tensor", 1)

    slot_mods = per_slot[:, None, :]
    near_set = prepare((tokens, near_tokens), slot_mods, w_wide, table, gains, extras, 0)
    far_tokens = after(far_tokens, near_set[2])
    attn_all, lin, q, k, v = prepare(
        (far_tokens, swap(far_tokens, "tensor", 1)), slot_mods, w_wide, table, gains, extras, 1, near_set
    )
    far_mixed, far_qlog = attend(q, k, v, 1)
    far_sum = pair_sum(rows_dot(far_mixed[half:], w_out_wide)).astype(jnp.bfloat16)
    far_got = swap(far_sum, "tensor", 2)
    far_cot = after(far_cot, far_mixed)
    cot_all = jnp.concatenate([cotangent, near_cot, far_cot, swap(far_cot, "tensor", 1)], axis=0)
    mixed, qlog = attend(after(q, far_sum), k, v, 0, (far_mixed, far_qlog))
    near_sum = pair_sum(rows_dot(mixed[:half], w_out_wide))
    branch_grad = (
        (per_slot[:, None, 5 * width :] * after(cot_all, mixed).astype(jnp.float32).reshape(4, SLOT_TOK, width))
        .astype(jnp.bfloat16)
        .reshape(2 * half, width)
    )
    grad_hidden = dot_cols(branch_grad, w_down)
    mixed_low = rows_dot(mixed, squeeze).astype(jnp.bfloat16)
    attn = near_sum + after(far_got, grad_hidden, mixed_low).astype(jnp.float32)

    resid = tokens.astype(jnp.float32)
    middle = resid + gate_a * attn

    def norm_rows(values, shift_by, scale_by):
        return modulated_norm(values[None], shift_by, scale_by)[0]

    normed_two, norm_two_back = jax.vjp(norm_rows, middle, shift_m, scale_m)
    normed_mlp = normed_two.astype(jnp.bfloat16)
    far_normed = swap(normed_mlp, "tensor", 2)
    near_part, *near_mlp = mlp((normed_mlp, swap(normed_mlp, "tensor", 1)), grad_hidden, w_gate, w_up, 0)
    far_normed = after(far_normed, near_part)
    far_part, mlp_all, hidden, gate_up_grad = mlp(
        (far_normed, swap(far_normed, "tensor", 1)), grad_hidden, w_gate, w_up, 2, near_mlp
    )
    sums = DpSums()
    bits = bits_of("dp")
    late_first = bits[1:] + bits[:1]
    half_width = width // 2
    down_term = dot_rows(hidden, branch_grad)
    half_units = down_term.shape[0] // 2
    sums.offer("down", functools.partial(halving_steps, down_term[:half_units], down_term[half_units:], late_first))
    far_sum = pair_sum(far_part).astype(jnp.bfloat16)
    far_got = swap(far_sum, "tensor", 2)
    tick = sums.at("down", far_sum)
    units = w_gate.shape[1]
    gate_term = dot_rows(after(mlp_all, tick), gate_up_grad[:, :units])
    up_term = dot_rows(after(mlp_all, gate_term), gate_up_grad[:, units:])
    half_width = width // 2
    sums.offer("early", functools.partial(halving_steps, gate_term[:half_width], up_term[:half_width], bits))
    sums.offer("late", functools.partial(halving_steps, gate_term[half_width:], up_term[half_width:], bits))
    tick = sums.at("terms", up_term)
    near_sum = pair_sum(after(near_part, tick))
    tick = sums.at("near", near_sum)
    grad_normed_mlp = near_sum + after(far_got, tick).astype(jnp.float32)

    grad_out = cotangent.astype(jnp.float32)
    grad_mid_norm, grad_shift_m, grad_scale_m = norm_two_back(grad_normed_mlp)
    grad_middle = grad_out + grad_mid_norm
    grad_gate_a = jnp.sum(attn * grad_middle, axis=0, keepdims=True)
    grad_attn = (gate_a * grad_middle).astype(jnp.bfloat16)
    far_ga = swap(grad_attn, "tensor", 2)
    near_ga = swap(grad_attn, "tensor", 1)
    tick = sums.at("middle", grad_attn)
    near_pull = pull(
        (grad_attn, after(near_ga, tick)), mixed, qlog, k, v, w_out_wide, squeeze, gains, table, lin, 0
    )
    far_ga = after(far_ga, near_pull[0])
    diag_ga = swap(far_ga, "tensor", 1)
    tick = sums.at("pulled", near_pull[0])
    ga_all, q_low, q_wide, gain_q, sum_k, sum_v = pull(
        (far_ga, after(diag_ga, tick)), mixed, qlog, k, v, w_out_wide, squeeze, gains, table, lin,
        2, near_pull[:3], near_pull[3:],
    )
    tick = sums.at("pulled_far", q_low)
    far_part, gain_far, *far_low = finish(
        after(q_wide, tick), sum_k, sum_v, lin, squeeze, gains, table, w_wide, 2
    )
    far_sum = pair_sum(far_part).astype(jnp.bfloat16)
    far_got = swap(far_sum, "tensor", 2)
    branch_far = pair_sum(rows_dot(after(hidden, far_sum)[half:], w_down)).astype(jnp.bfloat16)
    branch_near = pair_sum(rows_dot(after(hidden, branch_far)[:half], w_down))
    tick = sums.at("finished_far", branch_near)
    near_part, gain_near, k_low, v_low = finish(
        after(q_wide, tick), sum_k, sum_v, lin, squeeze, gains, table, w_wide, 0, far_low
    )
    query_term = dot_rows(after(attn_all, near_part), q_low)
    value_term = dot_rows(after(attn_all, query_term), v_low)
    sums.offer("query", functools.partial(halving_steps, query_term, value_term, bits))
    tick = sums.at("query", value_term)
    key_term = dot_rows(after(k_low, tick), attn_all)
    out_term = dot_rows(mixed_low, after(ga_all, key_term))
    sums.offer("key", functools.partial(halving_steps, key_term, out_term, bits))
    tick = sums.at("key", out_term)
    near_sum = pair_sum(after(near_part, tick))
    grad_normed_attn = near_sum + after(far_got, tick).astype(jnp.float32)
    gain_grads = head_order(jnp.concatenate([gain_q[:1], gain_far[:1] + gain_near[:1]], axis=0))

    branch_got = swap(after(branch_far, out_term), "tensor", 2)
    branch = branch_near + branch_got.astype(jnp.float32)
    output = (middle + gate_m * branch).astype(jnp.bfloat16)
    grad_gate_m = jnp.sum(branch * grad_out, axis=0, keepdims=True)

    _, norm_one_back = jax.vjp(norm_rows, resid, shift_a, scale_a)
    grad_resid_norm, grad_shift_a, grad_scale_a = norm_one_back(grad_normed_attn)
    grad_tokens = (grad_middle + grad_resid_norm).astype(jnp.bfloat16)

    grad_slot = jnp.concatenate(
        [
            grad_shift_a,
            grad_scale_a,
            grad_gate_a,
            grad_shift_m,
            grad_scale_m,
            grad_gate_m,
            gain_grads[:1],
            gain_grads[1:],
        ],
        axis=1,
    )
    pair_slots = jnp.concatenate([grad_slot, swap(grad_slot, "tensor", 2)], axis=0)
    grad_slots = jnp.concatenate([pair_slots, swap(pair_slots, "tensor", 1)], axis=0)
    mod_width = 6 * width
    pick_order = jnp.stack([rel_pick[0], rel_pick[2], rel_pick[1], rel_pick[3]])
    grad_items = lax.dot_general(
        pick_order,
        grad_slots[:, :mod_width],
        CONTRACT_ROWS,
        precision=lax.Precision.HIGHEST,
        preferred_element_type=jnp.float32,
    ).astype(jnp.bfloat16)
    gain_sum = jnp.sum(grad_slots[:, mod_width:], axis=0, keepdims=True)
    gain_rows = jnp.pad(gain_sum, ((0, item_count - 1), (0, 0)))
    ids = jnp.stack([labels[0] // 32, labels[0] % 32, tsteps[0] // 32, tsteps[0] % 32], axis=1)
    item_rows = jnp.concatenate([gain_rows, ids.astype(jnp.float32)], axis=1).astype(jnp.bfloat16)
    sums.offer("items", functools.partial(gather_steps, jnp.concatenate([grad_items, item_rows], axis=1)))
    grad_w = sums.finish(near_part)
    items_all = grad_w["items"][0]
    grad_modul_low = items_all[:, :mod_width]
    gains_end = mod_width + 2 * HEAD_DIM
    gain_total = jnp.sum(items_all[:, mod_width:gains_end].astype(jnp.float32), axis=0)
    grad_q_gain = gain_total[:HEAD_DIM]
    grad_k_gain = gain_total[HEAD_DIM:]
    ids = items_all[:, gains_end:].astype(jnp.int32)
    label_hot, cond_pre = condition(ids[:, 0] * 32 + ids[:, 1], ids[:, 2] * 32 + ids[:, 3])
    cond_full, silu_back = jax.vjp(jax.nn.silu, cond_pre)
    grad_w_mod = lax.dot_general(
        cond_full.astype(jnp.bfloat16), grad_modul_low, CONTRACT_ROWS, preferred_element_type=jnp.float32
    )
    grad_bias_full = jnp.sum(grad_modul_low.astype(jnp.float32), axis=0)
    grad_b_mod = lax.dynamic_slice_in_dim(grad_bias_full, tensor_place * bias_len, bias_len, 0)
    grad_cond_pre = silu_back(dot_cols(grad_modul_low, w_mod))[0]
    grad_class_table = lax.dot_general(
        label_hot,
        grad_cond_pre,
        CONTRACT_ROWS,
        precision=lax.Precision.HIGHEST,
        preferred_element_type=jnp.float32,
    )
    wide_rows = lambda parts: jnp.concatenate(parts, axis=0).astype(jnp.float32)
    return (
        output,
        grad_tokens,
        grad_w["query"][0].astype(jnp.float32),
        grad_w["key"][0].T.astype(jnp.float32),
        grad_w["query"][1].astype(jnp.float32),
        grad_w["key"][1].astype(jnp.float32),
        wide_rows([grad_w["early"][0], grad_w["late"][0]]),
        wide_rows([grad_w["early"][1], grad_w["late"][1]]),
        wide_rows(grad_w["down"]),
        grad_w_mod,
        grad_b_mod,
        grad_class_table,
        grad_q_gain,
        grad_k_gain,
    )


def solution(mesh):
    in_specs = (
        P(("dp", "tensor"), None),
        P(None, "tensor"),
        P(None, "tensor"),
        P(None, "tensor"),
        P("tensor", None),
        P(None, "tensor"),
        P(None, "tensor"),
        P("tensor", None),
        P("tensor", None),
        P("tensor"),
        P(None, "tensor"),
        P(),
        P(),
        P("dp", None),
        P("dp", None),
        P("dp", None),
        P(("dp", "tensor"), None),
    )
    out_specs = (
        P(("dp", "tensor"), None),
        P(("dp", "tensor"), None),
        P(None, "tensor"),
        P(None, "tensor"),
        P(None, "tensor"),
        P("tensor", None),
        P(None, "tensor"),
        P(None, "tensor"),
        P("tensor", None),
        P("tensor", None),
        P("tensor"),
        P(None, "tensor"),
        P(),
        P(),
    )
    return jax.shard_map(local, mesh=mesh, in_specs=in_specs, out_specs=out_specs, check_vma=False)
```

```python
import functools
import math

import jax
import jax.numpy as jnp
from jax import lax
from jax.experimental import pallas as pl
from jax.experimental.pallas import tpu as pltpu
from jax.sharding import PartitionSpec as P

D = 1152
HEAD_DIM = 72
PAD = 128
SIDE = 16
SLOT_TOK = 256
EPSILON = 1e-06
SCORE_LOG2 = math.log2(math.e) / math.sqrt(HEAD_DIM)
INV_ROOT = 1.0 / math.sqrt(HEAD_DIM)
BACK_LANE = PAD // 2
TOTAL_LANE = HEAD_DIM // 2
DOT_LANE = TOTAL_LANE + 1
ITEM_LANE = TOTAL_LANE + 4
LOG_LANE = ITEM_LANE + 8
FAR_ITEM = 16384.0
CONTRACT_ROWS = (((0,), (0,)), ((), ()))
CONTRACT_COLS = (((1,), (1,)), ((), ()))
VMEM_LIMIT = 28 * 1024 * 1024


def sinusoid(step_ids, first_col, col_count):
    half_width = D // 2
    feature = first_col + jnp.arange(col_count, dtype=jnp.int32)
    freq_index = (feature % half_width).astype(jnp.float32)
    rates = jnp.exp(-math.log(10000.0) * freq_index / half_width)
    angles = step_ids.astype(jnp.float32)[:, None] * rates[None, :]
    return jnp.where(feature[None, :] < half_width, jnp.cos(angles), jnp.sin(angles))


def grid_positions(slot_ids):
    slot_count = slot_ids.shape[0]
    slot_order = jnp.arange(slot_count, dtype=jnp.int32)
    same_item = (slot_ids[:, None] == slot_ids[None, :]) & (slot_ids[:, None] >= 0)
    members = jnp.sum(same_item.astype(jnp.int32), axis=1)
    first_slot = jnp.min(jnp.where(same_item, slot_order[None, :], slot_count), axis=1)
    first_slot = jnp.where(members > 0, first_slot, slot_order)
    side_len = jnp.where(members > 1, 2 * SIDE, SIDE)
    within = jnp.arange(SLOT_TOK, dtype=jnp.int32)
    place_in = (slot_order - first_slot)[:, None] * SLOT_TOK + within[None, :]
    return ((place_in // side_len[:, None]).reshape(-1), (place_in % side_len[:, None]).reshape(-1))


def modulated_norm(values, shift_by, scale_by):
    normed = values * lax.rsqrt(jnp.mean(values * values, axis=-1, keepdims=True) + EPSILON)
    return normed * (1.0 + scale_by[:, None, :]) + shift_by[:, None, :]


def full_dot(left, right, dims=(((1,), (0,)), ((), ()))):
    return lax.dot_general(left, right, dims, preferred_element_type=jnp.float32)


def rotate(values, cosine, sine):
    return values * cosine + pltpu.roll(values, BACK_LANE, 1) * sine


def lane_sum(values, on_mxu):
    if on_mxu:
        return full_dot(values.astype(jnp.bfloat16), jnp.ones((PAD, PAD), jnp.bfloat16))
    return jnp.sum(values, axis=-1, keepdims=True)


def head_inverse(lin, on_mxu):
    return lax.rsqrt(lane_sum(lin * lin, on_mxu) * (1.0 / HEAD_DIM) + EPSILON)


def table_parts(table_ref):
    return table_ref[:, :PAD], table_ref[:, PAD:]


def whole(array):
    return pl.BlockSpec(array.shape, lambda i: (0,) * array.ndim)


def pick_rows(first_ref, second_ref):
    return jnp.where(pl.program_id(0) == 0, first_ref[...], second_ref[...])


def slot_rows(cols, first):
    return pl.BlockSpec((SLOT_TOK, cols), lambda i: (i + first, 0))


def call_kernel(body, grid, args, in_specs, out_shape, out_specs, carried, flops, exps=0, first_carried=0, vmem=VMEM_LIMIT):
    carried = [] if carried is None else list(carried)
    count = len(args)
    moved = sum(a.size * a.dtype.itemsize for a in args)

    def wrapped(*refs):
        body(*refs[:count], *refs[count + len(carried) :])

    return pl.pallas_call(
        wrapped,
        grid=grid,
        in_specs=list(in_specs) + [pl.BlockSpec(memory_space=pl.ANY)] * len(carried),
        out_shape=out_shape,
        out_specs=out_specs,
        input_output_aliases={count + i: first_carried + i for i in range(len(carried))},
        compiler_params=pltpu.CompilerParams(vmem_limit_bytes=vmem),
        cost_estimate=pl.CostEstimate(flops=flops, bytes_accessed=moved, transcendentals=exps),
    )(*args, *carried)


def prepare_kernel(
    own_ref, other_ref, mod_ref, wq_ref, wk_ref, wv_ref, table_ref, gain_ref, extra_ref,
    normed_ref, lin_ref, q_ref, k_ref, v_ref,
):
    heads = q_ref.shape[1] // PAD
    span = heads * PAD
    width = own_ref.shape[1]
    for slot, rows_ref in enumerate((own_ref, other_ref)):
        x = rows_ref[...].astype(jnp.float32)
        rms = lax.rsqrt(jnp.mean(x * x, axis=-1, keepdims=True) + EPSILON)
        shift_by = mod_ref[slot, :, :width]
        scale_by = mod_ref[slot, :, width:]
        normed_ref[slot * SLOT_TOK : (slot + 1) * SLOT_TOK, :] = (
            x * rms * (1.0 + scale_by) + shift_by
        ).astype(jnp.bfloat16)
    normed = normed_ref[...]
    in_first = lax.broadcasted_iota(jnp.int32, (2 * SLOT_TOK, PAD), 0) < SLOT_TOK
    cosine, sine = table_parts(table_ref)
    for part, w_ref in enumerate((wq_ref, wk_ref, wv_ref)):
        lin = full_dot(normed, w_ref[...])
        for h in range(heads):
            cols = slice(h * PAD, (h + 1) * PAD)
            piece = lin[:, cols]
            extra = jnp.where(in_first, extra_ref[0, part : part + 1, :], extra_ref[1, part : part + 1, :])
            if part == 2:
                v_ref[:, cols] = (piece + extra).astype(jnp.bfloat16)
                continue
            lin_ref[:, part * span + h * PAD : part * span + (h + 1) * PAD] = piece.astype(jnp.bfloat16)
            gain = gain_ref[part : part + 1, :]
            turned = rotate(piece * head_inverse(piece, True) * gain, cosine, sine)
            out_ref = q_ref if part == 0 else k_ref
            out_ref[:, cols] = (turned + extra).astype(jnp.bfloat16)


def prepare(pair, per_slot, weights, table, gains, extras, part, carried=None):
    rows, width = 2 * SLOT_TOK, pair[0].shape[1]
    span = weights[0].shape[1]
    all_rows = table.shape[0]
    sizes = (width, 2 * span, span, span, span)
    half_rows = lambda cols: pl.BlockSpec((rows, cols), lambda i: (part, 0))
    return call_kernel(
        prepare_kernel,
        (1,),
        [*pair, per_slot, *weights, table, gains, extras],
        [
            *(whole(rows_in) for rows_in in pair),
            pl.BlockSpec((2, 1, 2 * width), lambda i: (part, 0, 0)),
            *(whole(w) for w in weights),
            half_rows(2 * PAD),
            whole(gains),
            pl.BlockSpec((2, 3, PAD), lambda i: (part, 0, 0)),
        ],
        [jax.ShapeDtypeStruct((all_rows, cols), jnp.bfloat16) for cols in sizes],
        [half_rows(cols) for cols in sizes],
        carried,
        6 * rows * width * span,
    )


def split_lanes(values, first_lane, shape):
    lane = lax.broadcasted_iota(jnp.int32, shape, 1)
    high = values.astype(jnp.bfloat16).astype(jnp.float32)
    rest = values - high
    mid = rest.astype(jnp.bfloat16).astype(jnp.float32)
    low = rest - mid
    return jnp.where(
        lane == first_lane,
        high,
        jnp.where(lane == first_lane + 1, mid, jnp.where(lane == first_lane + 2, low, 0.0)),
    )


def attend_kernel(q_ref, key_ref, value_ref, mixed_ref, qlog_ref):
    half = key_ref.shape[0] // 2
    for first in range(0, q_ref.shape[0], SLOT_TOK):
        rows = slice(first, first + SLOT_TOK)
        q = q_ref[rows, :]
        total = None
        for start in (0, half):
            keys = slice(start, start + half)
            weight = jnp.exp2(full_dot(q, key_ref[keys, :], CONTRACT_COLS) * SCORE_LOG2)
            term = full_dot(weight.astype(jnp.bfloat16), value_ref[keys, :])
            total = term if total is None else total + term
        row_sum = total[:, TOTAL_LANE : TOTAL_LANE + 1]
        mixed_ref[rows, :] = (total * (1.0 / row_sum)).astype(jnp.bfloat16)
        log_sum = jnp.log2(row_sum) * (-1.0 / SCORE_LOG2)
        qlog_ref[rows, :] = (q.astype(jnp.float32) + split_lanes(log_sum, LOG_LANE, q.shape)).astype(
            jnp.bfloat16
        )


def attend(q, k, v, part, carried=None):
    all_rows, span = q.shape
    rows = all_rows // 2
    heads = span // PAD
    mine = pl.BlockSpec((rows, PAD), lambda h: (part, h))
    every = pl.BlockSpec((all_rows, PAD), lambda h: (0, h))
    return call_kernel(
        attend_kernel,
        (heads,),
        [q, k, v],
        [mine, every, every],
        [jax.ShapeDtypeStruct(q.shape, jnp.bfloat16)] * 2,
        [mine, mine],
        carried,
        4 * rows * all_rows * span,
        rows * all_rows * heads,
    )


def unturn(grad, lin, gain, cosine, sine, on_mxu):
    turned = rotate(grad, cosine, -sine)
    inverse = head_inverse(lin, on_mxu)
    normed = lin * inverse
    gained = turned * gain
    mean = lane_sum(gained * normed, on_mxu) * (1.0 / HEAD_DIM)
    return inverse * (gained - normed * mean), jnp.sum(turned * normed, axis=0, keepdims=True)


def pull_kernel(
    own_ref, other_ref, mixed_ref, q_ref, key_ref, value_ref, wo_ref, squeeze_ref, gain_ref, table_ref, lin_ref,
    *rest,
):
    *before, ga_ref, dq_ref, wide_ref, gains_ref, dk_ref, dv_ref = rest
    heads = q_ref.shape[1] // PAD
    half = key_ref.shape[0] // 2

    @pl.when(pl.program_id(0) == 0)
    def _():
        if before:
            gains_before, dk_before, dv_before = before
            gains_ref[...] = gains_before[...]
            dk_ref[...] = dk_before[...]
            dv_ref[...] = dv_before[...]
        else:
            gains_ref[...] = jnp.zeros_like(gains_ref)
            dk_ref[...] = jnp.zeros_like(dk_ref)
            dv_ref[...] = jnp.zeros_like(dv_ref)

    cosine, sine = table_parts(table_ref)
    grad_attn = pick_rows(own_ref, other_ref)
    ga_ref[...] = grad_attn
    grad_mixed = full_dot(grad_attn, wo_ref[...], CONTRACT_COLS).astype(jnp.bfloat16)
    gain_sum = jnp.zeros((1, PAD), jnp.float32)
    for h in range(heads):
        cols = slice(h * PAD, (h + 1) * PAD)
        grad_low = grad_mixed[:, cols]
        grad_head = grad_low.astype(jnp.float32)
        mixed = mixed_ref[:, cols].astype(jnp.float32)
        row_dot = jnp.sum(grad_head * mixed, axis=-1, keepdims=True)
        grad_aug = (grad_head + split_lanes(-row_dot, DOT_LANE, grad_head.shape)).astype(jnp.bfloat16)
        q = q_ref[:, cols]
        dq = None
        for start in (0, half):
            key_rows = slice(start, start + half)
            key, value = key_ref[key_rows, cols], value_ref[key_rows, cols]
            probs = jnp.exp2(full_dot(key, q, CONTRACT_COLS) * SCORE_LOG2)
            grad_probs = full_dot(value, grad_aug, CONTRACT_COLS)
            grad_scores = (probs * grad_probs).astype(jnp.bfloat16)
            dv_ref[key_rows, cols] += full_dot(probs.astype(jnp.bfloat16), grad_low)
            dk_ref[key_rows, cols] += full_dot(grad_scores, q)
            term = full_dot(grad_scores, key, CONTRACT_ROWS)
            dq = term if dq is None else dq + term
        lin = lin_ref[:, cols].astype(jnp.float32)
        grad_lin, gain_term = unturn(dq * INV_ROOT, lin, gain_ref[0:1, :], cosine, sine, False)
        gain_sum = gain_sum + gain_term
        wide_ref[:, cols] = grad_lin.astype(jnp.bfloat16)
    gains_ref[0:1, :] += gain_sum
    dq_ref[...] = full_dot(wide_ref[...], squeeze_ref[...]).astype(jnp.bfloat16)


def pull(pair, mixed, qlog, k, v, w_out, squeeze, gains, table, lin, first, carried=None, earlier=None):
    rows, width = 2 * SLOT_TOK, pair[0].shape[1]
    all_rows, span = qlog.shape
    compact = squeeze.shape[1]
    args = [*pair, mixed, qlog, k, v, w_out, squeeze, gains, table, lin]
    specs = [*(whole(a) for a in pair), slot_rows(span, first), slot_rows(span, first)]
    specs += [whole(a) for a in (k, v, w_out, squeeze, gains)]
    specs += [slot_rows(2 * PAD, first), slot_rows(span, first)]
    sums = [jax.ShapeDtypeStruct(shape, jnp.float32) for shape in ((8, PAD), (all_rows, span), (all_rows, span))]
    if earlier is not None:
        args += earlier
        specs += [whole(a) for a in earlier]
    kept = [jax.ShapeDtypeStruct((all_rows, cols), jnp.bfloat16) for cols in (width, compact, span)]
    return call_kernel(
        pull_kernel,
        (rows // SLOT_TOK,),
        args,
        specs,
        kept + sums,
        [slot_rows(a.shape[1], first) for a in kept] + [whole(a) for a in sums],
        carried,
        10 * rows * all_rows * span,
        rows * all_rows * span // PAD,
    )


def finish_kernel(
    dq_ref, dk_ref, dv_ref, lin_ref, squeeze_ref, gain_ref, table_ref, wq_ref, wk_ref, wv_ref,
    part_ref, gains_ref, kc_ref, vc_ref,
):
    @pl.when(pl.program_id(0) == 0)
    def _():
        gains_ref[...] = jnp.zeros_like(gains_ref)

    cosine, sine = table_parts(table_ref)
    gain_sum = jnp.zeros((1, PAD), jnp.float32)
    k_grads = []
    for h in range(dk_ref.shape[1] // PAD):
        cols = slice(h * PAD, (h + 1) * PAD)
        grad_lin, gain_term = unturn(
            dk_ref[:, cols] * INV_ROOT, lin_ref[:, cols].astype(jnp.float32), gain_ref[1:2, :], cosine, sine, True
        )
        gain_sum = gain_sum + gain_term
        k_grads.append(grad_lin.astype(jnp.bfloat16))
    gains_ref[0:1, :] += gain_sum
    k_wide = jnp.concatenate(k_grads, axis=1)
    v_wide = dv_ref[...].astype(jnp.bfloat16)
    kc_ref[...] = full_dot(k_wide, squeeze_ref[...]).astype(jnp.bfloat16)
    vc_ref[...] = full_dot(v_wide, squeeze_ref[...]).astype(jnp.bfloat16)
    part_ref[...] = (
        full_dot(dq_ref[...], wq_ref[...], CONTRACT_COLS)
        + full_dot(k_wide, wk_ref[...], CONTRACT_COLS)
        + full_dot(v_wide, wv_ref[...], CONTRACT_COLS)
    ).astype(jnp.bfloat16)


def finish(dq, dk, dv, lin, squeeze, gains, table, weights, first, carried=None):
    all_rows, span = dk.shape
    rows = all_rows // 2
    width, compact = weights[0].shape[0], squeeze.shape[1]
    kept = [jax.ShapeDtypeStruct((all_rows, compact), jnp.bfloat16)] * 2
    fresh = [jax.ShapeDtypeStruct((rows, width), jnp.bfloat16), jax.ShapeDtypeStruct((8, PAD), jnp.float32)]
    return call_kernel(
        finish_kernel,
        (rows // SLOT_TOK,),
        [dq, dk, dv, lin, squeeze, gains, table, *weights],
        [
            slot_rows(span, first),
            slot_rows(span, first),
            slot_rows(span, first),
            pl.BlockSpec((SLOT_TOK, span), lambda i: (i + first, 1)),
            whole(squeeze),
            whole(gains),
            slot_rows(2 * PAD, first),
            *(whole(w) for w in weights),
        ],
        fresh + kept,
        [slot_rows(width, 0), whole(fresh[1])] + [slot_rows(compact, first)] * 2,
        carried,
        6 * rows * span * width,
        first_carried=2,
    )


def mlp_kernel(own_ref, other_ref, gh_ref, wg_ref, wu_ref, part_ref, rows_ref, hidden_ref, grad_ref):
    rows = pick_rows(own_ref, other_ref)
    rows_ref[...] = rows
    gate_lin = full_dot(rows, wg_ref[...])
    up_lin = full_dot(rows, wu_ref[...])
    grad_hidden = gh_ref[...]
    sigmoid = 1.0 / (1.0 + jnp.exp(-gate_lin))
    silu = gate_lin * sigmoid
    hidden_ref[...] = (silu * up_lin).astype(jnp.bfloat16)
    grad_up = (grad_hidden * silu).astype(jnp.bfloat16)
    grad_gate = (grad_hidden * up_lin * (sigmoid + silu * (1.0 - sigmoid))).astype(jnp.bfloat16)
    units = wg_ref.shape[1]
    grad_ref[:, :units] = grad_gate
    grad_ref[:, units:] = grad_up
    part_ref[...] = (
        full_dot(grad_gate, wg_ref[...], CONTRACT_COLS) + full_dot(grad_up, wu_ref[...], CONTRACT_COLS)
    ).astype(jnp.bfloat16)


def mlp(pair, grad_hidden, w_gate, w_up, first, carried=None):
    rows, width = 2 * SLOT_TOK, pair[0].shape[1]
    all_rows, units = grad_hidden.shape
    kept = [jax.ShapeDtypeStruct((all_rows, cols), jnp.bfloat16) for cols in (width, units, 2 * units)]
    return call_kernel(
        mlp_kernel,
        (rows // SLOT_TOK,),
        [*pair, grad_hidden, w_gate, w_up],
        [*(whole(a) for a in pair), slot_rows(units, first), whole(w_gate), whole(w_up)],
        [jax.ShapeDtypeStruct((rows, width), jnp.bfloat16), *kept],
        [slot_rows(width, 0)] + [slot_rows(a.shape[1], first) for a in kept],
        carried,
        8 * rows * width * units,
        rows * units,
        first_carried=1,
        vmem=2 * VMEM_LIMIT,
    )


PLAN = {
    "down": ("down",),
    "terms": ("early",),
    "near": ("down",),
    "middle": ("early", "late"),
    "pulled": ("down", "early", "late"),
    "pulled_far": ("down", "early", "late"),
    "finished_far": ("down", "early", "late"),
    "query": ("query",),
    "key": ("key", "early", "late"),
    "tail": (
        "query", "late", "key", "early", "query", "key", "query", "late", "key",
        "query", "items", "key", "down", "items", "query", "items", "key", "items",
        "query", "down", "key",
    ),
}


def swap(values, axis_name, bit):
    count = lax.axis_size(axis_name)
    return lax.ppermute(values, axis_name, [(i, i ^ bit) for i in range(count)])


def after(values, *earlier):
    return lax.optimization_barrier((values, *earlier))[0]


def bits_of(axis_name):
    count = lax.axis_size(axis_name)
    bits = []
    bit = 1
    while bit < count:
        bits.append(bit)
        bit *= 2
    assert bit == count
    return bits


def halving_steps(first, second, bits, earlier):
    place = lax.axis_index("dp")
    upper = (place // bits[0]) % 2 == 1
    first = after(first, *earlier)
    send = jnp.where(upper, first, second)
    got = swap(send, "dp", bits[0])
    earlier = yield send
    low = after(jnp.where(upper, second, first), *earlier)
    low = (low.astype(jnp.float32) + got.astype(jnp.float32)).astype(jnp.bfloat16)
    for bit in bits[1:]:
        half = low.shape[0] // 2
        part = (place // bit) % 2
        send = lax.dynamic_slice_in_dim(low, (1 - part) * half, half, 0)
        got = swap(send, "dp", bit)
        earlier = yield send
        mine = lax.dynamic_slice_in_dim(after(low, *earlier), part * half, half, 0)
        low = (mine.astype(jnp.float32) + got.astype(jnp.float32)).astype(jnp.bfloat16)
    for bit in reversed(bits[1:]):
        got = swap(low, "dp", bit)
        earlier = yield low
        low = after(low, *earlier)
        low = jnp.where(
            (place // bit) % 2 == 1, jnp.concatenate([got, low], axis=0), jnp.concatenate([low, got], axis=0)
        )
    got = swap(low, "dp", bits[0])
    earlier = yield low
    low = after(low, *earlier)
    yield jnp.where(upper, got, low), jnp.where(upper, low, got)


def gather_steps(values, earlier):
    values = after(values, *earlier)
    for bit in reversed(bits_of("dp")):
        got = swap(values, "dp", bit)
        earlier = yield values
        values = jnp.concatenate([after(values, *earlier), got], axis=0)
    yield (values,)


def tree_steps(first, second, earlier):
    place = lax.axis_index("dp")
    if lax.axis_size("dp") != 8:
        yield from halving_steps(first, second, bits_of("dp"), earlier)
        return
    upper = place % 2 == 1
    is_end = (place // 2 == 0) | (place // 2 == 3)

    def along(values, pairs):
        return lax.ppermute(values, "dp", [(2 * a + y, 2 * b + y) for a, b in pairs for y in range(2)])

    def plus(values, got):
        return (values.astype(jnp.float32) + got.astype(jnp.float32)).astype(jnp.bfloat16)

    first = after(first, *earlier)
    send = jnp.where(upper, first, second)
    got = swap(send, "dp", 1)
    earlier = yield send
    low = plus(after(jnp.where(upper, second, first), *earlier), got)
    got = along(low, [(0, 1), (3, 2)])
    earlier = yield low
    low = plus(after(low, *earlier), got)
    got = along(low, [(1, 2), (2, 1)])
    earlier = yield low
    low = plus(after(low, *earlier), got)
    got = along(low, [(1, 0), (2, 3)])
    earlier = yield low
    low = jnp.where(is_end, got, after(low, *earlier))
    got = swap(low, "dp", 1)
    earlier = yield low
    low = after(low, *earlier)
    yield jnp.where(upper, got, low), jnp.where(upper, low, got)


class DpSums:
    def __init__(self):
        self.steps = {}
        self.newest = {}

    def offer(self, name, steps):
        self.steps[name] = steps
        self.newest[name] = None

    def step(self, name, *earlier):
        if self.newest[name] is None:
            self.steps[name] = self.steps[name](earlier)
            self.newest[name] = next(self.steps[name])
        elif not isinstance(self.newest[name], tuple):
            self.newest[name] = self.steps[name].send(earlier)
        newest = self.newest[name]
        return newest[0] if isinstance(newest, tuple) else newest

    def at(self, point, tick):
        for name in PLAN[point]:
            tick = self.step(name, tick)
        return tick

    def finish(self, tick):
        tick = self.at("tail", tick)
        while not all(isinstance(newest, tuple) for newest in self.newest.values()):
            for name in self.newest:
                tick = self.step(name, tick)
        return self.newest


def rows_dot(source, weight):
    return jnp.dot(source, weight, preferred_element_type=jnp.float32)


def dot_cols(source, weight):
    return lax.dot_general(source, weight, CONTRACT_COLS, preferred_element_type=jnp.float32)


def dot_rows(left, right):
    return lax.dot_general(
        left, right, CONTRACT_ROWS, preferred_element_type=jnp.float32
    ).astype(jnp.bfloat16)


def pair_sum(part):
    low = part.astype(jnp.bfloat16)
    got = swap(low[SLOT_TOK:], "tensor", 1)
    return low[:SLOT_TOK].astype(jnp.float32) + got.astype(jnp.float32)


def lane_of(dims):
    quarter = HEAD_DIM // 4
    pair, rest = dims // (2 * quarter), dims % (2 * quarter)
    return pair * quarter + jnp.where(rest < quarter, rest, BACK_LANE + rest - quarter)


def head_order(values):
    quarter = HEAD_DIM // 4
    return jnp.concatenate(
        [values[:, first : first + quarter] for first in (0, BACK_LANE, quarter, BACK_LANE + quarter)], axis=1
    )


def rope_table(grid_row, grid_col):
    quarter = HEAD_DIM // 4
    lane = jnp.arange(2 * PAD, dtype=jnp.int32)
    dim = lane % BACK_LANE
    rates = jnp.exp(-math.log(10000.0) * (dim % quarter).astype(jnp.float32) / quarter)
    places = jnp.arange(2 * SIDE, dtype=jnp.int32)
    angles = places.astype(jnp.float32)[:, None] * rates[None]
    sine_v = jnp.where((lane % PAD < BACK_LANE)[None], -jnp.sin(angles), jnp.sin(angles))
    values = jnp.where((lane < PAD)[None], jnp.cos(angles), sine_v)
    by_row = jnp.where((dim < quarter)[None], values, 0.0)
    by_col = jnp.where(((dim >= quarter) & (dim < 2 * quarter))[None], values, 0.0)
    hot = jnp.concatenate([grid[:, None] == places[None] for grid in (grid_row, grid_col)], axis=1)
    return jnp.dot(
        hot.astype(jnp.float32), jnp.concatenate([by_row, by_col], axis=0), precision=lax.Precision.HIGHEST
    )


def lane_extras(slot_ids, item_count):
    lane = jnp.arange(PAD, dtype=jnp.int32)
    hot = (lane - ITEM_LANE)[None] == (slot_ids + 1)[:, None]
    item_lane = ((lane >= ITEM_LANE) & (lane <= ITEM_LANE + item_count))[None]
    log_lane = ((lane >= LOG_LANE) & (lane < LOG_LANE + 3))[None]
    for_key = jnp.where(item_lane & ~hot, -FAR_ITEM, 0.0) + jnp.where(log_lane, 1.0, 0.0)
    for_value = jnp.broadcast_to(((lane >= TOTAL_LANE) & (lane < DOT_LANE + 3))[None], hot.shape)
    return jnp.stack([hot.astype(jnp.float32), for_key, for_value.astype(jnp.float32)], axis=1)


def local(
    tokens,
    w_query,
    w_key,
    w_value,
    w_out,
    w_gate,
    w_up,
    w_down,
    w_mod,
    b_mod,
    class_table,
    q_gain,
    k_gain,
    slot_item,
    labels,
    tsteps,
    cotangent,
):
    tensor_count = lax.axis_size("tensor")
    tensor_place = lax.axis_index("tensor")
    slot_count = slot_item.shape[1]
    item_count = labels.shape[1]
    assert tensor_count == 4 and slot_count == 4 and item_count < LOG_LANE - ITEM_LANE
    width = tokens.shape[1]
    head_cols = w_query.shape[1]
    heads = head_cols // HEAD_DIM
    bias_len = b_mod.shape[0]
    slot_ids = slot_item[0]
    half = 2 * SLOT_TOK

    far_tokens = swap(tokens, "tensor", 2)
    near_tokens = swap(tokens, "tensor", 1)

    slots = jnp.arange(slot_count, dtype=jnp.int32)
    rel_hot = (tensor_place ^ slots)[:, None] == slots[None, :]
    rel_int = rel_hot.astype(jnp.int32)
    item_ids = jnp.arange(item_count, dtype=jnp.int32)
    class_ids = jnp.arange(class_table.shape[0], dtype=jnp.int32)

    def condition(label_ids, step_ids):
        label_hot = (label_ids[:, None] == class_ids[None, :]).astype(jnp.float32)
        embedded = rows_dot(label_hot.astype(jnp.bfloat16), class_table)
        cond_pre = embedded + sinusoid(step_ids, tensor_place * head_cols, head_cols)
        return label_hot, cond_pre

    _, cond_own = condition(labels[0], tsteps[0])
    bias_full = lax.dynamic_update_slice_in_dim(
        jnp.zeros((6 * width,), jnp.float32), b_mod, tensor_place * bias_len, 0
    )
    modul = rows_dot(jax.nn.silu(cond_own).astype(jnp.bfloat16), w_mod) + bias_full[None, :]
    modul = modul + swap(modul, "tensor", 1)
    modul_pair = modul
    modul = modul + swap(modul, "tensor", 2)
    pad_row = jnp.arange(heads * PAD, dtype=jnp.int32)[:, None]
    flat_col = jnp.arange(head_cols, dtype=jnp.int32)[None, :]
    squeeze = (
        (pad_row // PAD == flat_col // HEAD_DIM) & (pad_row % PAD == lane_of(flat_col % HEAD_DIM))
    ).astype(jnp.bfloat16)
    w_wide = [dot_cols(after(w, modul_pair), squeeze).astype(jnp.bfloat16) for w in (w_query, w_key, w_value)]
    w_out_wide = rows_dot(squeeze, after(w_out, modul_pair)).astype(jnp.bfloat16)
    rel_ids = jnp.sum(rel_int * slot_ids[None, :], axis=1)
    rel_pick = (rel_ids[:, None] == item_ids[None, :]).astype(jnp.float32)
    grid_row, grid_col = grid_positions(slot_ids)

    def rel_tokens(per_token):
        return jnp.sum(rel_int[:, :, None] * per_token.reshape(1, slot_count, SLOT_TOK), axis=1).reshape(-1)

    table = rope_table(*(after(rel_tokens(g), modul_pair) for g in (grid_row, grid_col)))
    extras = lane_extras(rel_ids, item_count)
    gain_lane = lane_of(jnp.arange(HEAD_DIM, dtype=jnp.int32))[:, None] == jnp.arange(PAD)[None, :]
    gains = jnp.dot(
        jnp.stack([q_gain, k_gain]), gain_lane.astype(jnp.float32), precision=lax.Precision.HIGHEST
    )

    per_slot = jnp.dot(rel_pick, modul, precision=lax.Precision.HIGHEST)
    shift_a, scale_a, gate_a, shift_m, scale_m, gate_m = jnp.split(per_slot[:1], 6, axis=1)
    cot_now = after(cotangent, modul_pair)
    far_cot = swap(cot_now, "tensor", 2)
    near_cot = swap(cot_now, "tensor", 1)

    slot_mods = per_slot[:, None, :]
    near_set = prepare((tokens, near_tokens), slot_mods, w_wide, table, gains, extras, 0)
    far_tokens = after(far_tokens, modul_pair)
    attn_all, lin, q, k, v = prepare(
        (far_tokens, swap(far_tokens, "tensor", 1)), slot_mods, w_wide, table, gains, extras, 1, near_set
    )
    far_mixed, far_qlog = attend(q, k, v, 1)
    far_sum = pair_sum(rows_dot(far_mixed[half:], w_out_wide)).astype(jnp.bfloat16)
    far_got = swap(far_sum, "tensor", 2)
    far_cot = after(far_cot, q)
    cot_all = jnp.concatenate([cotangent, near_cot, far_cot, swap(far_cot, "tensor", 1)], axis=0)
    mixed, qlog = attend(after(q, far_sum), k, v, 0, (far_mixed, far_qlog))
    near_sum = pair_sum(rows_dot(mixed[:half], w_out_wide))
    branch_grad = (
        (per_slot[:, None, 5 * width :] * after(cot_all, mixed).astype(jnp.float32).reshape(4, SLOT_TOK, width))
        .astype(jnp.bfloat16)
        .reshape(2 * half, width)
    )
    grad_hidden = dot_cols(branch_grad, w_down)
    mixed_low = rows_dot(mixed, squeeze).astype(jnp.bfloat16)
    attn = near_sum + after(far_got, grad_hidden, mixed_low).astype(jnp.float32)

    resid = tokens.astype(jnp.float32)
    middle = resid + gate_a * attn

    def norm_rows(values, shift_by, scale_by):
        return modulated_norm(values[None], shift_by, scale_by)[0]

    normed_two, norm_two_back = jax.vjp(norm_rows, middle, shift_m, scale_m)
    normed_mlp = normed_two.astype(jnp.bfloat16)
    far_normed = swap(normed_mlp, "tensor", 2)
    near_part, *near_mlp = mlp((normed_mlp, swap(normed_mlp, "tensor", 1)), grad_hidden, w_gate, w_up, 0)
    far_normed = after(far_normed, near_part)
    far_part, mlp_all, hidden, gate_up_grad = mlp(
        (far_normed, swap(far_normed, "tensor", 1)), grad_hidden, w_gate, w_up, 2, near_mlp
    )
    sums = DpSums()
    bits = bits_of("dp")
    late_first = bits[1:] + bits[:1]
    half_width = width // 2
    down_term = dot_rows(hidden, branch_grad)
    half_units = down_term.shape[0] // 2
    sums.offer("down", functools.partial(halving_steps, down_term[:half_units], down_term[half_units:], late_first))
    far_sum = pair_sum(far_part).astype(jnp.bfloat16)
    far_got = swap(far_sum, "tensor", 2)
    tick = sums.at("down", far_sum)
    units = w_gate.shape[1]
    gate_term = dot_rows(after(mlp_all, tick), gate_up_grad[:, :units])
    up_term = dot_rows(after(mlp_all, gate_term), gate_up_grad[:, units:])
    half_width = width // 2
    sums.offer("early", functools.partial(halving_steps, gate_term[:half_width], up_term[:half_width], bits))
    sums.offer("late", functools.partial(halving_steps, gate_term[half_width:], up_term[half_width:], bits))
    tick = sums.at("terms", up_term)
    near_sum = pair_sum(after(near_part, tick))
    tick = sums.at("near", near_sum)
    grad_normed_mlp = near_sum + after(far_got, tick).astype(jnp.float32)

    grad_out = cotangent.astype(jnp.float32)
    grad_mid_norm, grad_shift_m, grad_scale_m = norm_two_back(grad_normed_mlp)
    grad_middle = grad_out + grad_mid_norm
    grad_gate_a = jnp.sum(attn * grad_middle, axis=0, keepdims=True)
    grad_attn = (gate_a * grad_middle).astype(jnp.bfloat16)
    far_ga = swap(grad_attn, "tensor", 2)
    near_ga = swap(grad_attn, "tensor", 1)
    tick = sums.at("middle", grad_attn)
    near_pull = pull(
        (grad_attn, after(near_ga, tick)), mixed, qlog, k, v, w_out_wide, squeeze, gains, table, lin, 0
    )
    far_ga = after(far_ga, near_pull[0])
    diag_ga = swap(far_ga, "tensor", 1)
    tick = sums.at("pulled", near_pull[0])
    ga_all, q_low, q_wide, gain_q, sum_k, sum_v = pull(
        (far_ga, after(diag_ga, tick)), mixed, qlog, k, v, w_out_wide, squeeze, gains, table, lin,
        2, near_pull[:3], near_pull[3:],
    )
    tick = sums.at("pulled_far", q_low)
    far_part, gain_far, *far_low = finish(
        after(q_wide, tick), sum_k, sum_v, lin, squeeze, gains, table, w_wide, 2
    )
    far_sum = pair_sum(far_part).astype(jnp.bfloat16)
    far_got = swap(far_sum, "tensor", 2)
    branch_far = pair_sum(rows_dot(after(hidden, far_sum)[half:], w_down)).astype(jnp.bfloat16)
    branch_near = pair_sum(rows_dot(after(hidden, branch_far)[:half], w_down))
    tick = sums.at("finished_far", branch_near)
    near_part, gain_near, k_low, v_low = finish(
        after(q_wide, tick), sum_k, sum_v, lin, squeeze, gains, table, w_wide, 0, far_low
    )
    query_term = dot_rows(after(attn_all, near_part), q_low)
    value_term = dot_rows(after(attn_all, query_term), v_low)
    sums.offer("query", functools.partial(halving_steps, query_term, value_term, bits))
    tick = sums.at("query", value_term)
    key_term = dot_rows(after(k_low, tick), attn_all)
    out_term = dot_rows(mixed_low, after(ga_all, key_term))
    sums.offer("key", functools.partial(halving_steps, key_term, out_term, bits))
    tick = sums.at("key", out_term)
    near_sum = pair_sum(after(near_part, tick))
    grad_normed_attn = near_sum + after(far_got, tick).astype(jnp.float32)
    gain_grads = head_order(jnp.concatenate([gain_q[:1], gain_far[:1] + gain_near[:1]], axis=0))

    branch_got = swap(after(branch_far, out_term), "tensor", 2)
    branch = branch_near + branch_got.astype(jnp.float32)
    output = (middle + gate_m * branch).astype(jnp.bfloat16)
    grad_gate_m = jnp.sum(branch * grad_out, axis=0, keepdims=True)

    _, norm_one_back = jax.vjp(norm_rows, resid, shift_a, scale_a)
    grad_resid_norm, grad_shift_a, grad_scale_a = norm_one_back(grad_normed_attn)
    grad_tokens = (grad_middle + grad_resid_norm).astype(jnp.bfloat16)

    grad_slot = jnp.concatenate(
        [
            grad_shift_a,
            grad_scale_a,
            grad_gate_a,
            grad_shift_m,
            grad_scale_m,
            grad_gate_m,
            gain_grads[:1],
            gain_grads[1:],
        ],
        axis=1,
    )
    pair_slots = jnp.concatenate([grad_slot, swap(grad_slot, "tensor", 2)], axis=0)
    grad_slots = jnp.concatenate([pair_slots, swap(pair_slots, "tensor", 1)], axis=0)
    mod_width = 6 * width
    pick_order = jnp.stack([rel_pick[0], rel_pick[2], rel_pick[1], rel_pick[3]])
    grad_items = lax.dot_general(
        pick_order,
        grad_slots[:, :mod_width],
        CONTRACT_ROWS,
        precision=lax.Precision.HIGHEST,
        preferred_element_type=jnp.float32,
    ).astype(jnp.bfloat16)
    gain_sum = jnp.sum(grad_slots[:, mod_width:], axis=0, keepdims=True)
    gain_rows = jnp.pad(gain_sum, ((0, item_count - 1), (0, 0)))
    ids = jnp.stack([labels[0] // 32, labels[0] % 32, tsteps[0] // 32, tsteps[0] % 32], axis=1)
    item_rows = jnp.concatenate([gain_rows, ids.astype(jnp.float32)], axis=1).astype(jnp.bfloat16)
    sums.offer("items", functools.partial(gather_steps, jnp.concatenate([grad_items, item_rows], axis=1)))
    grad_w = sums.finish(near_part)
    items_all = grad_w["items"][0]
    grad_modul_low = items_all[:, :mod_width]
    gains_end = mod_width + 2 * HEAD_DIM
    gain_total = jnp.sum(items_all[:, mod_width:gains_end].astype(jnp.float32), axis=0)
    grad_q_gain = gain_total[:HEAD_DIM]
    grad_k_gain = gain_total[HEAD_DIM:]
    ids = items_all[:, gains_end:].astype(jnp.int32)
    label_hot, cond_pre = condition(ids[:, 0] * 32 + ids[:, 1], ids[:, 2] * 32 + ids[:, 3])
    cond_full, silu_back = jax.vjp(jax.nn.silu, cond_pre)
    grad_w_mod = lax.dot_general(
        cond_full.astype(jnp.bfloat16), grad_modul_low, CONTRACT_ROWS, preferred_element_type=jnp.float32
    )
    grad_bias_full = jnp.sum(grad_modul_low.astype(jnp.float32), axis=0)
    grad_b_mod = lax.dynamic_slice_in_dim(grad_bias_full, tensor_place * bias_len, bias_len, 0)
    grad_cond_pre = silu_back(dot_cols(grad_modul_low, w_mod))[0]
    grad_class_table = lax.dot_general(
        label_hot,
        grad_cond_pre,
        CONTRACT_ROWS,
        precision=lax.Precision.HIGHEST,
        preferred_element_type=jnp.float32,
    )
    wide_rows = lambda parts: jnp.concatenate(parts, axis=0).astype(jnp.float32)
    return (
        output,
        grad_tokens,
        grad_w["query"][0].astype(jnp.float32),
        grad_w["key"][0].T.astype(jnp.float32),
        grad_w["query"][1].astype(jnp.float32),
        grad_w["key"][1].astype(jnp.float32),
        wide_rows([grad_w["early"][0], grad_w["late"][0]]),
        wide_rows([grad_w["early"][1], grad_w["late"][1]]),
        wide_rows(grad_w["down"]),
        grad_w_mod,
        grad_b_mod,
        grad_class_table,
        grad_q_gain,
        grad_k_gain,
    )


def solution(mesh):
    in_specs = (
        P(("dp", "tensor"), None),
        P(None, "tensor"),
        P(None, "tensor"),
        P(None, "tensor"),
        P("tensor", None),
        P(None, "tensor"),
        P(None, "tensor"),
        P("tensor", None),
        P("tensor", None),
        P("tensor"),
        P(None, "tensor"),
        P(),
        P(),
        P("dp", None),
        P("dp", None),
        P("dp", None),
        P(("dp", "tensor"), None),
    )
    out_specs = (
        P(("dp", "tensor"), None),
        P(("dp", "tensor"), None),
        P(None, "tensor"),
        P(None, "tensor"),
        P(None, "tensor"),
        P("tensor", None),
        P(None, "tensor"),
        P(None, "tensor"),
        P("tensor", None),
        P("tensor", None),
        P("tensor"),
        P(None, "tensor"),
        P(),
        P(),
    )
    return jax.shard_map(local, mesh=mesh, in_specs=in_specs, out_specs=out_specs, check_vma=False)
```
